32 devices in a mesh: trow: 8 (over y, x, core), tcol: 4 (over z).
Axes of the slice: x: 2, y: 2, z: 4, core: 2. Of those that a mesh axis runs over, the one named last changes fastest.
Arguments:
- theta: float32 [25, 128, 1024], P(None, 'trow', 'tcol'), may hold values from -6 to 6
- salt: float32 [25, 128, 1024], P(None, 'trow', 'tcol'), may hold values from -6 to 6
- velocity_x: float32 [25, 128, 1024], P(None, 'trow', 'tcol'), may hold values from -0.5 to 0.5
- velocity_y: float32 [25, 128, 1024], P(None, 'trow', 'tcol'), may hold values from -0.5 to 0.5
- land_mask: int32 [25, 128, 1024], P(None, 'trow', 'tcol'), may hold values 0 or 1
- kappa: float32 [24, 128, 1024], P(None, 'trow', 'tcol'), may hold values from 0.02 to 5
- forcing: float32 [128, 1024], P('trow', 'tcol'), may hold values from -6 to 6
- bottom: int32 [128, 1024], P('trow', 'tcol'), may hold values from 0 to 25
- theta_cot: float32 [25, 128, 1024], P(None, 'trow', 'tcol'), may hold values from -6 to 6
- salt_cot: float32 [25, 128, 1024], P(None, 'trow', 'tcol'), may hold values from -6 to 6
- surface_cot: float32 [128, 1024], P('trow', 'tcol'), may hold values from -24 to 24
Outputs:
- theta_grad: float32 [25, 128, 1024], P(None, 'trow', 'tcol')
- salt_grad: float32 [25, 128, 1024], P(None, 'trow', 'tcol')
- kappa_grad: float32 [24, 128, 1024], P(None, 'trow', 'tcol')
- forcing_grad: float32 [128, 1024], P('trow', 'tcol')
The draws below stay inside these ranges and needn't reach their ends.
All inputs are finite; a program needn't handle non-finite values. No bound on the sum of `land_mask` on one device may be relied on, other than what follows from the above.
Results may differ from the reference program's by a relative error of at most 0.0001.
Values sent between devices are 32-bit elements; how exact they have to be, the bound alone decides.
A program may use at most 64 MiB of HBM per device.

```python
import math
import jax
import jax.numpy as jnp
from jax import lax

NZ = 25
KZ = 24
ITERS = 4
NX = 128
NY = 1024


def draw_surface_cot(key, part):
    row_position = jnp.arange(NX, dtype=jnp.float32) / NX
    col_position = jnp.arange(NY, dtype=jnp.float32) / NY
    rising = (3.0 ** row_position)[:, None] * (3.0 ** col_position)[None, :] / 3.0
    key_first = jax.random.fold_in(key, 0)
    values = jax.random.normal(key_first, (NX, NY), jnp.float32) * rising
    return jnp.clip(values, -24.0, 24.0)


def place_ends(result, stream_key, smallest, top_value):
    spot = [jax.random.randint(jax.random.fold_in(stream_key, axis), (), 0, length) for axis, length in enumerate(result.shape)]
    main_axis = result.shape.index(max(result.shape))
    next_to = spot[:main_axis] + [(spot[main_axis] + 1) % result.shape[main_axis]] + spot[main_axis + 1:]
    return result.at[tuple(spot)].set(smallest).at[tuple(next_to)].set(top_value)


def level_of(rng, extent, cuts, least, top_value):
    loudness = 1.0
    for position, parts in cuts:
        steps = jax.random.uniform(jax.random.fold_in(jax.random.fold_in(rng, 6), position), (parts,), jnp.float32, least / len(cuts), top_value / len(cuts))
        loudness = loudness * jnp.repeat(jnp.exp(steps), extent[position] // parts).reshape((-1,) + (1,) * (len(extent) - 1 - position))
    return loudness


def scatter_about(key, extent, scale, bound, cuts=(), kind=jnp.bfloat16):
    gain = level_of(key, extent, cuts, -0.22, 0.18) if cuts else 1.0
    drawn = jax.random.normal(key, extent, jnp.float32) * scale * gain
    return jnp.minimum(jnp.maximum(drawn, -bound), bound).astype(kind)


def setup_inputs(seed: int = 0) -> dict:
    streams_of = jax.random.split(jax.random.key(seed), 12)
    theta = scatter_about(streams_of[0], (NZ, NX, NY), 1.0, 6.0, ((1, 8), (2, 4)), jnp.float32)
    salt = scatter_about(streams_of[1], (NZ, NX, NY), 1.0, 6.0, ((1, 8), (2, 4)), jnp.float32)
    velocity_x = jnp.clip(jax.random.uniform(streams_of[2], (NZ, NX, NY), jnp.float32, -0.5, 0.5) * level_of(streams_of[2], (NZ, NX, NY), ((1, 8), (2, 4)), -0.4, 0.0), -0.5, 0.5)
    velocity_y = jnp.clip(jax.random.uniform(streams_of[3], (NZ, NX, NY), jnp.float32, -0.5, 0.5) * level_of(streams_of[3], (NZ, NX, NY), ((1, 8), (2, 4)), -0.4, 0.0), -0.5, 0.5)
    land_mask = place_ends((jax.random.randint(streams_of[4], (NZ, NX, NY), 0, 8) < 7).astype(jnp.int32), jax.random.fold_in(streams_of[4], 1), 0, 1)
    kappa = jnp.clip(jnp.exp(math.log(5.0) - 5.521461 * jax.random.uniform(streams_of[5], (KZ, NX, NY), jnp.float32) ** level_of(streams_of[5], (KZ, NX, NY), ((1, 8), (2, 4)), -0.2, 0.2)), 0.02, 5.0)
    forcing = scatter_about(streams_of[6], (NX, NY), 1.0, 6.0, ((0, 8), (1, 4)), jnp.float32)
    bottom = place_ends(jax.random.randint(streams_of[7], (NX, NY), 0, NZ + 1), jax.random.fold_in(streams_of[7], 1), 0, NZ).astype(jnp.int32)
    theta_cot = scatter_about(streams_of[8], (NZ, NX, NY), 1.0, 6.0, ((1, 8), (2, 4)), jnp.float32)
    salt_cot = scatter_about(streams_of[9], (NZ, NX, NY), 1.0, 6.0, ((1, 8), (2, 4)), jnp.float32)
    surface_cot = draw_surface_cot(jax.random.fold_in(streams_of[11], 71), 0)
    return {"theta": theta, "salt": salt, "velocity_x": velocity_x, "velocity_y": velocity_y, "land_mask": land_mask, "kappa": kappa, "forcing": forcing, "bottom": bottom, "theta_cot": theta_cot, "salt_cot": salt_cot, "surface_cot": surface_cot}


def cut_along(array, start, count, axis_index):
    return lax.slice_in_dim(array, start, start + count, axis=axis_index)


def forward_change(padded_tracer, padded_velocity, padded_wet, axis_index, length):
    opened = cut_along(padded_velocity, 1, length + 1, axis_index) * cut_along(padded_wet, 1, length + 1, axis_index) * cut_along(padded_wet, 2, length + 1, axis_index)
    centre = cut_along(padded_tracer, 1, length + 1, axis_index) + cut_along(padded_tracer, 2, length + 1, axis_index)
    outer = cut_along(padded_tracer, 0, length + 1, axis_index) + cut_along(padded_tracer, 3, length + 1, axis_index)
    fluxes = opened * (7.0 * centre - outer) / 12.0
    return cut_along(fluxes, 1, length, axis_index) - cut_along(fluxes, 0, length, axis_index)


def adjoint_change(padded_lambda, padded_velocity, padded_wet, axis_index, length):
    opened = cut_along(padded_velocity, 0, length + 3, axis_index) * cut_along(padded_wet, 0, length + 3, axis_index) * cut_along(padded_wet, 1, length + 3, axis_index)
    faces = opened * (cut_along(padded_lambda, 0, length + 3, axis_index) - cut_along(padded_lambda, 1, length + 3, axis_index))
    return (7.0 * (cut_along(faces, 2, length, axis_index) + cut_along(faces, 1, length, axis_index)) - cut_along(faces, 3, length, axis_index) - cut_along(faces, 0, length, axis_index)) / 12.0


def advect(padded_tracer, padded_ux, padded_uy, padded_wet, tracer):
    row_count = padded_tracer.shape[1] - 4
    col_count = padded_tracer.shape[2] - 4
    along_rows = forward_change(padded_tracer[:, :, 2:-2], padded_ux[:, :, 2:-2], padded_wet[:, :, 2:-2], 1, row_count)
    along_cols = forward_change(padded_tracer[:, 2:-2, :], padded_uy[:, 2:-2, :], padded_wet[:, 2:-2, :], 2, col_count)
    return tracer - along_rows - along_cols


def advect_adjoint(padded_lambda, padded_ux, padded_uy, padded_wet, lambda_field, wet):
    row_count = padded_lambda.shape[1] - 4
    col_count = padded_lambda.shape[2] - 4
    along_rows = adjoint_change(padded_lambda[:, :, 2:-2], padded_ux[:, :, 2:-2], padded_wet[:, :, 2:-2], 1, row_count)
    along_cols = adjoint_change(padded_lambda[:, 2:-2, :], padded_uy[:, 2:-2, :], padded_wet[:, 2:-2, :], 2, col_count)
    return lambda_field - wet * (along_rows + along_cols)


def factorize(couple, depth):
    inverses = []
    ratios = []
    for depth_index in range(depth):
        diagonal = jnp.ones_like(couple[0])
        if depth_index > 0:
            diagonal = diagonal + couple[depth_index - 1] - couple[depth_index - 1] * ratios[depth_index - 1]
        if depth_index < depth - 1:
            diagonal = diagonal + couple[depth_index]
        inverse = 1.0 / diagonal
        inverses.append(inverse)
        if depth_index < depth - 1:
            ratios.append(couple[depth_index] * inverse)
    return inverses, ratios


def solve_columns(inverses, ratios, couple, rhs):
    depth = rhs.shape[0]
    sweeps = []
    carried = rhs[0] * inverses[0]
    sweeps.append(carried)
    for depth_index in range(1, depth):
        carried = (rhs[depth_index] + couple[depth_index - 1] * carried) * inverses[depth_index]
        sweeps.append(carried)
    results = [sweeps[depth - 1]]
    for depth_index in range(depth - 2, -1, -1):
        results.append(sweeps[depth_index] + ratios[depth_index] * results[-1])
    return jnp.stack(results[::-1])


def pad_rims(array):
    return jnp.pad(array, ((0, 0), (2, 2), (2, 2)))


def surface_apply(field, diagonal):
    padded = jnp.pad(field, 1)
    beside = padded[2:, 1:-1] + padded[:-2, 1:-1] + padded[1:-1, 2:] + padded[1:-1, :-2]
    return diagonal * field - beside


def conjugate(target, diagonal):
    solution = jnp.zeros_like(target)
    residual = target
    direction = target
    norm_now = jnp.sum(residual * residual)
    for iteration in range(ITERS):
        image = surface_apply(direction, diagonal)
        step_size = norm_now / jnp.sum(direction * image)
        solution = solution + step_size * direction
        residual = residual - step_size * image
        if iteration + 1 < ITERS:
            norm_next = jnp.sum(residual * residual)
            direction = residual + (norm_next / norm_now) * direction
            norm_now = norm_next
    return solution


def reference(theta, salt, velocity_x, velocity_y, land_mask, kappa, forcing, bottom, theta_cot, salt_cot, surface_cot):
    depth = theta.shape[0]
    levels = jnp.arange(depth, dtype=jnp.int32)[:, None, None]
    wet = land_mask.astype(jnp.float32) * (levels < bottom[None]).astype(jnp.float32)
    padded_ux = pad_rims(velocity_x)
    padded_uy = pad_rims(velocity_y)
    padded_wet = pad_rims(wet)
    theta_adv = advect(pad_rims(theta * wet), padded_ux, padded_uy, padded_wet, theta)
    salt_adv = advect(pad_rims(salt * wet), padded_ux, padded_uy, padded_wet, salt)
    couple = [kappa[depth_index] * wet[depth_index] * wet[depth_index + 1] for depth_index in range(depth - 1)]
    inverses, ratios = factorize(couple, depth)
    source = jnp.concatenate([theta_adv[:1] + (forcing * wet[0])[None], theta_adv[1:]], axis=0)
    theta_mix = solve_columns(inverses, ratios, couple, source)
    salt_mix = solve_columns(inverses, ratios, couple, salt_adv)
    diagonal = 4.2 + bottom.astype(jnp.float32) / depth
    zeta = conjugate(surface_cot, diagonal)
    theta_total = theta_cot + 0.2 * wet * zeta[None]
    salt_total = salt_cot - 0.15 * wet * zeta[None]
    theta_mu = solve_columns(inverses, ratios, couple, theta_total)
    salt_mu = solve_columns(inverses, ratios, couple, salt_total)
    opened = wet[:-1] * wet[1:]
    kappa_grad = -opened * ((theta_mu[:-1] - theta_mu[1:]) * (theta_mix[:-1] - theta_mix[1:]) + (salt_mu[:-1] - salt_mu[1:]) * (salt_mix[:-1] - salt_mix[1:]))
    forcing_grad = zeta + wet[0] * theta_mu[0]
    theta_grad = advect_adjoint(pad_rims(theta_mu), padded_ux, padded_uy, padded_wet, theta_mu, wet)
    salt_grad = advect_adjoint(pad_rims(salt_mu), padded_ux, padded_uy, padded_wet, salt_mu, wet)
    return theta_grad, salt_grad, kappa_grad, forcing_grad
```

```python
import functools
import jax
import jax.numpy as jnp
from jax import lax
from jax.experimental import pallas as pl
from jax.experimental.pallas import tpu as pltpu
from jax.sharding import PartitionSpec as P

ITERS = 4
LANES = 128
RIM = 8
LOW, HIGH = 0.2, 9.2
CENTRE, RADIUS = (HIGH + LOW) / 2, (HIGH - LOW) / 2
MESH = pl.DeviceIdType.MESH
F32 = jnp.float32


def put(out, k, value):
    out[k] = value if out[k] is None else out[k] + value


def times_operator(poly):
    out = [None] * (len(poly) + 1)
    for k, c in enumerate(poly):
        put(out, k, CENTRE * c)
        if k == 0:
            put(out, 1, RADIUS * c)
        else:
            half = (0.5 * RADIUS) * c
            put(out, k + 1, half)
            put(out, k - 1, half)
    return out


def inner(p, q, table):
    total = None
    for i, a in enumerate(p):
        part = None
        for j, b in enumerate(q):
            term = b * table[i][j]
            part = term if part is None else part + term
        part = a * part
        total = part if total is None else total + part
    return total


def add_scaled(p, scale, q):
    out = []
    for k in range(max(len(p), len(q))):
        if k >= len(p):
            out.append(scale * q[k])
        elif k >= len(q):
            out.append(p[k])
        else:
            out.append(p[k] + scale * q[k])
    return out


def weights_from(moments):
    table = [
        [
            moments[j] if i == 0 else moments[i] if j == 0 else 0.5 * (moments[i + j] + moments[abs(i - j)])
            for j in range(ITERS + 1)
        ]
        for i in range(ITERS)
    ]
    residual = [jnp.ones_like(moments[0])]
    direction = residual
    result = []
    norm_now = moments[0]
    for iteration in range(ITERS):
        image = times_operator(direction)
        step = norm_now / inner(direction, image, table)
        result = add_scaled(result, step, direction)
        if iteration + 1 < ITERS:
            residual = add_scaled(residual, -step, image)
            norm_next = inner(residual, residual, table)
            direction = add_scaled(residual, norm_next / norm_now, direction)
            norm_now = norm_next
    return result


def lane_index(rows):
    return lax.broadcasted_iota(jnp.int32, (rows, LANES), 1)


def roll(x, amount):
    return pltpu.roll(x, amount % LANES if isinstance(amount, int) else amount, 1)


def ahead(parts, by, lane):
    turned = [roll(p, -by) for p in parts] + [jnp.zeros_like(parts[0])]
    return [jnp.where(lane < LANES - by, turned[h], turned[h + 1]) for h in range(len(parts))]


def behind(parts, by, lane):
    turned = [jnp.zeros_like(parts[0])] + [roll(p, by) for p in parts]
    return [jnp.where(lane < by, turned[h], turned[h + 1]) for h in range(len(parts))]


def guarded(condition, action):
    @pl.when(condition)
    def _():
        action()


def kernel(
    sizes,
    theta_in, salt_in, vx_in, vy_in, land_in, kappa_in, forcing_in, bottom_in, theta_cot_in, salt_cot_in, surface_in,
    theta_grad, salt_grad, kappa_grad, forcing_grad,
    theta, salt, vx, vy, land, kappa, forcing, theta_cot, salt_cot,
    surface, bottom, wet, wet_after, first, second, open_y, inverse, link, ratio, theta_mix, salt_mix,
    theta_adj, salt_adj, k_fixed, k_zeta, zeta, seam_own, seam_left, seam_right, seam, slots,
    local_sem, rim_send, rim_recv, halo_send, halo_recv, sum_send, sum_recv,
):
    depth, rows, cols = sizes
    halves = cols // LANES
    top, end = RIM, RIM + rows
    mesh_rows, mesh_cols = lax.axis_size("trow"), lax.axis_size("tcol")
    count = mesh_rows * mesh_cols
    row, col = lax.axis_index("trow"), lax.axis_index("tcol")
    has_before, has_after = row > 0, row < mesh_rows - 1
    has_left, has_right = col > 0, col < mesh_cols - 1
    lane = lane_index(rows)
    spot = ((lane + 2) & 3) - 2

    def at(f, h, k):
        return (f * halves + h) * depth + k

    surface[...] = jnp.zeros_like(surface)
    bottom[...] = jnp.zeros_like(bottom)
    seam_left[...] = jnp.zeros_like(seam_left)
    seam_right[...] = jnp.zeros_like(seam_right)

    started = []

    def fetch(src, dst):
        copy = pltpu.make_async_copy(src, dst, local_sem.at[len(started)])
        copy.start()
        started.append(copy)
        return copy

    middle = pl.ds(LANES, cols)
    get_surface = fetch(surface_in, surface.at[pl.ds(RIM, rows), middle])
    get_bottom = fetch(bottom_in, bottom.at[pl.ds(RIM, rows), middle])

    def fetch_halves(src, dst):
        return [
            fetch(src.at[:, :, pl.ds(h * LANES, LANES)], dst.at[pl.ds(h * src.shape[0], src.shape[0])])
            for h in range(halves)
        ]

    get_land = fetch_halves(land_in, land)
    get_theta = fetch_halves(theta_in, theta)
    get_salt = fetch_halves(salt_in, salt)
    get_vx = fetch_halves(vx_in, vx)
    get_vy = fetch_halves(vy_in, vy)
    get_kappa = fetch_halves(kappa_in, kappa)
    get_theta_cot = fetch_halves(theta_cot_in, theta_cot)
    get_salt_cot = fetch_halves(salt_cot_in, salt_cot)
    get_forcing = fetch(forcing_in, forcing)

    def arrived(copies):
        for copy in copies:
            copy.wait()

    barrier = pltpu.get_barrier_semaphore()

    def other(i):
        return (lax.rem(row + lax.div(i, mesh_cols), mesh_rows), lax.rem(col + lax.rem(i, mesh_cols), mesh_cols))

    def greet(i, carry):
        pl.semaphore_signal(barrier, inc=1, device_id=other(i), device_id_type=MESH)
        return carry

    lax.fori_loop(1, count, greet, 0)
    pl.semaphore_wait(barrier, count - 1)

    rims = []
    for dr in (-1, 0, 1):
        for dc in (-1, 0, 1):
            if dr == 0 and dc == 0:
                continue
            conditions = [has_before] * (dr < 0) + [has_after] * (dr > 0) + [has_left] * (dc < 0) + [has_right] * (dc > 0)
            sources = [has_after] * (dr < 0) + [has_before] * (dr > 0) + [has_right] * (dc < 0) + [has_left] * (dc > 0)
            src_rows = pl.ds(0, RIM) if dr < 0 else pl.ds(rows - RIM, RIM) if dr > 0 else pl.ds(0, rows)
            src_cols = pl.ds(0, LANES) if dc < 0 else pl.ds(cols - LANES, LANES) if dc > 0 else pl.ds(0, cols)
            dst_rows = pl.ds(end, RIM) if dr < 0 else pl.ds(0, RIM) if dr > 0 else pl.ds(top, rows)
            dst_cols = pl.ds(LANES + cols, LANES) if dc < 0 else pl.ds(0, LANES) if dc > 0 else middle
            for src, dst in ((surface_in, surface), (bottom_in, bottom)):
                i = len(rims)
                copy = pltpu.make_async_remote_copy(
                    src_ref=src.at[src_rows, src_cols],
                    dst_ref=dst.at[dst_rows, dst_cols],
                    send_sem=rim_send.at[i],
                    recv_sem=rim_recv.at[i],
                    device_id=(row + dr, col + dc),
                    device_id_type=MESH,
                )
                rims.append((copy, functools.reduce(jnp.logical_and, conditions), functools.reduce(jnp.logical_and, sources)))
    for copy, sends, _ in rims:
        guarded(sends, copy.start)

    arrived([get_bottom] + get_land)

    def wet_level(k, carry):
        for h in range(halves):
            depth_here = bottom[top:end, LANES * (h + 1) : LANES * (h + 2)]
            value = jnp.where(k < depth_here, land[h * depth + k].astype(F32), 0.0)
            wet[h * depth + k, 0:rows] = value
            wet[h * depth + k, rows : rows + RIM] = jnp.ones((RIM, LANES), F32)
        return carry

    lax.fori_loop(0, depth, wet_level, 0)

    def wet_at(h, k):
        return wet[h * depth + k, 0:rows]

    arrived(get_theta + get_salt + get_vx + get_vy)

    def pack(k, parts, packed):
        both = jnp.where(lane < LANES // 2, parts[0], parts[-1])
        here = ((lane + 2 - 4 * k) & (LANES - 1)) < 4
        return jnp.where(here, roll(both, 4 * k), packed)

    def prepare(k, packs):
        wets = [wet_at(h, k) for h in range(halves)]
        wets_ahead = ahead(wets, 1, lane)
        qt, qs, uy = [], [], []
        for h in range(halves):
            i = h * depth + k
            qt.append(theta[i] * wets[h])
            qs.append(salt[i] * wets[h])
            uy.append(vy[i])
            first[at(0, h, k), top:end] = qt[h]
            first[at(1, h, k), top:end] = qs[h]
            first[at(2, h, k), top:end] = vx[i] * wets[h] * wet[i, 1 : rows + 1] * (1.0 / 12.0)
            open_y[i] = uy[h] * wets[h] * wets_ahead[h] * (1.0 / 12.0)
        return tuple(pack(k, parts, packed) for parts, packed in zip((qt, qs, uy, wets), packs))

    blank = jnp.zeros((rows, LANES), F32)
    for f, packed in enumerate(lax.fori_loop(0, depth, prepare, (blank,) * 4)):
        seam_own[f] = packed

    def remote(src, dst, i, device):
        return pltpu.make_async_remote_copy(
            src_ref=src, dst_ref=dst, send_sem=halo_send.at[i], recv_sem=halo_recv.at[i], device_id=device, device_id_type=MESH
        )

    after, before = (row + 1, col), (row - 1, col)
    right, left = (row, col + 1), (row, col - 1)
    both_tracers = pl.ds(0, 3 * halves * depth)
    stage_one = [
        (remote(first.at[both_tracers, pl.ds(end - 2, 2)], first.at[both_tracers, pl.ds(top - 2, 2)], 0, after), has_after, has_before),
        (remote(first.at[both_tracers, pl.ds(top, 2)], first.at[both_tracers, pl.ds(end, 2)], 1, before), has_before, has_after),
        (remote(wet.at[:, pl.ds(0, 1)], wet_after.at[:, pl.ds(0, 1)], 2, before), has_before, has_after),
        (remote(seam_own.at[pl.ds(0, 4)], seam_left.at[pl.ds(0, 4)], 3, right), has_right, has_left),
        (remote(seam_own.at[pl.ds(0, 4)], seam_right.at[pl.ds(0, 4)], 4, left), has_left, has_right),
    ]
    for copy, sends, _ in stage_one:
        guarded(sends, copy.start)

    def clear(missing, ref, start):
        @pl.when(missing)
        def _():
            def one(i, carry):
                ref[i, start : start + 2] = jnp.zeros((2, LANES), F32)
                return carry

            lax.fori_loop(0, ref.shape[0], one, 0)

    for ref in (first, second):
        clear(jnp.logical_not(has_before), ref, top - 2)
        clear(jnp.logical_not(has_after), ref, end)
    clear(jnp.logical_not(has_after), wet_after, 0)

    get_surface.wait()
    for copy, _, receives in rims:
        guarded(receives, copy.wait_recv)
    wide = (rows + 2 * RIM, cols + 2 * LANES)
    row_at = lax.broadcasted_iota(jnp.int32, wide, 0) - RIM + row * rows
    col_at = lax.broadcasted_iota(jnp.int32, wide, 1) - LANES + col * cols
    inside = ((row_at >= 0) & (row_at < rows * mesh_rows)) & ((col_at >= 0) & (col_at < cols * mesh_cols))
    scaled = (bottom[...].astype(F32) * (1.0 / depth) + (4.2 - CENTRE)) * (1.0 / RADIUS)
    basis = [surface[...]]
    for k in range(ITERS):
        field = basis[-1]
        beside = (pltpu.roll(field, 1, 0) + pltpu.roll(field, wide[0] - 1, 0)) + (
            pltpu.roll(field, 1, 1) + pltpu.roll(field, wide[1] - 1, 1)
        )
        image = scaled * field - beside * (1.0 / RADIUS)
        if k > 0:
            image = 2.0 * image - basis[-2]
        basis.append(jnp.where(inside, image, 0.0))

    def own_product(a, b):
        product = basis[a][top:end, LANES : LANES + cols] * basis[b][top:end, LANES : LANES + cols]
        tiles = [
            product[i : i + 8, j : j + LANES] for i in range(0, rows, 8) for j in range(0, cols, LANES)
        ]
        return functools.reduce(jnp.add, tiles)

    partial = [own_product(a, b) for a, b in ((0, 0), (0, 1), (0, 2), (0, 3), (0, 4), (2, 3), (3, 3), (3, 4))]
    small_lane = lane_index(8)
    width = LANES // 2
    while len(partial) > 1:
        folded = [p + pltpu.roll(p, LANES - width, 1) for p in partial]
        half = len(folded) // 2
        take_first = (small_lane & (2 * width - 1)) < width
        partial = [
            jnp.where(take_first, folded[i], pltpu.roll(folded[i + half], width, 1)) for i in range(half)
        ]
        width //= 2
    slots[0:1] = jnp.sum(partial[0], axis=0, keepdims=True)

    def sum_copy(i):
        return pltpu.make_async_remote_copy(
            src_ref=slots.at[pl.ds(0, 1)],
            dst_ref=slots.at[pl.ds(i, 1)],
            send_sem=sum_send.at[i],
            recv_sem=sum_recv.at[i],
            device_id=other(i),
            device_id_type=MESH,
        )

    def send_sum(i, carry):
        sum_copy(i).start()
        return carry

    lax.fori_loop(1, count, send_sum, 0)
    for k in range(ITERS):
        for h in range(halves + 2):
            zeta[k, h] = basis[k][:, h * LANES : (h + 1) * LANES]

    arrived(get_kappa + get_theta_cot + get_salt_cot)

    def couple_at(h, k):
        return kappa[h * (depth - 1) + k] * wet_at(h, k) * wet_at(h, k + 1)

    def down_level(k, couples, carry):
        out = []
        for h in range(halves):
            num, den, couple_before, yt, ys, yw = carry[h]
            i = h * depth + k
            den_next = num + couples[h] * den if couples is not None else num
            num_next = den_next + couples[h] * num if couples is not None else num
            inv = den * (1.0 / den_next)
            lower = couple_before * inv
            inverse[i] = inv
            link[i] = lower
            if couples is not None:
                ratio[i] = couples[h] * inv
            yt = theta_cot[i] * inv + lower * yt
            ys = salt_cot[i] * inv + lower * ys
            yw = wet_at(h, k) * inv + lower * yw
            second[at(0, h, k), top:end] = yt
            second[at(1, h, k), top:end] = ys
            second[at(2, h, k), top:end] = yw
            out.append((num_next, den_next, couples[h] if couples is not None else couple_before, yt, ys, yw))
        return tuple(out)

    one = jnp.ones((rows, LANES), F32)
    carry = ((one, one, blank, blank, blank, blank),) * halves
    carry = lax.fori_loop(0, depth - 1, lambda k, c: down_level(k, [couple_at(h, k) for h in range(halves)], c), carry)
    carry = down_level(depth - 1, None, carry)

    def up_level(i, carry):
        k = depth - 2 - i
        values, packs = carry
        new = []
        for f in range(3):
            parts = []
            for h in range(halves):
                x = second[at(f, h, k), top:end] + ratio[h * depth + k] * values[f][h]
                second[at(f, h, k), top:end] = x
                parts.append(x)
            new.append(tuple(parts))
        return tuple(new), tuple(pack(k, new[f], packs[f]) for f in range(3))

    last = tuple(tuple(carry[h][3 + f] for h in range(halves)) for f in range(3))
    packs = tuple(pack(depth - 1, last[f], blank) for f in range(3))
    _, packs = lax.fori_loop(0, depth - 1, up_level, (last, packs))
    for f in range(3):
        seam_own[4 + f] = packs[f]
    stage_two = [
        (remote(second.at[:, pl.ds(end - 2, 2)], second.at[:, pl.ds(top - 2, 2)], 5, after), has_after, has_before),
        (remote(second.at[:, pl.ds(top, 2)], second.at[:, pl.ds(end, 2)], 6, before), has_before, has_after),
        (remote(seam_own.at[pl.ds(4, 3)], seam_left.at[pl.ds(4, 3)], 7, right), has_right, has_left),
        (remote(seam_own.at[pl.ds(4, 3)], seam_right.at[pl.ds(4, 3)], 8, left), has_left, has_right),
    ]
    for copy, sends, _ in stage_two:
        guarded(sends, copy.start)

    for copy, sends, receives in stage_one:
        guarded(sends, copy.wait_send)
        guarded(receives, copy.wait_recv)

    def close_faces(i, carry):
        first[2 * halves * depth + i, top - 1 : top] = first[2 * halves * depth + i, top - 1 : top] * wet[i, 0:1]
        first[2 * halves * depth + i, end - 1 : end] = first[2 * halves * depth + i, end - 1 : end] * wet_after[i, 0:1]
        return carry

    lax.fori_loop(0, halves * depth, close_faces, 0)

    def across_left(f):
        return jnp.where(spot < 0, seam_left[f], seam_own[f])

    def across_right(f):
        return jnp.where(spot < 0, seam_own[f], seam_right[f])

    wet_left, wet_right = across_left(3), across_right(3)
    open_left = across_left(2) * wet_left * roll(wet_left, -1) * (1.0 / 12.0)
    open_right = across_right(2) * wet_right * roll(wet_right, -1) * (1.0 / 12.0)

    def forward_seam(f):
        q = across_left(f)
        flux = open_left * (7.0 * (q + roll(q, -1)) - roll(q, 1) - roll(q, -2))
        flux = jnp.where(spot == -1, flux, 0.0)
        cross = jnp.where(spot == 0, open_left * roll(q, 1), 0.0)
        at_left = roll(flux, 1) + cross - roll(cross, 1)
        q = across_right(f)
        flux = open_right * (7.0 * (q + roll(q, -1)) - roll(q, 1) - roll(q, -2))
        flux = jnp.where(spot == -1, flux, 0.0)
        cross = jnp.where(spot == -2, open_right * roll(q, -2), 0.0)
        at_right = cross - flux - roll(cross, 1)
        return jnp.where(spot >= 0, at_left, at_right)

    def adjoint_seam(m_left, m_right):
        faces = jnp.where(spot < 0, open_left * (m_left - roll(m_left, -1)), 0.0)
        at_left = 7.0 * roll(faces, 1) - roll(faces, 2)
        faces = jnp.where((spot == -1) | (spot == 0), open_right * (m_right - roll(m_right, -1)), 0.0)
        at_right = 7.0 * faces - roll(faces, -1)
        return jnp.where(spot >= 0, at_left, jnp.where(spot == -2, -roll(faces, -1), at_right))

    def unpack(k, f):
        turned = roll(seam[f], LANES - 4 * k)
        parts = [None] * halves
        parts[0] = jnp.where(lane < 2, turned, 0.0)
        parts[-1] = jnp.where(lane >= LANES - 2, turned, 0.0)
        return parts

    seam[0] = forward_seam(0)
    seam[1] = forward_seam(1)
    get_forcing.wait()
    for h in range(halves):
        theta[h * depth] = theta[h * depth] + forcing[:, h * LANES : (h + 1) * LANES] * wet_at(h, 0)

    def advected(k, f, raw):
        centre = [first[at(f, h, k), top:end] for h in range(halves)]
        next_one, next_two, previous = ahead(centre, 1, lane), ahead(centre, 2, lane), behind(centre, 1, lane)
        fluxes = [
            open_y[h * depth + k] * (7.0 * (centre[h] + next_one[h]) - previous[h] - next_two[h]) for h in range(halves)
        ]
        fluxes_before = behind(fluxes, 1, lane)
        edges = unpack(k, f)
        out = []
        for h in range(halves):
            q = [first[at(f, h, k), top + s : end + s] for s in (-2, -1, 0, 1, 2)]
            here = first[at(2, h, k), top:end] * (7.0 * (q[2] + q[3]) - q[1] - q[4])
            ahead_of = first[at(2, h, k), top - 1 : end - 1] * (7.0 * (q[1] + q[2]) - q[0] - q[3])
            value = raw[h * depth + k] - (here - ahead_of) - (fluxes[h] - fluxes_before[h])
            out.append(value if edges[h] is None else value + edges[h])
        return out

    def forward_down(k, carry):
        adv_t, adv_s = advected(k, 0, theta), advected(k, 1, salt)
        out = []
        for h in range(halves):
            i = h * depth + k
            yt = adv_t[h] * inverse[i] + link[i] * carry[h][0]
            ys = adv_s[h] * inverse[i] + link[i] * carry[h][1]
            theta_mix[i] = yt
            salt_mix[i] = ys
            out.append((yt, ys))
        return tuple(out)

    carry = lax.fori_loop(0, depth, forward_down, ((blank, blank),) * halves)

    def forward_up(n, carry):
        k = depth - 2 - n
        out = []
        for h in range(halves):
            i = h * depth + k
            xt = theta_mix[i] + ratio[i] * carry[h][0]
            xs = salt_mix[i] + ratio[i] * carry[h][1]
            dt, ds = xt - carry[h][0], xs - carry[h][1]
            at_, as_, aw = [
                second[at(f, h, k), top:end] - second[at(f, h, k + 1), top:end] for f in range(3)
            ]
            closed = -wet_at(h, k) * wet_at(h, k + 1)
            k_fixed[i] = closed * (at_ * dt + as_ * ds)
            k_zeta[i] = closed * aw * (0.2 * dt - 0.15 * ds)
            out.append((xt, xs))
        return tuple(out)

    lax.fori_loop(0, depth - 1, forward_up, carry)

    for copy, sends, receives in stage_two:
        guarded(receives, copy.wait_recv)
    seam[0] = adjoint_seam(across_left(4), across_right(4))
    seam[1] = adjoint_seam(across_left(5), across_right(5))

    def adjoint_level(k, windows, edges):
        centre = [windows[h][2] for h in range(halves)]
        nexts = ahead(centre, 1, lane)
        faces = [open_y[h * depth + k] * (centre[h] - nexts[h]) for h in range(halves)]
        face_next, face_one, face_two = ahead(faces, 1, lane), behind(faces, 1, lane), behind(faces, 2, lane)
        out = []
        for h in range(halves):
            m = windows[h]
            hx = [first[at(2, h, k), top + s : end + s] * (m[s + 2] - m[s + 3]) for s in (-2, -1, 0, 1)]
            change = 7.0 * ((hx[2] + hx[1]) + (faces[h] + face_one[h])) - (hx[3] + hx[0]) - (face_next[h] + face_two[h])
            if edges[h] is not None:
                change = change + edges[h]
            out.append(centre[h] - wet_at(h, k) * change)
        return out

    def adjoint_fixed(k, carry):
        for f, target in ((0, theta_adj), (1, salt_adj)):
            windows = [
                [second[at(f, h, k), top + s : end + s] for s in (-2, -1, 0, 1, 2)] for h in range(halves)
            ]
            result = adjoint_level(k, windows, unpack(k, f))
            for h in range(halves):
                target[h * depth + k] = result[h]
        return carry

    lax.fori_loop(0, depth, adjoint_fixed, 0)

    def got_sum(i, carry):
        sum_copy(i).wait_recv()
        return carry

    lax.fori_loop(1, count, got_sum, 0)
    total = jnp.sum(slots[...], axis=0, keepdims=True)
    for step in (8, 4, 2, 1):
        total = total + pltpu.roll(total, LANES - step, 1)
    m = [jnp.broadcast_to(total[:, 16 * g : 16 * g + 1], (8, LANES)) for g in range(8)]
    m = m[:5] + [2.0 * m[5] - m[1], 2.0 * m[6] - m[0], 2.0 * m[7] - m[1]]
    weights = [jnp.concatenate([w] * (wide[0] // 8), axis=0) for w in weights_from(m)]
    for h in range(halves + 2):
        zeta[0, h] = (weights[0] * zeta[0, h] + weights[1] * zeta[1, h]) + (weights[2] * zeta[2, h] + weights[3] * zeta[3, h])

    def everywhere(outer, inner_part):
        value = jnp.where(lane >= LANES - 2, outer, jnp.where(lane < 2, inner_part, 0.0))
        for step in (4, 8, 16, 32, 64):
            value = value + roll(value, step)
        return value

    zeta_left = everywhere(zeta[0, 0, top:end], zeta[0, 1, top:end])
    zeta_right = everywhere(zeta[0, halves, top:end], zeta[0, halves + 1, top:end])
    seam[0] = adjoint_seam(across_left(6) * zeta_left, across_right(6) * zeta_right)

    def finish(k, carry):
        windows = [
            [second[at(2, h, k), top + s : end + s] * zeta[0, h + 1, top + s : end + s] for s in (-2, -1, 0, 1, 2)]
            for h in range(halves)
        ]
        result = adjoint_level(k, windows, unpack(k, 0))
        for h in range(halves):
            i = h * depth + k
            theta_grad[k, :, h * LANES : (h + 1) * LANES] = theta_adj[i] + 0.2 * result[h]
            salt_grad[k, :, h * LANES : (h + 1) * LANES] = salt_adj[i] - 0.15 * result[h]
        return carry

    lax.fori_loop(0, depth, finish, 0)

    def finish_kappa(k, carry):
        for h in range(halves):
            i = h * depth + k
            kappa_grad[k, :, h * LANES : (h + 1) * LANES] = k_fixed[i] + k_zeta[i] * zeta[0, h + 1, top:end]
        return carry

    lax.fori_loop(0, depth - 1, finish_kappa, 0)
    for h in range(halves):
        z = zeta[0, h + 1, top:end]
        theta_top = second[at(0, h, 0), top:end] + 0.2 * z * second[at(2, h, 0), top:end]
        forcing_grad[:, h * LANES : (h + 1) * LANES] = z + wet_at(h, 0) * theta_top

    for copy, sends, _ in rims + stage_two:
        guarded(sends, copy.wait_send)

    def sent_sum(i, carry):
        sum_copy(i).wait_send()
        return carry

    lax.fori_loop(1, count, sent_sum, 0)


def shards(*args):
    theta, bottom = args[0], args[7]
    depth, rows, cols = theta.shape
    halves = cols // LANES
    count = lax.axis_size("trow") * lax.axis_size("tcol")
    tall = rows + 2 * RIM
    V = pltpu.VMEM
    DMA = pltpu.SemaphoreType.DMA
    flat = V((halves * depth, rows, LANES), F32)
    ints = V((halves * depth, rows, LANES), jnp.int32)
    upper = V((halves * (depth - 1), rows, LANES), F32)
    tile = V((7, rows, LANES), F32)
    scratch = [
        flat, flat, flat, flat, ints, upper, V((rows, cols), F32), flat, flat,
        V((tall, cols + 2 * LANES), F32), V((tall, cols + 2 * LANES), jnp.int32),
        V((halves * depth, rows + RIM, LANES), F32), V((halves * depth, RIM, LANES), F32),
        V((3 * halves * depth, tall, LANES), F32), V((3 * halves * depth, tall, LANES), F32),
        flat, flat, flat, flat, flat, flat, flat, flat, flat, flat,
        V((ITERS, halves + 2, tall, LANES), F32), tile, tile, tile, V((2, rows, LANES), F32),
        V((count, LANES), F32),
        DMA((3 + 8 * halves,)), DMA((16,)), DMA((16,)), DMA((9,)), DMA((9,)), DMA((count,)), DMA((count,)),
    ]
    outs = [(depth, rows, cols), (depth, rows, cols), (depth - 1, rows, cols), (rows, cols)]
    return tuple(
        pl.pallas_call(
            functools.partial(kernel, (depth, rows, cols)),
            out_shape=[jax.ShapeDtypeStruct(o, F32) for o in outs],
            in_specs=[pl.BlockSpec(memory_space=pltpu.HBM)] * len(args),
            out_specs=[pl.BlockSpec(memory_space=pltpu.VMEM)] * len(outs),
            scratch_shapes=scratch,
            compiler_params=pltpu.CompilerParams(
                collective_id=0, has_side_effects=True, vmem_limit_bytes=48 * 1024 * 1024
            ),
        )(*[pltpu.with_memory_space_constraint(a, pltpu.HBM) for a in args])
    )


def solution(mesh):
    cube, plane = P(None, "trow", "tcol"), P("trow", "tcol")
    in_specs = (cube,) * 6 + (plane,) * 2 + (cube,) * 2 + (plane,)
    out_specs = (cube,) * 3 + (plane,)
    return jax.shard_map(shards, mesh=mesh, in_specs=in_specs, out_specs=out_specs, check_vma=False)
```

```python
import functools
import jax
import jax.numpy as jnp
from jax import lax
from jax.experimental import pallas as pl
from jax.experimental.pallas import tpu as pltpu
from jax.sharding import PartitionSpec as P

ITERS = 4
LANES = 128
RIM = 8
LOW, HIGH = 0.2, 9.2
CENTRE, RADIUS = (HIGH + LOW) / 2, (HIGH - LOW) / 2
MESH = pl.DeviceIdType.MESH
F32 = jnp.float32


def put(out, k, value):
    out[k] = value if out[k] is None else out[k] + value


def times_operator(poly):
    out = [None] * (len(poly) + 1)
    for k, c in enumerate(poly):
        put(out, k, CENTRE * c)
        if k == 0:
            put(out, 1, RADIUS * c)
        else:
            half = (0.5 * RADIUS) * c
            put(out, k + 1, half)
            put(out, k - 1, half)
    return out


def inner(p, q, table):
    total = None
    for i, a in enumerate(p):
        part = None
        for j, b in enumerate(q):
            term = b * table[i][j]
            part = term if part is None else part + term
        part = a * part
        total = part if total is None else total + part
    return total


def add_scaled(p, scale, q):
    out = []
    for k in range(max(len(p), len(q))):
        if k >= len(p):
            out.append(scale * q[k])
        elif k >= len(q):
            out.append(p[k])
        else:
            out.append(p[k] + scale * q[k])
    return out


def weights_from(moments):
    table = [
        [
            moments[j] if i == 0 else moments[i] if j == 0 else 0.5 * (moments[i + j] + moments[abs(i - j)])
            for j in range(ITERS + 1)
        ]
        for i in range(ITERS)
    ]
    residual = [jnp.ones_like(moments[0])]
    direction = residual
    result = []
    norm_now = moments[0]
    for iteration in range(ITERS):
        image = times_operator(direction)
        step = norm_now / inner(direction, image, table)
        result = add_scaled(result, step, direction)
        if iteration + 1 < ITERS:
            residual = add_scaled(residual, -step, image)
            norm_next = inner(residual, residual, table)
            direction = add_scaled(residual, norm_next / norm_now, direction)
            norm_now = norm_next
    return result


def lane_index(rows):
    return lax.broadcasted_iota(jnp.int32, (rows, LANES), 1)


def roll(x, amount):
    return pltpu.roll(x, amount % LANES if isinstance(amount, int) else amount & (LANES - 1), 1)


def shifted(parts, rim, k, by, lane):
    if by > 0:
        turned = [roll(p, -by) for p in parts] + [roll(rim, LANES - 4 * k - by)]
        edge = LANES - by
    else:
        turned = [roll(rim, LANES - 4 * k - by)] + [roll(p, -by) for p in parts]
        edge = -by
    return [jnp.where(lane < edge, turned[h], turned[h + 1]) for h in range(len(parts))]


def by_groups(start, stop, group, body, carry):
    count = (stop - start) // group
    carry = lax.fori_loop(0, count, lambda i, c: body([start + i * group + u for u in range(group)], c), carry)
    rest = list(range(start + count * group, stop))
    return body(rest, carry) if rest else carry


def guarded(condition, action):
    @pl.when(condition)
    def _():
        action()


def solve_kernel(
    sizes,
    theta_in, salt_in, vx_in, vy_in, land_in, kappa_in, forcing_in, bottom_in, theta_cot_in, salt_cot_in, surface_in,
    cross, theta_adj, salt_adj, k_fixed, k_zeta, zeta, top_parts, sums,
    theta, salt, vx, vy, land, kappa, forcing, theta_cot, salt_cot,
    surface, bottom, wet, wet_after, first, second, open_y, inverse, link, ratio, theta_mix, salt_mix,
    seam_own, seam_left, seam_right, rim, slots,
    local_sem, rim_send, rim_recv, halo_send, halo_recv, sum_send, sum_recv,
):
    depth, rows, cols = sizes
    halves = cols // LANES
    top, end = RIM, RIM + rows
    mesh_rows, mesh_cols = lax.axis_size("trow"), lax.axis_size("tcol")
    count = mesh_rows * mesh_cols
    row, col = lax.axis_index("trow"), lax.axis_index("tcol")
    has_before, has_after = row > 0, row < mesh_rows - 1
    has_left, has_right = col > 0, col < mesh_cols - 1
    lane = lane_index(rows)
    spot = ((lane + 2) & 3) - 2
    blank = jnp.zeros((rows, LANES), F32)
    span = range(halves)

    def at(f, h, k):
        return (f * halves + h) * depth + k

    surface[...] = jnp.zeros_like(surface)
    bottom[...] = jnp.zeros_like(bottom)
    seam_left[...] = jnp.zeros_like(seam_left)
    seam_right[...] = jnp.zeros_like(seam_right)

    barrier = pltpu.get_barrier_semaphore()

    def others(action):
        for dc in range(1, mesh_cols):
            action(dc, (row, lax.rem(col + dc, mesh_cols)))

        def one_row(dr, carry):
            there = lax.rem(row + dr, mesh_rows)
            for dc in range(mesh_cols):
                action(dr * mesh_cols + dc, (there, lax.rem(col + dc, mesh_cols)))
            return carry

        lax.fori_loop(1, mesh_rows, one_row, 0)

    others(lambda i, device: pl.semaphore_signal(barrier, inc=1, device_id=device, device_id_type=MESH))

    started = []

    def fetch(src, dst):
        copy = pltpu.make_async_copy(src, dst, local_sem.at[len(started)])
        copy.start()
        started.append(copy)
        return copy

    middle = pl.ds(LANES, cols)
    get_surface = fetch(surface_in, surface.at[pl.ds(RIM, rows), middle])
    get_bottom = fetch(bottom_in, bottom.at[pl.ds(RIM, rows), middle])

    def fetch_halves(src, dst):
        return [
            fetch(src.at[:, :, pl.ds(h * LANES, LANES)], dst.at[pl.ds(h * src.shape[0], src.shape[0])]) for h in span
        ]

    get_land = fetch_halves(land_in, land)
    get_theta = fetch_halves(theta_in, theta)
    get_salt = fetch_halves(salt_in, salt)
    get_vx = fetch_halves(vx_in, vx)
    get_vy = fetch_halves(vy_in, vy)
    get_kappa = fetch_halves(kappa_in, kappa)
    get_theta_cot = fetch_halves(theta_cot_in, theta_cot)
    get_salt_cot = fetch_halves(salt_cot_in, salt_cot)
    get_forcing = fetch(forcing_in, forcing)

    def arrived(copies):
        for copy in copies:
            copy.wait()

    pl.semaphore_wait(barrier, count - 1)

    rims = []
    for dr in (-1, 0, 1):
        for dc in (-1, 0, 1):
            if dr == 0 and dc == 0:
                continue
            targets = [has_before] * (dr < 0) + [has_after] * (dr > 0) + [has_left] * (dc < 0) + [has_right] * (dc > 0)
            sources = [has_after] * (dr < 0) + [has_before] * (dr > 0) + [has_right] * (dc < 0) + [has_left] * (dc > 0)
            src_rows = pl.ds(0, RIM) if dr < 0 else pl.ds(rows - RIM, RIM) if dr > 0 else pl.ds(0, rows)
            src_cols = pl.ds(0, LANES) if dc < 0 else pl.ds(cols - LANES, LANES) if dc > 0 else pl.ds(0, cols)
            dst_rows = pl.ds(end, RIM) if dr < 0 else pl.ds(0, RIM) if dr > 0 else pl.ds(top, rows)
            dst_cols = pl.ds(LANES + cols, LANES) if dc < 0 else pl.ds(0, LANES) if dc > 0 else middle
            for src, dst in ((surface_in, surface), (bottom_in, bottom)):
                i = len(rims)
                copy = pltpu.make_async_remote_copy(
                    src_ref=src.at[src_rows, src_cols],
                    dst_ref=dst.at[dst_rows, dst_cols],
                    send_sem=rim_send.at[i],
                    recv_sem=rim_recv.at[i],
                    device_id=(row + dr, col + dc),
                    device_id_type=MESH,
                )
                rims.append((copy, functools.reduce(jnp.logical_and, targets), functools.reduce(jnp.logical_and, sources)))
    for copy, sends, _ in rims:
        guarded(sends, copy.start)

    arrived([get_bottom] + get_land)

    def wet_levels(levels, carry):
        for k in levels:
            for h in span:
                depth_here = bottom[top:end, LANES * (h + 1) : LANES * (h + 2)]
                wet[h * depth + k, 0:rows] = jnp.where(k < depth_here, land[h * depth + k].astype(F32), 0.0)
                wet[h * depth + k, rows : rows + RIM] = jnp.ones((RIM, LANES), F32)
        return carry

    by_groups(0, depth, 5, wet_levels, 0)

    def wet_at(h, k):
        return wet[h * depth + k, 0:rows]

    arrived(get_theta + get_salt + get_vx + get_vy)

    def pack(k, parts, packed):
        both = jnp.where(lane < LANES // 2, parts[0], parts[-1])
        here = ((lane + 2 - 4 * k) & (LANES - 1)) < 4
        return jnp.where(here, roll(both, 4 * k), packed)

    def prepare(levels, packs):
        for k in levels:
            wets = [wet_at(h, k) for h in span]
            qt, qs, uy = [], [], []
            for h in span:
                i = h * depth + k
                qt.append(theta[i] * wets[h])
                qs.append(salt[i] * wets[h])
                uy.append(vy[i])
                first[at(0, h, k), top:end] = qt[h]
                first[at(1, h, k), top:end] = qs[h]
                first[at(2, h, k), top:end] = vx[i] * wets[h] * wet[i, 1 : rows + 1] * (1.0 / 12.0)
            packs = tuple(pack(k, parts, packed) for parts, packed in zip((qt, qs, uy, wets), packs))
        return packs

    for f, packed in enumerate(by_groups(0, depth, 5, prepare, (blank,) * 4)):
        seam_own[f] = packed

    def remote(src, dst, i, device):
        return pltpu.make_async_remote_copy(
            src_ref=src, dst_ref=dst, send_sem=halo_send.at[i], recv_sem=halo_recv.at[i], device_id=device, device_id_type=MESH
        )

    after, before = (row + 1, col), (row - 1, col)
    right, left = (row, col + 1), (row, col - 1)
    low, high, below, above = pl.ds(end - 2, 2), pl.ds(top, 2), pl.ds(top - 2, 2), pl.ds(end, 2)
    stage_one = [
        (remote(first.at[:, low], first.at[:, below], 0, after), has_after, has_before),
        (remote(first.at[:, high], first.at[:, above], 1, before), has_before, has_after),
        (remote(wet.at[:, pl.ds(0, 1)], wet_after.at[:, pl.ds(0, 1)], 2, before), has_before, has_after),
        (remote(seam_own.at[pl.ds(0, 4)], seam_left.at[pl.ds(0, 4)], 3, right), has_right, has_left),
        (remote(seam_own.at[pl.ds(0, 4)], seam_right.at[pl.ds(0, 4)], 4, left), has_left, has_right),
    ]
    for copy, sends, _ in stage_one:
        guarded(sends, copy.start)

    def clear(missing, ref, start):
        @pl.when(missing)
        def _():
            ref[:, start : start + 2] = jnp.zeros((ref.shape[0], 2, LANES), F32)

    for ref in (first, second):
        clear(jnp.logical_not(has_before), ref, top - 2)
        clear(jnp.logical_not(has_after), ref, end)
    clear(jnp.logical_not(has_after), wet_after, 0)

    get_surface.wait()
    for copy, _, receives in rims:
        guarded(receives, copy.wait_recv)
    wide = (rows + 2 * RIM, cols + 2 * LANES)
    row_at = lax.broadcasted_iota(jnp.int32, wide, 0) - RIM + row * rows
    col_at = lax.broadcasted_iota(jnp.int32, wide, 1) - LANES + col * cols
    inside = ((row_at >= 0) & (row_at < rows * mesh_rows)) & ((col_at >= 0) & (col_at < cols * mesh_cols))
    scaled = (bottom[...].astype(F32) * (1.0 / depth) + (4.2 - CENTRE)) * (1.0 / RADIUS)
    basis = [surface[...]]
    for k in range(ITERS):
        field = basis[-1]
        beside = (pltpu.roll(field, 1, 0) + pltpu.roll(field, wide[0] - 1, 0)) + (
            pltpu.roll(field, 1, 1) + pltpu.roll(field, wide[1] - 1, 1)
        )
        image = scaled * field - beside * (1.0 / RADIUS)
        if k > 0:
            image = 2.0 * image - basis[-2]
        basis.append(jnp.where(inside, image, 0.0))

    def own_product(a, b):
        product = basis[a][top:end, LANES : LANES + cols] * basis[b][top:end, LANES : LANES + cols]
        tiles = [product[i : i + 8, j : j + LANES] for i in range(0, rows, 8) for j in range(0, cols, LANES)]
        return functools.reduce(jnp.add, tiles)

    partial = [own_product(a, b) for a, b in ((0, 0), (0, 1), (0, 2), (0, 3), (0, 4), (2, 3), (3, 3), (3, 4))]
    small_lane = lane_index(8)
    width = LANES // 2
    while len(partial) > 1:
        half = len(partial) // 2
        take_first = (small_lane & (2 * width - 1)) < width
        partial = [
            jnp.where(take_first, a + roll(a, -width), b + roll(b, width)) for a, b in zip(partial[:half], partial[half:])
        ]
        width //= 2
    slots[0:1] = jnp.sum(partial[0], axis=0, keepdims=True)

    def sum_copy(i, device):
        return pltpu.make_async_remote_copy(
            src_ref=slots.at[pl.ds(0, 1)],
            dst_ref=slots.at[pl.ds(i, 1)],
            send_sem=sum_send.at[i],
            recv_sem=sum_recv.at[i],
            device_id=device,
            device_id_type=MESH,
        )

    others(lambda i, device: sum_copy(i, device).start())
    for k in range(ITERS):
        for h in range(halves + 2):
            zeta[k * (halves + 2) + h] = basis[k][:, h * LANES : (h + 1) * LANES]

    arrived(get_kappa + get_theta_cot + get_salt_cot)

    def down_level(k, last, carry):
        out = []
        for h in span:
            num, den, couple_before, yt, ys, yw = carry[h]
            i = h * depth + k
            wet_here = wet_at(h, k)
            if last:
                den_next = num_next = num
                couple = couple_before
            else:
                couple = kappa[h * (depth - 1) + k] * wet_here * wet_at(h, k + 1)
                den_next = num + couple * den
                num_next = den_next + couple * num
            inv = den * (1.0 / den_next)
            lower = couple_before * inv
            inverse[i] = inv
            link[i] = lower
            if not last:
                ratio[i] = couple * inv
            yt = theta_cot[i] * inv + lower * yt
            ys = salt_cot[i] * inv + lower * ys
            yw = wet_here * inv + lower * yw
            second[at(0, h, k), top:end] = yt
            second[at(1, h, k), top:end] = ys
            second[at(2, h, k), top:end] = yw
            out.append((num_next, den_next, couple, yt, ys, yw))
        return tuple(out)

    def down(levels, carry):
        for k in levels:
            carry = down_level(k, False, carry)
        return carry

    one = jnp.ones((rows, LANES), F32)
    carry = by_groups(0, depth - 1, 4, down, ((one, one, blank, blank, blank, blank),) * halves)
    carry = down_level(depth - 1, True, carry)

    def up(steps, values):
        for n in steps:
            k = depth - 2 - n
            new = []
            for f in range(3):
                parts = []
                for h in span:
                    x = second[at(f, h, k), top:end] + ratio[h * depth + k] * values[f][h]
                    second[at(f, h, k), top:end] = x
                    parts.append(x)
                new.append(tuple(parts))
            values = tuple(new)
        return values

    by_groups(0, depth - 1, 4, up, tuple(tuple(carry[h][3 + f] for h in span) for f in range(3)))

    def pack_second(levels, packs):
        for k in levels:
            packs = tuple(pack(k, [second[at(f, h, k), top:end] for h in span], packs[f]) for f in range(3))
        return packs

    for f, packed in enumerate(by_groups(0, depth, 5, pack_second, (blank,) * 3)):
        seam_own[4 + f] = packed
    stage_two = [
        (remote(second.at[:, low], second.at[:, below], 5, after), has_after, has_before),
        (remote(second.at[:, high], second.at[:, above], 6, before), has_before, has_after),
        (remote(seam_own.at[pl.ds(4, 3)], seam_left.at[pl.ds(4, 3)], 7, right), has_right, has_left),
        (remote(seam_own.at[pl.ds(4, 3)], seam_right.at[pl.ds(4, 3)], 8, left), has_left, has_right),
    ]
    for copy, sends, _ in stage_two:
        guarded(sends, copy.start)

    for copy, sends, receives in stage_one:
        guarded(sends, copy.wait_send)
        guarded(receives, copy.wait_recv)
    faces = 2 * halves * depth
    first[faces:, top - 1 : top] = first[faces:, top - 1 : top] * wet[:, 0:1]
    first[faces:, end - 1 : end] = first[faces:, end - 1 : end] * wet_after[:, 0:1]

    def open_across(uy, near):
        return uy * near * roll(near, -1) * (1.0 / 12.0)

    inner_side = spot < 0
    rim[0] = jnp.where(inner_side, seam_left[0], seam_right[0])
    rim[1] = jnp.where(inner_side, seam_left[1], seam_right[1])
    rim[3] = jnp.where(inner_side, seam_left[3], seam_right[3])
    open_left = open_across(seam_left[2], jnp.where(inner_side, seam_left[3], seam_own[3]))
    open_right = open_across(seam_right[2], seam_right[3])
    rim[2] = jnp.where(inner_side, open_left, open_right)

    def open_columns(levels, carry):
        ahead = [shifted([wet_at(h, k) for h in span], rim[3], k, 1, lane) for k in levels]
        for k, wets_ahead in zip(levels, ahead):
            for h in span:
                i = h * depth + k
                open_y[i] = vy[i] * wet_at(h, k) * wets_ahead[h] * (1.0 / 12.0)
        return carry

    by_groups(0, depth, 5, open_columns, 0)
    get_forcing.wait()
    for h in span:
        theta[h * depth] = theta[h * depth] + forcing[:, h * LANES : (h + 1) * LANES] * wet_at(h, 0)

    def column_shifts(ref, f, k, edges):
        centre = [ref[at(f, h, k), top:end] for h in span]
        return {s: shifted(centre, edges, k, s, lane) for s in (-2, -1, 1, 2)}

    def face_shifts(k, steps):
        centre = [open_y[h * depth + k] for h in span]
        return {s: shifted(centre, rim[2], k, s, lane) for s in steps}

    def forward_down(levels, carry):
        moved = [(face_shifts(k, (-1,)), [column_shifts(first, f, k, rim[f]) for f in range(2)]) for k in levels]
        for k, (uy, turned) in zip(levels, moved):
            out = []
            for h in span:
                i = h * depth + k
                found = []
                for f, raw in ((0, theta), (1, salt)):
                    q = [first[at(f, h, k), top + s : end + s] for s in (-2, -1, 0, 1, 2)]
                    c = turned[f]
                    row_here = first[at(2, h, k), top:end] * (7.0 * (q[2] + q[3]) - (q[1] + q[4]))
                    row_back = first[at(2, h, k), top - 1 : end - 1] * (7.0 * (q[1] + q[2]) - (q[0] + q[3]))
                    col_here = open_y[i] * (7.0 * (q[2] + c[1][h]) - (c[-1][h] + c[2][h]))
                    col_back = uy[-1][h] * (7.0 * (c[-1][h] + q[2]) - (c[-2][h] + c[1][h]))
                    value = raw[i] - (row_here - row_back) - (col_here - col_back)
                    found.append(value * inverse[i] + link[i] * carry[h][f])
                theta_mix[i] = found[0]
                salt_mix[i] = found[1]
                out.append(tuple(found))
            carry = tuple(out)
        return carry

    carry = by_groups(0, depth, 5, forward_down, ((blank, blank),) * halves)

    def forward_up(steps, carry):
        for n in steps:
            k = depth - 2 - n
            out = []
            for h in span:
                i = h * depth + k
                xt = theta_mix[i] + ratio[i] * carry[h][0]
                xs = salt_mix[i] + ratio[i] * carry[h][1]
                dt, ds = xt - carry[h][0], xs - carry[h][1]
                step_t, step_s, step_w = [
                    second[at(f, h, k), top:end] - second[at(f, h, k + 1), top:end] for f in range(3)
                ]
                closed = -wet_at(h, k) * wet_at(h, k + 1)
                k_fixed[h * (depth - 1) + k] = closed * (step_t * dt + step_s * ds)
                k_zeta[h * (depth - 1) + k] = closed * step_w * (0.2 * dt - 0.15 * ds)
                out.append((xt, xs))
            carry = tuple(out)
        return carry

    by_groups(0, depth - 1, 4, forward_up, carry)

    for copy, _, receives in stage_two:
        guarded(receives, copy.wait_recv)
    for f in range(3):
        rim[4 + f] = jnp.where(inner_side, seam_left[4 + f], seam_right[4 + f])

    def arms(u, wets):
        v = [wets * x for x in u]
        back, here = 7.0 * v[1], 7.0 * v[2]
        return v[0], -(back + v[0]), back - here, here + v[3], -v[3]

    def adjoint(levels, carry):
        moved = [
            (face_shifts(k, (-2, -1, 1)), [column_shifts(second, f, k, rim[4 + f]) for f in range(3)]) for k in levels
        ]
        for k, (uy, turned) in zip(levels, moved):
            for h in span:
                i = h * depth + k
                wets = wet_at(h, k)
                r = arms([first[at(2, h, k), top + s : end + s] for s in (-2, -1, 0, 1)], wets)
                c = arms([uy[-2][h], uy[-1][h], open_y[i], uy[1][h]], wets)
                weights = [(1.0 + r[2]) + c[2], r[0], r[1], r[3], r[4], c[0], c[1], c[3], c[4]]
                for f in range(3):
                    values = [second[at(f, h, k), top + s : end + s] for s in (0, -2, -1, 1, 2)]
                    values += [turned[f][s][h] for s in (-2, -1, 1, 2)]
                    terms = [w * m for w, m in zip(weights, values)]
                    if f == 2:
                        for n in range(9):
                            cross[at(n, h, k)] = terms[n]
                    else:
                        pairs = [terms[n] + terms[n + 1] for n in range(1, 9, 2)]
                        total = terms[0] + ((pairs[0] + pairs[1]) + (pairs[2] + pairs[3]))
                        (theta_adj, salt_adj)[f][i] = total
        return carry

    by_groups(0, depth, 5, adjoint, 0)
    for h in span:
        top_parts[h] = wet_at(h, 0) * second[at(0, h, 0), top:end]
        top_parts[halves + h] = 1.0 + 0.2 * (wet_at(h, 0) * second[at(2, h, 0), top:end])

    others(lambda i, device: sum_copy(i, device).wait_recv())
    sums[...] = jnp.broadcast_to(jnp.sum(slots[...], axis=0, keepdims=True), sums.shape)
    for copy, sends, _ in rims + stage_two:
        guarded(sends, copy.wait_send)
    others(lambda i, device: sum_copy(i, device).wait_send())


def finish_kernel(
    sizes,
    cross, theta_adj, salt_adj, k_fixed, k_zeta, basis, top_parts, sums,
    theta_out, salt_out, kappa_out, forcing_out,
    zeta, theta_grad, salt_grad, kappa_grad, forcing_grad, sems,
):
    depth, rows, cols = sizes
    halves = cols // LANES
    top, end = RIM, RIM + rows
    span = range(halves)
    lane = lane_index(rows)
    total = sums[...]
    for step in (8, 4, 2, 1):
        total = total + roll(total, -step)
    m = [jnp.broadcast_to(total[:, 16 * g : 16 * g + 1], (8, LANES)) for g in range(8)]
    m = m[:5] + [2.0 * m[5] - m[1], 2.0 * m[6] - m[0], 2.0 * m[7] - m[1]]
    weights = [jnp.concatenate([w] * ((rows + 2 * RIM) // 8), axis=0) for w in weights_from(m)]
    tiles = halves + 2
    for h in range(tiles):
        b = [basis[k * tiles + h] for k in range(ITERS)]
        zeta[h] = (weights[0] * b[0] + weights[1] * b[1]) + (weights[2] * b[2] + weights[3] * b[3])
    level = [zeta[h, top:end] for h in range(tiles)]
    around = []
    for h in span:
        near = [level[h + 1]] + [zeta[h + 1, top + s : end + s] for s in (-2, -1, 1, 2)]
        for s in (-2, -1, 1, 2):
            if s > 0:
                near.append(jnp.where(lane < LANES - s, roll(level[h + 1], -s), roll(level[h + 2], -s)))
            else:
                near.append(jnp.where(lane < -s, roll(level[h], -s), roll(level[h + 1], -s)))
        around.append(near)
    for h in span:
        forcing_grad[:, h * LANES : (h + 1) * LANES] = top_parts[h] + around[h][0] * top_parts[halves + h]
    put_forcing = pltpu.make_async_copy(forcing_grad, forcing_out, sems.at[0])
    put_forcing.start()
    group = 5
    groups = depth // group
    copies = [put_forcing]
    for g in range(groups + (depth % group > 0)):
        for k in range(g * group, min(depth, (g + 1) * group)):
            for h in span:
                i = h * depth + k
                where = slice(h * LANES, (h + 1) * LANES)
                terms = [cross[(n * halves + h) * depth + k] * around[h][n] for n in range(9)]
                pairs = [terms[n] + terms[n + 1] for n in range(1, 9, 2)]
                change = terms[0] + ((pairs[0] + pairs[1]) + (pairs[2] + pairs[3]))
                theta_grad[k, :, where] = theta_adj[i] + 0.2 * change
                salt_grad[k, :, where] = salt_adj[i] - 0.15 * change
                if k < depth - 1:
                    j = h * (depth - 1) + k
                    kappa_grad[k, :, where] = k_fixed[j] + k_zeta[j] * around[h][0]
        for src, dst in ((theta_grad, theta_out), (salt_grad, salt_out), (kappa_grad, kappa_out)):
            first, last = g * group, min(src.shape[0], (g + 1) * group)
            if first < last:
                part = pl.ds(first, last - first)
                copy = pltpu.make_async_copy(src.at[part], dst.at[part], sems.at[len(copies)])
                copy.start()
                copies.append(copy)
    for copy in copies:
        copy.wait()


def shards(*args):
    theta = args[0]
    depth, rows, cols = theta.shape
    halves = cols // LANES
    count = lax.axis_size("trow") * lax.axis_size("tcol")
    tall = rows + 2 * RIM
    V = pltpu.VMEM
    DMA = pltpu.SemaphoreType.DMA
    flat = V((halves * depth, rows, LANES), F32)
    ints = V((halves * depth, rows, LANES), jnp.int32)
    upper = V((halves * (depth - 1), rows, LANES), F32)
    tile = V((7, rows, LANES), F32)
    scratch = [
        flat, flat, flat, flat, ints, upper, V((rows, cols), F32), flat, flat,
        V((tall, cols + 2 * LANES), F32), V((tall, cols + 2 * LANES), jnp.int32),
        V((halves * depth, rows + RIM, LANES), F32), V((halves * depth, RIM, LANES), F32),
        V((3 * halves * depth, tall, LANES), F32), V((3 * halves * depth, tall, LANES), F32),
        flat, flat, flat, flat, flat, flat,
        tile, tile, tile, tile, V((count, LANES), F32),
        DMA((3 + 8 * halves,)), DMA((16,)), DMA((16,)), DMA((9,)), DMA((9,)), DMA((count,)), DMA((count,)),
    ]
    parts = [
        (9 * halves * depth, rows, LANES), (halves * depth, rows, LANES), (halves * depth, rows, LANES),
        (halves * (depth - 1), rows, LANES), (halves * (depth - 1), rows, LANES),
        (ITERS * (halves + 2), tall, LANES), (2 * halves, rows, LANES), (8, LANES),
    ]
    found = pl.pallas_call(
        functools.partial(solve_kernel, (depth, rows, cols)),
        out_shape=[jax.ShapeDtypeStruct(o, F32) for o in parts],
        in_specs=[pl.BlockSpec(memory_space=pltpu.HBM)] * len(args),
        out_specs=[pl.BlockSpec(memory_space=V)] * len(parts),
        scratch_shapes=scratch,
        compiler_params=pltpu.CompilerParams(
            collective_id=0, has_side_effects=True, vmem_limit_bytes=40 * 1024 * 1024
        ),
    )(*[pltpu.with_memory_space_constraint(a, pltpu.HBM) for a in args])
    outs = [(depth, rows, cols), (depth, rows, cols), (depth - 1, rows, cols), (rows, cols)]
    return tuple(
        pl.pallas_call(
            functools.partial(finish_kernel, (depth, rows, cols)),
            out_shape=[jax.ShapeDtypeStruct(o, F32) for o in outs],
            in_specs=[pl.BlockSpec(memory_space=V)] * len(parts),
            out_specs=[pl.BlockSpec(memory_space=pltpu.HBM)] * len(outs),
            scratch_shapes=[V((halves + 2, tall, LANES), F32)] + [V(o, F32) for o in outs] + [DMA((1 + 3 * (depth // 5 + 1),))],
            compiler_params=pltpu.CompilerParams(vmem_limit_bytes=16 * 1024 * 1024),
        )(*found)
    )


def solution(mesh):
    cube, plane = P(None, "trow", "tcol"), P("trow", "tcol")
    in_specs = (cube,) * 6 + (plane,) * 2 + (cube,) * 2 + (plane,)
    out_specs = (cube,) * 3 + (plane,)
    return jax.shard_map(shards, mesh=mesh, in_specs=in_specs, out_specs=out_specs, check_vma=False)
```

```python
import functools
import jax
import jax.numpy as jnp
from jax import lax
from jax.experimental import pallas as pl
from jax.experimental.pallas import tpu as pltpu
from jax.sharding import PartitionSpec as P

ITERS = 4
LANES = 128
RIM = 8
LOW, HIGH = 0.2, 9.2
CENTRE, RADIUS = (HIGH + LOW) / 2, (HIGH - LOW) / 2
MESH = pl.DeviceIdType.MESH
F32 = jnp.float32


def put(out, k, value):
    out[k] = value if out[k] is None else out[k] + value


def times_operator(poly):
    out = [None] * (len(poly) + 1)
    for k, c in enumerate(poly):
        put(out, k, CENTRE * c)
        if k == 0:
            put(out, 1, RADIUS * c)
        else:
            half = (0.5 * RADIUS) * c
            put(out, k + 1, half)
            put(out, k - 1, half)
    return out


def inner(p, q, table):
    total = None
    for i, a in enumerate(p):
        part = None
        for j, b in enumerate(q):
            term = b * table[i][j]
            part = term if part is None else part + term
        part = a * part
        total = part if total is None else total + part
    return total


def add_scaled(p, scale, q):
    out = []
    for k in range(max(len(p), len(q))):
        if k >= len(p):
            out.append(scale * q[k])
        elif k >= len(q):
            out.append(p[k])
        else:
            out.append(p[k] + scale * q[k])
    return out


def weights_from(moments):
    table = [
        [
            moments[j] if i == 0 else moments[i] if j == 0 else 0.5 * (moments[i + j] + moments[abs(i - j)])
            for j in range(ITERS + 1)
        ]
        for i in range(ITERS)
    ]
    residual = [jnp.ones_like(moments[0])]
    direction = residual
    result = []
    norm_now = moments[0]
    for iteration in range(ITERS):
        image = times_operator(direction)
        step = norm_now / inner(direction, image, table)
        result = add_scaled(result, step, direction)
        if iteration + 1 < ITERS:
            residual = add_scaled(residual, -step, image)
            norm_next = inner(residual, residual, table)
            direction = add_scaled(residual, norm_next / norm_now, direction)
            norm_now = norm_next
    return result


def lane_index(rows):
    return lax.broadcasted_iota(jnp.int32, (rows, LANES), 1)


def roll(x, amount):
    return pltpu.roll(x, amount % LANES if isinstance(amount, int) else amount & (LANES - 1), 1)


def shifted(parts, ends, by, lane):
    if by > 0:
        joined = [jnp.where(lane < by, nearby, p) for p, nearby in zip(parts, parts[1:] + [ends])]
    else:
        joined = [jnp.where(lane >= LANES + by, nearby, p) for p, nearby in zip(parts, [ends] + parts[:-1])]
    return [roll(p, -by) for p in joined]


GROUP = 5


def by_groups(start, stop, group, body, carry):
    count = (stop - start) // group
    carry = lax.fori_loop(0, count, lambda i, c: body([start + i * group + u for u in range(group)], c), carry)
    rest = list(range(start + count * group, stop))
    return body(rest, carry) if rest else carry


def signed_sum(terms):
    return terms[0] + (((terms[1] + terms[2]) - (terms[5] + terms[6])) + ((terms[3] + terms[4]) - (terms[7] + terms[8])))


def guarded(condition, action):
    @pl.when(condition)
    def _():
        action()


def solve_kernel(
    sizes,
    theta_in, salt_in, vx_in, vy_in, land_in, kappa_in, forcing_in, bottom_in, theta_cot_in, salt_cot_in, surface_in,
    cross, theta_adj, salt_adj, k_fixed, k_zeta, zeta, top_parts, sums,
    theta, salt, vx, vy, land, kappa, forcing, theta_cot, salt_cot,
    surface, bottom, wet, wet_after, first, second, open_y, inverse, link, ratio, theta_mix, salt_mix,
    seam_own, seam_left, seam_right, ends, slots,
    local_sem, rim_send, rim_recv, halo_send, halo_recv, sum_send, sum_recv,
):
    depth, rows, cols = sizes
    halves = cols // LANES
    top, end = RIM, RIM + rows
    mesh_rows, mesh_cols = lax.axis_size("trow"), lax.axis_size("tcol")
    count = mesh_rows * mesh_cols
    row, col = lax.axis_index("trow"), lax.axis_index("tcol")
    has_before, has_after = row > 0, row < mesh_rows - 1
    has_left, has_right = col > 0, col < mesh_cols - 1
    lane = lane_index(rows)
    spot = ((lane + 2) & 3) - 2
    blank = jnp.zeros((rows, LANES), F32)
    span = range(halves)

    chunks = depth // GROUP
    per_chunk = 3 * halves * GROUP

    def at(f, h, k):
        return (k * 3 + f) * halves + h

    surface[...] = jnp.zeros_like(surface)
    bottom[...] = jnp.zeros_like(bottom)
    seam_left[...] = jnp.zeros_like(seam_left)
    seam_right[...] = jnp.zeros_like(seam_right)

    barrier = pltpu.get_barrier_semaphore()

    def others(action):
        for dc in range(1, mesh_cols):
            action(dc, (row, lax.rem(col + dc, mesh_cols)))

        def one_row(dr, carry):
            there = lax.rem(row + dr, mesh_rows)
            for dc in range(mesh_cols):
                action(dr * mesh_cols + dc, (there, lax.rem(col + dc, mesh_cols)))
            return carry

        lax.fori_loop(1, mesh_rows, one_row, 0)

    others(lambda i, device: pl.semaphore_signal(barrier, inc=1, device_id=device, device_id_type=MESH))

    started = []

    def fetch(src, dst):
        copy = pltpu.make_async_copy(src, dst, local_sem.at[len(started)])
        copy.start()
        started.append(copy)
        return copy

    middle = pl.ds(LANES, cols)
    get_surface = fetch(surface_in, surface.at[pl.ds(RIM, rows), middle])
    get_bottom = fetch(bottom_in, bottom.at[pl.ds(RIM, rows), middle])

    def fetch_halves(src, dst):
        return [
            fetch(src.at[:, :, pl.ds(h * LANES, LANES)], dst.at[pl.ds(h * src.shape[0], src.shape[0])]) for h in span
        ]

    get_land = fetch_halves(land_in, land)
    get_theta = fetch_halves(theta_in, theta)
    get_salt = fetch_halves(salt_in, salt)
    get_vx = fetch_halves(vx_in, vx)
    get_vy = fetch_halves(vy_in, vy)
    get_forcing = fetch(forcing_in, forcing)
    get_kappa = fetch_halves(kappa_in, kappa)
    get_theta_cot = fetch_halves(theta_cot_in, theta_cot)
    get_salt_cot = fetch_halves(salt_cot_in, salt_cot)

    def arrived(copies):
        for copy in copies:
            copy.wait()

    arrived([get_bottom] + get_land)

    def wet_levels(levels, carry):
        for k in levels:
            for h in span:
                depth_here = bottom[top:end, LANES * (h + 1) : LANES * (h + 2)]
                wet[h * depth + k, 0:rows] = jnp.where(k < depth_here, land[h * depth + k].astype(F32), 0.0)
                wet[h * depth + k, rows : rows + RIM] = jnp.ones((RIM, LANES), F32)
        return carry

    by_groups(0, depth, 5, wet_levels, 0)

    def wet_at(h, k):
        return wet[h * depth + k, 0:rows]

    arrived(get_theta + get_salt + get_vx + get_vy)

    def pack(k, parts, packed):
        both = jnp.where(lane < LANES // 2, parts[0], parts[-1])
        here = ((lane + 2 - 4 * k) & (LANES - 1)) < 4
        return jnp.where(here, roll(both, 4 * k), packed)

    def prepare(levels, packs):
        for k in levels:
            wets = [wet_at(h, k) for h in span]
            qt, qs, uy = [], [], []
            for h in span:
                i = h * depth + k
                qt.append(theta[i] * wets[h])
                qs.append(salt[i] * wets[h])
                uy.append(vy[i])
                first[at(0, h, k), top:end] = qt[h]
                first[at(1, h, k), top:end] = qs[h]
                first[at(2, h, k), top:end] = vx[i] * wets[h] * wet[i, 1 : rows + 1] * (1.0 / 12.0)
            packs = tuple(pack(k, parts, packed) for parts, packed in zip((qt, qs, uy, wets), packs))
        return packs

    for f, packed in enumerate(by_groups(0, depth, 5, prepare, (blank,) * 4)):
        seam_own[f] = packed

    pl.semaphore_wait(barrier, count - 1)

    rims = []
    for dr in (-1, 0, 1):
        for dc in (-1, 0, 1):
            if dr == 0 and dc == 0:
                continue
            targets = [has_before] * (dr < 0) + [has_after] * (dr > 0) + [has_left] * (dc < 0) + [has_right] * (dc > 0)
            sources = [has_after] * (dr < 0) + [has_before] * (dr > 0) + [has_right] * (dc < 0) + [has_left] * (dc > 0)
            src_rows = pl.ds(0, RIM) if dr < 0 else pl.ds(rows - RIM, RIM) if dr > 0 else pl.ds(0, rows)
            src_cols = pl.ds(0, LANES) if dc < 0 else pl.ds(cols - LANES, LANES) if dc > 0 else pl.ds(0, cols)
            dst_rows = pl.ds(end, RIM) if dr < 0 else pl.ds(0, RIM) if dr > 0 else pl.ds(top, rows)
            dst_cols = pl.ds(LANES + cols, LANES) if dc < 0 else pl.ds(0, LANES) if dc > 0 else middle
            for src, dst in ((surface_in, surface), (bottom_in, bottom)):
                i = len(rims)
                copy = pltpu.make_async_remote_copy(
                    src_ref=src.at[src_rows, src_cols],
                    dst_ref=dst.at[dst_rows, dst_cols],
                    send_sem=rim_send.at[i],
                    recv_sem=rim_recv.at[i],
                    device_id=(row + dr, col + dc),
                    device_id_type=MESH,
                )
                rims.append((copy, functools.reduce(jnp.logical_and, targets), functools.reduce(jnp.logical_and, sources)))
    for copy, sends, _ in rims:
        guarded(sends, copy.start)

    def remote(src, dst, i, device):
        return pltpu.make_async_remote_copy(
            src_ref=src, dst_ref=dst, send_sem=halo_send.at[i], recv_sem=halo_recv.at[i], device_id=device, device_id_type=MESH
        )

    after, before = (row + 1, col), (row - 1, col)
    right, left = (row, col + 1), (row, col - 1)
    def row_copies(ref, base, g):
        part = pl.ds(g * per_chunk, per_chunk)
        return [
            (remote(ref.at[part, pl.ds(end - 2, 2)], ref.at[part, pl.ds(top - 2, 2)], base + g, after), has_after, has_before),
            (remote(ref.at[part, pl.ds(top, 2)], ref.at[part, pl.ds(end, 2)], base + chunks + g, before), has_before, has_after),
        ]

    def edge_copies(first_field, fields, base):
        part = pl.ds(first_field, fields)
        return [
            (remote(seam_own.at[part], seam_left.at[part], base, right), has_right, has_left),
            (remote(seam_own.at[part], seam_right.at[part], base + 1, left), has_left, has_right),
        ]

    def send_rows(ref, base):
        for g in range(chunks):
            for copy, sends, _ in row_copies(ref, base, g):
                guarded(sends, copy.start)

    edges_one, edges_two = edge_copies(0, 4, 0), edge_copies(4, 3, 2)
    wet_copy = remote(wet.at[:, pl.ds(0, 1)], wet_after.at[:, pl.ds(0, 1)], 4, before)
    rows_one, rows_two = 5, 5 + 2 * chunks
    for copy, sends, _ in edges_one + [(wet_copy, has_before, has_after)]:
        guarded(sends, copy.start)
    send_rows(first, rows_one)

    def clear(missing, ref, start):
        @pl.when(missing)
        def _():
            ref[:, start : start + 2] = jnp.zeros((ref.shape[0], 2, LANES), F32)

    for ref in (first, second):
        clear(jnp.logical_not(has_before), ref, top - 2)
        clear(jnp.logical_not(has_after), ref, end)
    clear(jnp.logical_not(has_after), wet_after, 0)

    arrived(get_kappa + get_theta_cot + get_salt_cot)

    def down_level(k, last, carry):
        out = []
        for h in span:
            num, den, couple_before, yt, ys, yw = carry[h]
            i = h * depth + k
            wet_here = wet_at(h, k)
            if last:
                den_next = num_next = num
                couple = couple_before
            else:
                couple = kappa[h * (depth - 1) + k] * wet_here * wet_at(h, k + 1)
                den_next = num + couple * den
                num_next = den_next + couple * num
            inv = den * (1.0 / den_next)
            lower = couple_before * inv
            inverse[i] = inv
            link[i] = lower
            if not last:
                ratio[i] = couple * inv
            yt = theta_cot[i] * inv + lower * yt
            ys = salt_cot[i] * inv + lower * ys
            yw = wet_here * inv + lower * yw
            second[at(0, h, k), top:end] = yt
            second[at(1, h, k), top:end] = ys
            second[at(2, h, k), top:end] = yw
            out.append((num_next, den_next, couple, yt, ys, yw))
        return tuple(out)

    def down(levels, carry):
        for k in levels:
            carry = down_level(k, False, carry)
        return carry

    one = jnp.ones((rows, LANES), F32)
    carry = by_groups(0, depth - 1, 4, down, ((one, one, blank, blank, blank, blank),) * halves)
    carry = down_level(depth - 1, True, carry)

    def up(steps, values):
        for n in steps:
            k = depth - 2 - n
            new = []
            for f in range(3):
                parts = []
                for h in span:
                    x = second[at(f, h, k), top:end] + ratio[h * depth + k] * values[f][h]
                    second[at(f, h, k), top:end] = x
                    parts.append(x)
                new.append(tuple(parts))
            values = tuple(new)
        return values

    by_groups(0, depth - 1, 4, up, tuple(tuple(carry[h][3 + f] for h in span) for f in range(3)))

    def pack_second(levels, packs):
        for k in levels:
            packs = tuple(pack(k, [second[at(f, h, k), top:end] for h in span], packs[f]) for f in range(3))
        return packs

    for f, packed in enumerate(by_groups(0, depth, 5, pack_second, (blank,) * 3)):
        seam_own[4 + f] = packed
    for copy, sends, _ in edges_two:
        guarded(sends, copy.start)
    send_rows(second, rows_two)

    get_surface.wait()
    for copy, _, receives in rims:
        guarded(receives, copy.wait_recv)
    wide = (rows + 2 * RIM, cols + 2 * LANES)
    row_at = lax.broadcasted_iota(jnp.int32, wide, 0) - RIM + row * rows
    col_at = lax.broadcasted_iota(jnp.int32, wide, 1) - LANES + col * cols
    inside = ((row_at >= 0) & (row_at < rows * mesh_rows)) & ((col_at >= 0) & (col_at < cols * mesh_cols))
    scaled = (bottom[...].astype(F32) * (1.0 / depth) + (4.2 - CENTRE)) * (1.0 / RADIUS)
    basis = [surface[...]]
    for k in range(ITERS):
        field = basis[-1]
        beside = (pltpu.roll(field, 1, 0) + pltpu.roll(field, wide[0] - 1, 0)) + (
            pltpu.roll(field, 1, 1) + pltpu.roll(field, wide[1] - 1, 1)
        )
        image = scaled * field - beside * (1.0 / RADIUS)
        if k > 0:
            image = 2.0 * image - basis[-2]
        basis.append(jnp.where(inside, image, 0.0))

    def own_product(a, b):
        product = basis[a][top:end, LANES : LANES + cols] * basis[b][top:end, LANES : LANES + cols]
        tiles = [product[i : i + 8, j : j + LANES] for i in range(0, rows, 8) for j in range(0, cols, LANES)]
        return functools.reduce(jnp.add, tiles)

    partial = [own_product(a, b) for a, b in ((0, 0), (0, 1), (0, 2), (0, 3), (0, 4), (2, 3), (3, 3), (3, 4))]
    small_lane = lane_index(8)
    width = LANES // 2
    while len(partial) > 1:
        half = len(partial) // 2
        take_first = (small_lane & (2 * width - 1)) < width
        partial = [
            jnp.where(take_first, a + roll(a, -width), b + roll(b, width)) for a, b in zip(partial[:half], partial[half:])
        ]
        width //= 2
    slots[0:1] = jnp.sum(partial[0], axis=0, keepdims=True)

    def sum_copy(i, device):
        return pltpu.make_async_remote_copy(
            src_ref=slots.at[pl.ds(0, 1)],
            dst_ref=slots.at[pl.ds(i, 1)],
            send_sem=sum_send.at[i],
            recv_sem=sum_recv.at[i],
            device_id=device,
            device_id_type=MESH,
        )

    others(lambda i, device: sum_copy(i, device).start())
    for k in range(ITERS):
        for h in range(halves + 2):
            zeta[k * (halves + 2) + h] = basis[k][:, h * LANES : (h + 1) * LANES]

    for copy, sends, receives in edges_one + [(wet_copy, has_before, has_after)]:
        guarded(sends, copy.wait_send)
        guarded(receives, copy.wait_recv)

    def open_across(uy, near):
        return uy * near * roll(near, -1) * (1.0 / 12.0)

    inner_side = spot < 0
    open_left = open_across(seam_left[2], jnp.where(inner_side, seam_left[3], seam_own[3]))
    open_right = open_across(seam_right[2], seam_right[3])

    def unpack(fields):
        def one_group(levels, carry):
            for k in levels:
                for f, packed in fields:
                    ends[f * depth + k] = roll(packed, LANES - 4 * k)
            return carry

        by_groups(0, depth, 5, one_group, 0)

    def both_sides(f):
        return jnp.where(inner_side, seam_left[f], seam_right[f])

    unpack([(0, both_sides(0)), (1, both_sides(1)), (2, jnp.where(inner_side, open_left, open_right)), (3, both_sides(3))])

    def open_columns(levels, carry):
        ahead = [shifted([wet_at(h, k) for h in span], ends[3 * depth + k], 1, lane) for k in levels]
        for k, wets_ahead in zip(levels, ahead):
            for h in span:
                i = h * depth + k
                open_y[i] = vy[i] * wet_at(h, k) * wets_ahead[h] * (1.0 / 12.0)
        return carry

    by_groups(0, depth, 5, open_columns, 0)
    get_forcing.wait()
    for h in span:
        theta[h * depth] = theta[h * depth] + forcing[:, h * LANES : (h + 1) * LANES] * wet_at(h, 0)

    def column_shifts(ref, f, k, beyond):
        centre = [ref[at(f, h, k), top:end] for h in span]
        return {s: shifted(centre, ends[beyond * depth + k], s, lane) for s in (-2, -1, 1, 2)}

    def face_shifts(k, steps):
        centre = [open_y[h * depth + k] for h in span]
        return {s: shifted(centre, ends[2 * depth + k], s, lane) for s in steps}

    def got_rows(ref, base, levels, sent_too):
        for copy, sends, receives in row_copies(ref, base, lax.div(levels[0], GROUP)):
            if sent_too:
                guarded(sends, copy.wait_send)
            guarded(receives, copy.wait_recv)

    def forward_down(levels, carry):
        got_rows(first, rows_one, levels, True)
        for k in levels:
            for h in span:
                f, i = at(2, h, k), h * depth + k
                first[f, top - 1 : top] = first[f, top - 1 : top] * wet[i, 0:1]
                first[f, end - 1 : end] = first[f, end - 1 : end] * wet_after[i, 0:1]
        moved = [(face_shifts(k, (-1,)), [column_shifts(first, f, k, f) for f in range(2)]) for k in levels]
        for k, (uy, turned) in zip(levels, moved):
            out = []
            for h in span:
                i = h * depth + k
                found = []
                for f, raw in ((0, theta), (1, salt)):
                    q = [first[at(f, h, k), top + s : end + s] for s in (-2, -1, 0, 1, 2)]
                    c = turned[f]
                    row_here = first[at(2, h, k), top:end] * (7.0 * (q[2] + q[3]) - (q[1] + q[4]))
                    row_back = first[at(2, h, k), top - 1 : end - 1] * (7.0 * (q[1] + q[2]) - (q[0] + q[3]))
                    col_here = open_y[i] * (7.0 * (q[2] + c[1][h]) - (c[-1][h] + c[2][h]))
                    col_back = uy[-1][h] * (7.0 * (c[-1][h] + q[2]) - (c[-2][h] + c[1][h]))
                    value = raw[i] - (row_here - row_back) - (col_here - col_back)
                    found.append(value * inverse[i] + link[i] * carry[h][f])
                theta_mix[i] = found[0]
                salt_mix[i] = found[1]
                out.append(tuple(found))
            carry = tuple(out)
        return carry

    carry = by_groups(0, depth, GROUP, forward_down, ((blank, blank),) * halves)

    def forward_up(steps, carry):
        for n in steps:
            k = depth - 2 - n
            out = []
            for h in span:
                i = h * depth + k
                xt = theta_mix[i] + ratio[i] * carry[h][0]
                xs = salt_mix[i] + ratio[i] * carry[h][1]
                dt, ds = xt - carry[h][0], xs - carry[h][1]
                step_t, step_s, step_w = [
                    second[at(f, h, k), top:end] - second[at(f, h, k + 1), top:end] for f in range(3)
                ]
                closed = -wet_at(h, k) * wet_at(h, k + 1)
                k_fixed[h * (depth - 1) + k] = closed * (step_t * dt + step_s * ds)
                k_zeta[h * (depth - 1) + k] = closed * step_w * (0.2 * dt - 0.15 * ds)
                out.append((xt, xs))
            carry = tuple(out)
        return carry

    by_groups(0, depth - 1, 4, forward_up, carry)

    for copy, sends, receives in edges_two:
        guarded(sends, copy.wait_send)
        guarded(receives, copy.wait_recv)
    unpack([(4 + f, both_sides(4 + f)) for f in range(3)])

    def arms(u, wets):
        v = [wets * x for x in u]
        back, here = 7.0 * v[1], 7.0 * v[2]
        return v[0], back + v[0], back - here, here + v[3], v[3]

    def adjoint(levels, carry):
        got_rows(second, rows_two, levels, True)
        moved = [
            (face_shifts(k, (-2, -1, 1)), [column_shifts(second, f, k, 4 + f) for f in range(3)]) for k in levels
        ]
        for k, (uy, turned) in zip(levels, moved):
            for h in span:
                i = h * depth + k
                wets = wet_at(h, k)
                r = arms([first[at(2, h, k), top + s : end + s] for s in (-2, -1, 0, 1)], wets)
                c = arms([uy[-2][h], uy[-1][h], open_y[i], uy[1][h]], wets)
                weights = [(1.0 + r[2]) + c[2], r[0], r[3], c[0], c[3], r[1], r[4], c[1], c[4]]
                for f in range(3):
                    values = [second[at(f, h, k), top + s : end + s] for s in (0, -2, 1)]
                    values += [turned[f][s][h] for s in (-2, 1)]
                    values += [second[at(f, h, k), top + s : end + s] for s in (-1, 2)]
                    values += [turned[f][s][h] for s in (-1, 2)]
                    terms = [w * m for w, m in zip(weights, values)]
                    if f == 2:
                        for n in range(9):
                            cross[(n * halves + h) * depth + k] = terms[n]
                    else:
                        (theta_adj, salt_adj)[f][i] = signed_sum(terms)
        return carry

    by_groups(0, depth, GROUP, adjoint, 0)
    for h in span:
        top_parts[h] = wet_at(h, 0) * second[at(0, h, 0), top:end]
        top_parts[halves + h] = 1.0 + 0.2 * (wet_at(h, 0) * second[at(2, h, 0), top:end])

    others(lambda i, device: sum_copy(i, device).wait_recv())
    sums[...] = jnp.broadcast_to(jnp.sum(slots[...], axis=0, keepdims=True), sums.shape)
    for copy, sends, _ in rims:
        guarded(sends, copy.wait_send)
    others(lambda i, device: sum_copy(i, device).wait_send())


def finish_kernel(
    sizes,
    cross, theta_adj, salt_adj, k_fixed, k_zeta, basis, top_parts, sums,
    theta_out, salt_out, kappa_out, forcing_out,
    zeta, theta_grad, salt_grad, kappa_grad, forcing_grad, sems,
):
    depth, rows, cols = sizes
    halves = cols // LANES
    top, end = RIM, RIM + rows
    span = range(halves)
    lane = lane_index(rows)
    total = sums[...]
    for step in (8, 4, 2, 1):
        total = total + roll(total, -step)
    m = [jnp.broadcast_to(total[:, 16 * g : 16 * g + 1], (8, LANES)) for g in range(8)]
    m = m[:5] + [2.0 * m[5] - m[1], 2.0 * m[6] - m[0], 2.0 * m[7] - m[1]]
    weights = [jnp.concatenate([w] * ((rows + 2 * RIM) // 8), axis=0) for w in weights_from(m)]
    tiles = halves + 2
    for h in range(tiles):
        b = [basis[k * tiles + h] for k in range(ITERS)]
        zeta[h] = (weights[0] * b[0] + weights[1] * b[1]) + (weights[2] * b[2] + weights[3] * b[3])
    level = [zeta[h, top:end] for h in range(tiles)]
    around = []
    for h in span:
        by_row = {s: zeta[h + 1, top + s : end + s] for s in (-2, -1, 1, 2)}
        by_col = {
            s: jnp.where(lane < LANES - s, roll(level[h + 1], -s), roll(level[h + 2], -s))
            if s > 0
            else jnp.where(lane < -s, roll(level[h], -s), roll(level[h + 1], -s))
            for s in (-2, -1, 1, 2)
        }
        around.append(
            [level[h + 1], by_row[-2], by_row[1], by_col[-2], by_col[1], by_row[-1], by_row[2], by_col[-1], by_col[2]]
        )
    for h in span:
        forcing_grad[:, h * LANES : (h + 1) * LANES] = top_parts[h] + around[h][0] * top_parts[halves + h]
    put_forcing = pltpu.make_async_copy(forcing_grad, forcing_out, sems.at[0])
    put_forcing.start()
    group = 5
    groups = depth // group
    copies = [put_forcing]
    for g in range(groups + (depth % group > 0)):
        for k in range(g * group, min(depth, (g + 1) * group)):
            for h in span:
                i = h * depth + k
                where = slice(h * LANES, (h + 1) * LANES)
                terms = [cross[(n * halves + h) * depth + k] * around[h][n] for n in range(9)]
                change = signed_sum(terms)
                theta_grad[k, :, where] = theta_adj[i] + 0.2 * change
                salt_grad[k, :, where] = salt_adj[i] - 0.15 * change
                if k < depth - 1:
                    j = h * (depth - 1) + k
                    kappa_grad[k, :, where] = k_fixed[j] + k_zeta[j] * around[h][0]
        for src, dst in ((theta_grad, theta_out), (salt_grad, salt_out), (kappa_grad, kappa_out)):
            first, last = g * group, min(src.shape[0], (g + 1) * group)
            if first < last:
                part = pl.ds(first, last - first)
                copy = pltpu.make_async_copy(src.at[part], dst.at[part], sems.at[len(copies)])
                copy.start()
                copies.append(copy)
    for copy in copies:
        copy.wait()


def shards(*args):
    theta = args[0]
    depth, rows, cols = theta.shape
    halves = cols // LANES
    count = lax.axis_size("trow") * lax.axis_size("tcol")
    tall = rows + 2 * RIM
    V = pltpu.VMEM
    DMA = pltpu.SemaphoreType.DMA
    flat = V((halves * depth, rows, LANES), F32)
    ints = V((halves * depth, rows, LANES), jnp.int32)
    upper = V((halves * (depth - 1), rows, LANES), F32)
    tile = V((7, rows, LANES), F32)
    halo = DMA((5 + 4 * (depth // GROUP),))
    scratch = [
        flat, flat, flat, flat, ints, upper, V((rows, cols), F32), flat, flat,
        V((tall, cols + 2 * LANES), F32), V((tall, cols + 2 * LANES), jnp.int32),
        V((halves * depth, rows + RIM, LANES), F32), V((halves * depth, RIM, LANES), F32),
        V((3 * halves * depth, tall, LANES), F32), V((3 * halves * depth, tall, LANES), F32),
        flat, flat, flat, flat, flat, flat,
        tile, tile, tile, V((7 * depth, rows, LANES), F32), V((count, LANES), F32),
        DMA((3 + 8 * halves,)), DMA((16,)), DMA((16,)), halo, halo, DMA((count,)), DMA((count,)),
    ]
    parts = [
        (9 * halves * depth, rows, LANES), (halves * depth, rows, LANES), (halves * depth, rows, LANES),
        (halves * (depth - 1), rows, LANES), (halves * (depth - 1), rows, LANES),
        (ITERS * (halves + 2), tall, LANES), (2 * halves, rows, LANES), (8, LANES),
    ]
    found = pl.pallas_call(
        functools.partial(solve_kernel, (depth, rows, cols)),
        out_shape=[jax.ShapeDtypeStruct(o, F32) for o in parts],
        in_specs=[pl.BlockSpec(memory_space=pltpu.HBM)] * len(args),
        out_specs=[pl.BlockSpec(memory_space=V)] * len(parts),
        scratch_shapes=scratch,
        compiler_params=pltpu.CompilerParams(
            collective_id=0, has_side_effects=True, vmem_limit_bytes=40 * 1024 * 1024
        ),
    )(*[pltpu.with_memory_space_constraint(a, pltpu.HBM) for a in args])
    outs = [(depth, rows, cols), (depth, rows, cols), (depth - 1, rows, cols), (rows, cols)]
    return tuple(
        pl.pallas_call(
            functools.partial(finish_kernel, (depth, rows, cols)),
            out_shape=[jax.ShapeDtypeStruct(o, F32) for o in outs],
            in_specs=[pl.BlockSpec(memory_space=V)] * len(parts),
            out_specs=[pl.BlockSpec(memory_space=pltpu.HBM)] * len(outs),
            scratch_shapes=[V((halves + 2, tall, LANES), F32)] + [V(o, F32) for o in outs] + [DMA((1 + 3 * (depth // 5 + 1),))],
            compiler_params=pltpu.CompilerParams(vmem_limit_bytes=16 * 1024 * 1024),
        )(*found)
    )


def solution(mesh):
    cube, plane = P(None, "trow", "tcol"), P("trow", "tcol")
    in_specs = (cube,) * 6 + (plane,) * 2 + (cube,) * 2 + (plane,)
    out_specs = (cube,) * 3 + (plane,)
    return jax.shard_map(shards, mesh=mesh, in_specs=in_specs, out_specs=out_specs, check_vma=False)
```

```python
import functools
import jax
import jax.numpy as jnp
from jax import lax
from jax.experimental import pallas as pl
from jax.experimental.pallas import tpu as pltpu
from jax.sharding import PartitionSpec as P

ITERS = 4
LANES = 128
RIM = 8
LOW, HIGH = 0.2, 9.2
CENTRE, RADIUS = (HIGH + LOW) / 2, (HIGH - LOW) / 2
MESH = pl.DeviceIdType.MESH
F32 = jnp.float32


def put(out, k, value):
    out[k] = value if out[k] is None else out[k] + value


def times_operator(poly):
    out = [None] * (len(poly) + 1)
    for k, c in enumerate(poly):
        put(out, k, CENTRE * c)
        if k == 0:
            put(out, 1, RADIUS * c)
        else:
            half = (0.5 * RADIUS) * c
            put(out, k + 1, half)
            put(out, k - 1, half)
    return out


def inner(p, q, table):
    total = None
    for i, a in enumerate(p):
        part = None
        for j, b in enumerate(q):
            term = b * table[i][j]
            part = term if part is None else part + term
        part = a * part
        total = part if total is None else total + part
    return total


def add_scaled(p, scale, q):
    out = []
    for k in range(max(len(p), len(q))):
        if k >= len(p):
            out.append(scale * q[k])
        elif k >= len(q):
            out.append(p[k])
        else:
            out.append(p[k] + scale * q[k])
    return out


def weights_from(moments):
    table = [
        [
            moments[j] if i == 0 else moments[i] if j == 0 else 0.5 * (moments[i + j] + moments[abs(i - j)])
            for j in range(ITERS + 1)
        ]
        for i in range(ITERS)
    ]
    residual = [jnp.ones_like(moments[0])]
    direction = residual
    result = []
    norm_now = moments[0]
    for iteration in range(ITERS):
        image = times_operator(direction)
        step = norm_now / inner(direction, image, table)
        result = add_scaled(result, step, direction)
        if iteration + 1 < ITERS:
            residual = add_scaled(residual, -step, image)
            norm_next = inner(residual, residual, table)
            direction = add_scaled(residual, norm_next / norm_now, direction)
            norm_now = norm_next
    return result


def lane_index(rows):
    return lax.broadcasted_iota(jnp.int32, (rows, LANES), 1)


def roll(x, amount):
    return pltpu.roll(x, amount % LANES if isinstance(amount, int) else amount & (LANES - 1), 1)


def shifted(parts, ends, by, lane):
    if by > 0:
        joined = [jnp.where(lane < by, nearby, p) for p, nearby in zip(parts, parts[1:] + [ends])]
    else:
        joined = [jnp.where(lane >= LANES + by, nearby, p) for p, nearby in zip(parts, [ends] + parts[:-1])]
    return [roll(p, -by) for p in joined]


GROUP = 5


def by_groups(start, stop, group, body, carry):
    count = (stop - start) // group
    carry = lax.fori_loop(0, count, lambda i, c: body([start + i * group + u for u in range(group)], c), carry)
    rest = list(range(start + count * group, stop))
    return body(rest, carry) if rest else carry


def signed_sum(terms):
    return terms[0] + (((terms[1] + terms[2]) - (terms[5] + terms[6])) + ((terms[3] + terms[4]) - (terms[7] + terms[8])))


def guarded(condition, action):
    @pl.when(condition)
    def _():
        action()


def solve_kernel(
    sizes,
    theta_in, salt_in, vx_in, vy_in, land_in, kappa_in, forcing_in, bottom_in, theta_cot_in, salt_cot_in, surface_in,
    theta_grad, salt_grad, kappa_grad, forcing_grad,
    theta, salt, vx, vy, land, kappa, forcing, theta_cot, salt_cot,
    surface, bottom, wet, wet_after, first, second, open_y, inverse, link, ratio, theta_mix, salt_mix,
    seam_own, seam_left, seam_right, ends, slots, cross, k_fixed, k_zeta, zeta,
    local_sem, rim_send, rim_recv, halo_send, halo_recv, sum_send, sum_recv,
):
    depth, rows, cols = sizes
    halves = cols // LANES
    top, end = RIM, RIM + rows
    mesh_rows, mesh_cols = lax.axis_size("trow"), lax.axis_size("tcol")
    count = mesh_rows * mesh_cols
    row, col = lax.axis_index("trow"), lax.axis_index("tcol")
    has_before, has_after = row > 0, row < mesh_rows - 1
    has_left, has_right = col > 0, col < mesh_cols - 1
    lane = lane_index(rows)
    spot = ((lane + 2) & 3) - 2
    blank = jnp.zeros((rows, LANES), F32)
    span = range(halves)

    chunks = depth // GROUP
    per_chunk = 3 * halves * GROUP

    def at(f, h, k):
        return (k * 3 + f) * halves + h

    surface[...] = jnp.zeros_like(surface)
    bottom[...] = jnp.zeros_like(bottom)
    seam_left[...] = jnp.zeros_like(seam_left)
    seam_right[...] = jnp.zeros_like(seam_right)

    barrier = pltpu.get_barrier_semaphore()

    def others(action):
        for dc in range(1, mesh_cols):
            action(dc, (row, lax.rem(col + dc, mesh_cols)))

        def one_row(dr, carry):
            there = lax.rem(row + dr, mesh_rows)
            for dc in range(mesh_cols):
                action(dr * mesh_cols + dc, (there, lax.rem(col + dc, mesh_cols)))
            return carry

        lax.fori_loop(1, mesh_rows, one_row, 0)

    others(lambda i, device: pl.semaphore_signal(barrier, inc=1, device_id=device, device_id_type=MESH))

    started = []

    def fetch(src, dst):
        copy = pltpu.make_async_copy(src, dst, local_sem.at[len(started)])
        copy.start()
        started.append(copy)
        return copy

    middle = pl.ds(LANES, cols)
    get_surface = fetch(surface_in, surface.at[pl.ds(RIM, rows), middle])
    get_bottom = fetch(bottom_in, bottom.at[pl.ds(RIM, rows), middle])

    def fetch_halves(src, dst):
        return [
            fetch(src.at[:, :, pl.ds(h * LANES, LANES)], dst.at[pl.ds(h * src.shape[0], src.shape[0])]) for h in span
        ]

    get_land = fetch_halves(land_in, land)
    get_theta = fetch_halves(theta_in, theta)
    get_salt = fetch_halves(salt_in, salt)
    get_vx = fetch_halves(vx_in, vx)
    get_vy = fetch_halves(vy_in, vy)
    get_forcing = fetch(forcing_in, forcing)
    get_kappa = fetch_halves(kappa_in, kappa)
    get_theta_cot = fetch_halves(theta_cot_in, theta_cot)
    get_salt_cot = fetch_halves(salt_cot_in, salt_cot)

    def arrived(copies):
        for copy in copies:
            copy.wait()

    arrived([get_bottom] + get_land)

    def wet_levels(levels, carry):
        for k in levels:
            for h in span:
                depth_here = bottom[top:end, LANES * (h + 1) : LANES * (h + 2)]
                wet[h * depth + k, 0:rows] = jnp.where(k < depth_here, land[h * depth + k].astype(F32), 0.0)
                wet[h * depth + k, rows : rows + RIM] = jnp.ones((RIM, LANES), F32)
        return carry

    by_groups(0, depth, 5, wet_levels, 0)

    def wet_at(h, k):
        return wet[h * depth + k, 0:rows]

    arrived(get_theta + get_salt + get_vx + get_vy)

    def pack(k, parts, packed):
        both = jnp.where(lane < LANES // 2, parts[0], parts[-1])
        here = ((lane + 2 - 4 * k) & (LANES - 1)) < 4
        return jnp.where(here, roll(both, 4 * k), packed)

    def prepare(levels, packs):
        for k in levels:
            wets = [wet_at(h, k) for h in span]
            qt, qs, uy = [], [], []
            for h in span:
                i = h * depth + k
                qt.append(theta[i] * wets[h])
                qs.append(salt[i] * wets[h])
                uy.append(vy[i])
                first[at(0, h, k), top:end] = qt[h]
                first[at(1, h, k), top:end] = qs[h]
                first[at(2, h, k), top:end] = vx[i] * wets[h] * wet[i, 1 : rows + 1] * (1.0 / 12.0)
            packs = tuple(pack(k, parts, packed) for parts, packed in zip((qt, qs, uy, wets), packs))
        return packs

    for f, packed in enumerate(by_groups(0, depth, 5, prepare, (blank,) * 4)):
        seam_own[f] = packed

    pl.semaphore_wait(barrier, count - 1)

    rims = []
    for dr in (-1, 0, 1):
        for dc in (-1, 0, 1):
            if dr == 0 and dc == 0:
                continue
            targets = [has_before] * (dr < 0) + [has_after] * (dr > 0) + [has_left] * (dc < 0) + [has_right] * (dc > 0)
            sources = [has_after] * (dr < 0) + [has_before] * (dr > 0) + [has_right] * (dc < 0) + [has_left] * (dc > 0)
            src_rows = pl.ds(0, RIM) if dr < 0 else pl.ds(rows - RIM, RIM) if dr > 0 else pl.ds(0, rows)
            src_cols = pl.ds(0, LANES) if dc < 0 else pl.ds(cols - LANES, LANES) if dc > 0 else pl.ds(0, cols)
            dst_rows = pl.ds(end, RIM) if dr < 0 else pl.ds(0, RIM) if dr > 0 else pl.ds(top, rows)
            dst_cols = pl.ds(LANES + cols, LANES) if dc < 0 else pl.ds(0, LANES) if dc > 0 else middle
            for src, dst in ((surface_in, surface), (bottom_in, bottom)):
                i = len(rims)
                copy = pltpu.make_async_remote_copy(
                    src_ref=src.at[src_rows, src_cols],
                    dst_ref=dst.at[dst_rows, dst_cols],
                    send_sem=rim_send.at[i],
                    recv_sem=rim_recv.at[i],
                    device_id=(row + dr, col + dc),
                    device_id_type=MESH,
                )
                rims.append((copy, functools.reduce(jnp.logical_and, targets), functools.reduce(jnp.logical_and, sources)))
    for copy, sends, _ in rims:
        guarded(sends, copy.start)

    def remote(src, dst, i, device):
        return pltpu.make_async_remote_copy(
            src_ref=src, dst_ref=dst, send_sem=halo_send.at[i], recv_sem=halo_recv.at[i], device_id=device, device_id_type=MESH
        )

    after, before = (row + 1, col), (row - 1, col)
    right, left = (row, col + 1), (row, col - 1)
    def row_copies(ref, base, g):
        part = pl.ds(g * per_chunk, per_chunk)
        return [
            (remote(ref.at[part, pl.ds(end - 2, 2)], ref.at[part, pl.ds(top - 2, 2)], base + g, after), has_after, has_before),
            (remote(ref.at[part, pl.ds(top, 2)], ref.at[part, pl.ds(end, 2)], base + chunks + g, before), has_before, has_after),
        ]

    def edge_copies(first_field, fields, base):
        part = pl.ds(first_field, fields)
        return [
            (remote(seam_own.at[part], seam_left.at[part], base, right), has_right, has_left),
            (remote(seam_own.at[part], seam_right.at[part], base + 1, left), has_left, has_right),
        ]

    def send_rows(ref, base):
        for g in range(chunks):
            for copy, sends, _ in row_copies(ref, base, g):
                guarded(sends, copy.start)

    edges_one, edges_two = edge_copies(0, 4, 0), edge_copies(4, 3, 2)
    wet_copy = remote(wet.at[:, pl.ds(0, 1)], wet_after.at[:, pl.ds(0, 1)], 4, before)
    rows_one, rows_two = 5, 5 + 2 * chunks
    for copy, sends, _ in edges_one + [(wet_copy, has_before, has_after)]:
        guarded(sends, copy.start)
    send_rows(first, rows_one)

    def clear(missing, ref, start):
        @pl.when(missing)
        def _():
            ref[:, start : start + 2] = jnp.zeros((ref.shape[0], 2, LANES), F32)

    for ref in (first, second):
        clear(jnp.logical_not(has_before), ref, top - 2)
        clear(jnp.logical_not(has_after), ref, end)
    clear(jnp.logical_not(has_after), wet_after, 0)

    arrived(get_kappa + get_theta_cot + get_salt_cot)

    def down_level(k, last, carry):
        out = []
        for h in span:
            num, den, couple_before, yt, ys, yw = carry[h]
            i = h * depth + k
            wet_here = wet_at(h, k)
            if last:
                den_next = num_next = num
                couple = couple_before
            else:
                couple = kappa[h * (depth - 1) + k] * wet_here * wet_at(h, k + 1)
                den_next = num + couple * den
                num_next = den_next + couple * num
            inv = den * (1.0 / den_next)
            lower = couple_before * inv
            inverse[i] = inv
            link[i] = lower
            if not last:
                ratio[i] = couple * inv
            yt = theta_cot[i] * inv + lower * yt
            ys = salt_cot[i] * inv + lower * ys
            yw = wet_here * inv + lower * yw
            second[at(0, h, k), top:end] = yt
            second[at(1, h, k), top:end] = ys
            second[at(2, h, k), top:end] = yw
            out.append((num_next, den_next, couple, yt, ys, yw))
        return tuple(out)

    def down(levels, carry):
        for k in levels:
            carry = down_level(k, False, carry)
        return carry

    one = jnp.ones((rows, LANES), F32)
    carry = by_groups(0, depth - 1, 4, down, ((one, one, blank, blank, blank, blank),) * halves)
    carry = down_level(depth - 1, True, carry)

    def up(steps, values):
        for n in steps:
            k = depth - 2 - n
            new = []
            for f in range(3):
                parts = []
                for h in span:
                    x = second[at(f, h, k), top:end] + ratio[h * depth + k] * values[f][h]
                    second[at(f, h, k), top:end] = x
                    parts.append(x)
                new.append(tuple(parts))
            values = tuple(new)
        return values

    by_groups(0, depth - 1, 4, up, tuple(tuple(carry[h][3 + f] for h in span) for f in range(3)))

    def pack_second(levels, packs):
        for k in levels:
            packs = tuple(pack(k, [second[at(f, h, k), top:end] for h in span], packs[f]) for f in range(3))
        return packs

    for f, packed in enumerate(by_groups(0, depth, 5, pack_second, (blank,) * 3)):
        seam_own[4 + f] = packed
    for copy, sends, _ in edges_two:
        guarded(sends, copy.start)
    send_rows(second, rows_two)

    get_surface.wait()
    for copy, _, receives in rims:
        guarded(receives, copy.wait_recv)
    wide = (rows + 2 * RIM, cols + 2 * LANES)
    row_at = lax.broadcasted_iota(jnp.int32, wide, 0) - RIM + row * rows
    col_at = lax.broadcasted_iota(jnp.int32, wide, 1) - LANES + col * cols
    inside = ((row_at >= 0) & (row_at < rows * mesh_rows)) & ((col_at >= 0) & (col_at < cols * mesh_cols))
    scaled = (bottom[...].astype(F32) * (1.0 / depth) + (4.2 - CENTRE)) * (1.0 / RADIUS)
    basis = [surface[...]]
    for k in range(ITERS):
        field = basis[-1]
        beside = (pltpu.roll(field, 1, 0) + pltpu.roll(field, wide[0] - 1, 0)) + (
            pltpu.roll(field, 1, 1) + pltpu.roll(field, wide[1] - 1, 1)
        )
        image = scaled * field - beside * (1.0 / RADIUS)
        if k > 0:
            image = 2.0 * image - basis[-2]
        basis.append(jnp.where(inside, image, 0.0))

    def own_product(a, b):
        product = basis[a][top:end, LANES : LANES + cols] * basis[b][top:end, LANES : LANES + cols]
        tiles = [product[i : i + 8, j : j + LANES] for i in range(0, rows, 8) for j in range(0, cols, LANES)]
        return functools.reduce(jnp.add, tiles)

    partial = [own_product(a, b) for a, b in ((0, 0), (0, 1), (0, 2), (0, 3), (0, 4), (2, 3), (3, 3), (3, 4))]
    small_lane = lane_index(8)
    width = LANES // 2
    while len(partial) > 1:
        half = len(partial) // 2
        take_first = (small_lane & (2 * width - 1)) < width
        partial = [
            jnp.where(take_first, a + roll(a, -width), b + roll(b, width)) for a, b in zip(partial[:half], partial[half:])
        ]
        width //= 2
    slots[0:1] = jnp.sum(partial[0], axis=0, keepdims=True)

    def sum_copy(i, device):
        return pltpu.make_async_remote_copy(
            src_ref=slots.at[pl.ds(0, 1)],
            dst_ref=slots.at[pl.ds(i, 1)],
            send_sem=sum_send.at[i],
            recv_sem=sum_recv.at[i],
            device_id=device,
            device_id_type=MESH,
        )

    others(lambda i, device: sum_copy(i, device).start())
    for k in range(ITERS):
        for h in range(halves + 2):
            zeta[k * (halves + 2) + h] = basis[k][:, h * LANES : (h + 1) * LANES]

    for copy, sends, receives in edges_one + [(wet_copy, has_before, has_after)]:
        guarded(sends, copy.wait_send)
        guarded(receives, copy.wait_recv)

    def open_across(uy, near):
        return uy * near * roll(near, -1) * (1.0 / 12.0)

    inner_side = spot < 0
    open_left = open_across(seam_left[2], jnp.where(inner_side, seam_left[3], seam_own[3]))
    open_right = open_across(seam_right[2], seam_right[3])

    def unpack(fields):
        def one_group(levels, carry):
            for k in levels:
                for f, packed in fields:
                    ends[f * depth + k] = roll(packed, LANES - 4 * k)
            return carry

        by_groups(0, depth, 5, one_group, 0)

    def both_sides(f):
        return jnp.where(inner_side, seam_left[f], seam_right[f])

    unpack([(0, both_sides(0)), (1, both_sides(1)), (2, jnp.where(inner_side, open_left, open_right)), (3, both_sides(3))])

    def open_columns(levels, carry):
        ahead = [shifted([wet_at(h, k) for h in span], ends[3 * depth + k], 1, lane) for k in levels]
        for k, wets_ahead in zip(levels, ahead):
            for h in span:
                i = h * depth + k
                open_y[i] = vy[i] * wet_at(h, k) * wets_ahead[h] * (1.0 / 12.0)
        return carry

    by_groups(0, depth, 5, open_columns, 0)
    get_forcing.wait()
    for h in span:
        theta[h * depth] = theta[h * depth] + forcing[:, h * LANES : (h + 1) * LANES] * wet_at(h, 0)

    def column_shifts(ref, f, k, beyond):
        centre = [ref[at(f, h, k), top:end] for h in span]
        return {s: shifted(centre, ends[beyond * depth + k], s, lane) for s in (-2, -1, 1, 2)}

    def face_shifts(k, steps):
        centre = [open_y[h * depth + k] for h in span]
        return {s: shifted(centre, ends[2 * depth + k], s, lane) for s in steps}

    def got_rows(ref, base, levels, sent_too):
        for copy, sends, receives in row_copies(ref, base, lax.div(levels[0], GROUP)):
            if sent_too:
                guarded(sends, copy.wait_send)
            guarded(receives, copy.wait_recv)

    def forward_down(levels, carry):
        got_rows(first, rows_one, levels, True)
        for k in levels:
            for h in span:
                f, i = at(2, h, k), h * depth + k
                first[f, top - 1 : top] = first[f, top - 1 : top] * wet[i, 0:1]
                first[f, end - 1 : end] = first[f, end - 1 : end] * wet_after[i, 0:1]
        moved = [(face_shifts(k, (-1,)), [column_shifts(first, f, k, f) for f in range(2)]) for k in levels]
        for k, (uy, turned) in zip(levels, moved):
            out = []
            for h in span:
                i = h * depth + k
                found = []
                for f, raw in ((0, theta), (1, salt)):
                    q = [first[at(f, h, k), top + s : end + s] for s in (-2, -1, 0, 1, 2)]
                    c = turned[f]
                    row_here = first[at(2, h, k), top:end] * (7.0 * (q[2] + q[3]) - (q[1] + q[4]))
                    row_back = first[at(2, h, k), top - 1 : end - 1] * (7.0 * (q[1] + q[2]) - (q[0] + q[3]))
                    col_here = open_y[i] * (7.0 * (q[2] + c[1][h]) - (c[-1][h] + c[2][h]))
                    col_back = uy[-1][h] * (7.0 * (c[-1][h] + q[2]) - (c[-2][h] + c[1][h]))
                    value = raw[i] - (row_here - row_back) - (col_here - col_back)
                    found.append(value * inverse[i] + link[i] * carry[h][f])
                theta_mix[i] = found[0]
                salt_mix[i] = found[1]
                out.append(tuple(found))
            carry = tuple(out)
        return carry

    carry = by_groups(0, depth, GROUP, forward_down, ((blank, blank),) * halves)

    def forward_up(steps, carry):
        for n in steps:
            k = depth - 2 - n
            out = []
            for h in span:
                i = h * depth + k
                xt = theta_mix[i] + ratio[i] * carry[h][0]
                xs = salt_mix[i] + ratio[i] * carry[h][1]
                dt, ds = xt - carry[h][0], xs - carry[h][1]
                step_t, step_s, step_w = [
                    second[at(f, h, k), top:end] - second[at(f, h, k + 1), top:end] for f in range(3)
                ]
                closed = -wet_at(h, k) * wet_at(h, k + 1)
                k_fixed[h * (depth - 1) + k] = closed * (step_t * dt + step_s * ds)
                k_zeta[h * (depth - 1) + k] = closed * step_w * (0.2 * dt - 0.15 * ds)
                out.append((xt, xs))
            carry = tuple(out)
        return carry

    by_groups(0, depth - 1, 4, forward_up, carry)

    def arms(u, wets):
        v = [wets * x for x in u]
        back, here = 7.0 * v[1], 7.0 * v[2]
        return v[0], back + v[0], back - here, here + v[3], v[3]

    def coefficients(levels, carry):
        moved = [face_shifts(k, (-2, -1, 1)) for k in levels]
        for k, uy in zip(levels, moved):
            for h in span:
                i = h * depth + k
                wets = wet_at(h, k)
                r = arms([first[at(2, h, k), top + s : end + s] for s in (-2, -1, 0, 1)], wets)
                c = arms([uy[-2][h], uy[-1][h], open_y[i], uy[1][h]], wets)
                for n, w in enumerate([(1.0 + r[2]) + c[2], r[0], r[3], c[0], c[3], r[1], r[4], c[1], c[4]]):
                    cross[9 * i + n] = w
        return carry

    by_groups(0, depth, GROUP, coefficients, 0)

    others(lambda i, device: sum_copy(i, device).wait_recv())
    total = jnp.broadcast_to(jnp.sum(slots[...], axis=0, keepdims=True), (8, LANES))
    for step in (8, 4, 2, 1):
        total = total + roll(total, -step)
    m = [jnp.broadcast_to(total[:, 16 * g : 16 * g + 1], (8, LANES)) for g in range(8)]
    m = m[:5] + [2.0 * m[5] - m[1], 2.0 * m[6] - m[0], 2.0 * m[7] - m[1]]
    weights = [jnp.concatenate([w] * (wide[0] // 8), axis=0) for w in weights_from(m)]
    tiles = halves + 2
    for h in range(tiles):
        b = [zeta[k * tiles + h] for k in range(ITERS)]
        zeta[h] = (weights[0] * b[0] + weights[1] * b[1]) + (weights[2] * b[2] + weights[3] * b[3])

    for copy, sends, receives in edges_two:
        guarded(sends, copy.wait_send)
        guarded(receives, copy.wait_recv)
    beyond = jnp.where(lane >= LANES // 2, zeta[0, top:end], zeta[tiles - 1, top:end])
    far_t, far_s, far_w = both_sides(4), both_sides(5), both_sides(6)

    def unpack_mu(levels, carry):
        for k in levels:
            turned = [roll(p, LANES - 4 * k) for p in (far_t, far_s, far_w)]
            lifted = turned[2] * beyond
            ends[4 * depth + k] = turned[0] + 0.2 * lifted
            ends[5 * depth + k] = turned[1] - 0.15 * lifted
        return carry

    by_groups(0, depth, 5, unpack_mu, 0)

    def finish(levels, carry):
        got_rows(second, rows_two, levels, True)
        for k in levels:
            for h in span:
                area = pl.ds(top - 2, rows + 8)
                lifted = second[at(2, h, k), area] * zeta[h + 1, area]
                second[at(0, h, k), area] = second[at(0, h, k), area] + 0.2 * lifted
                second[at(1, h, k), area] = second[at(1, h, k), area] - 0.15 * lifted
        moved = [[column_shifts(second, f, k, 4 + f) for f in range(2)] for k in levels]
        for k, turned in zip(levels, moved):
            for h in span:
                i = h * depth + k
                where = slice(h * LANES, (h + 1) * LANES)
                for f, out in ((0, theta_grad), (1, salt_grad)):
                    values = [second[at(f, h, k), top + s : end + s] for s in (0, -2, 1)]
                    values += [turned[f][s][h] for s in (-2, 1)]
                    values += [second[at(f, h, k), top + s : end + s] for s in (-1, 2)]
                    values += [turned[f][s][h] for s in (-1, 2)]
                    out[k, :, where] = signed_sum([cross[9 * i + n] * v for n, v in enumerate(values)])
        return carry

    by_groups(0, depth, GROUP, finish, 0)

    def finish_kappa(levels, carry):
        for k in levels:
            for h in span:
                j = h * (depth - 1) + k
                kappa_grad[k, :, h * LANES : (h + 1) * LANES] = k_fixed[j] + k_zeta[j] * zeta[h + 1, top:end]
        return carry

    by_groups(0, depth - 1, 4, finish_kappa, 0)
    for h in span:
        forcing_grad[:, h * LANES : (h + 1) * LANES] = zeta[h + 1, top:end] + wet_at(h, 0) * second[at(0, h, 0), top:end]

    for copy, sends, _ in rims:
        guarded(sends, copy.wait_send)
    others(lambda i, device: sum_copy(i, device).wait_send())


def write_kernel(*refs):
    count = (len(refs) - 1) // 2
    sems = refs[-1]
    copies = [pltpu.make_async_copy(refs[i], refs[count + i], sems.at[i]) for i in range(count)]
    for copy in copies:
        copy.start()
    for copy in copies:
        copy.wait()


def shards(*args):
    theta = args[0]
    depth, rows, cols = theta.shape
    halves = cols // LANES
    count = lax.axis_size("trow") * lax.axis_size("tcol")
    tall = rows + 2 * RIM
    V = pltpu.VMEM
    DMA = pltpu.SemaphoreType.DMA
    flat = V((halves * depth, rows, LANES), F32)
    ints = V((halves * depth, rows, LANES), jnp.int32)
    upper = V((halves * (depth - 1), rows, LANES), F32)
    tile = V((7, rows, LANES), F32)
    halo = DMA((5 + 4 * (depth // GROUP),))
    scratch = [
        flat, flat, flat, flat, ints, upper, V((rows, cols), F32), flat, flat,
        V((tall, cols + 2 * LANES), F32), V((tall, cols + 2 * LANES), jnp.int32),
        V((halves * depth, rows + RIM, LANES), F32), V((halves * depth, RIM, LANES), F32),
        V((3 * halves * depth, tall, LANES), F32), V((3 * halves * depth, tall, LANES), F32),
        flat, flat, flat, flat, flat, flat,
        tile, tile, tile, V((7 * depth, rows, LANES), F32), V((count, LANES), F32),
        V((9 * halves * depth, rows, LANES), F32), upper, upper, V((ITERS * (halves + 2), tall, LANES), F32),
        DMA((3 + 8 * halves,)), DMA((16,)), DMA((16,)), halo, halo, DMA((count,)), DMA((count,)),
    ]
    outs = [(depth, rows, cols), (depth, rows, cols), (depth - 1, rows, cols), (rows, cols)]
    shapes = [jax.ShapeDtypeStruct(o, F32) for o in outs]
    found = pl.pallas_call(
        functools.partial(solve_kernel, (depth, rows, cols)),
        out_shape=shapes,
        in_specs=[pl.BlockSpec(memory_space=pltpu.HBM)] * len(args),
        out_specs=[pl.BlockSpec(memory_space=V)] * len(outs),
        scratch_shapes=scratch,
        compiler_params=pltpu.CompilerParams(
            collective_id=0, has_side_effects=True, vmem_limit_bytes=40 * 1024 * 1024
        ),
    )(*[pltpu.with_memory_space_constraint(a, pltpu.HBM) for a in args])
    return tuple(
        pl.pallas_call(
            write_kernel,
            out_shape=shapes,
            in_specs=[pl.BlockSpec(memory_space=V)] * len(outs),
            out_specs=[pl.BlockSpec(memory_space=pltpu.HBM)] * len(outs),
            scratch_shapes=[DMA((len(outs),))],
            compiler_params=pltpu.CompilerParams(vmem_limit_bytes=1024 * 1024),
        )(*found)
    )


def solution(mesh):
    cube, plane = P(None, "trow", "tcol"), P("trow", "tcol")
    in_specs = (cube,) * 6 + (plane,) * 2 + (cube,) * 2 + (plane,)
    out_specs = (cube,) * 3 + (plane,)
    return jax.shard_map(shards, mesh=mesh, in_specs=in_specs, out_specs=out_specs, check_vma=False)
```

```python
import functools
import jax
import jax.numpy as jnp
from jax import lax
from jax.experimental import pallas as pl
from jax.experimental.pallas import tpu as pltpu
from jax.sharding import PartitionSpec as P

ITERS = 4
LANES = 128
RIM = 8
LOW, HIGH = 0.2, 9.2
CENTRE, RADIUS = (HIGH + LOW) / 2, (HIGH - LOW) / 2
MESH = pl.DeviceIdType.MESH
F32 = jnp.float32


def put(out, k, value):
    out[k] = value if out[k] is None else out[k] + value


def times_operator(poly):
    out = [None] * (len(poly) + 1)
    for k, c in enumerate(poly):
        put(out, k, CENTRE * c)
        if k == 0:
            put(out, 1, RADIUS * c)
        else:
            half = (0.5 * RADIUS) * c
            put(out, k + 1, half)
            put(out, k - 1, half)
    return out


def inner(p, q, table):
    total = None
    for i, a in enumerate(p):
        part = None
        for j, b in enumerate(q):
            term = b * table[i][j]
            part = term if part is None else part + term
        part = a * part
        total = part if total is None else total + part
    return total


def add_scaled(p, scale, q):
    out = []
    for k in range(max(len(p), len(q))):
        if k >= len(p):
            out.append(scale * q[k])
        elif k >= len(q):
            out.append(p[k])
        else:
            out.append(p[k] + scale * q[k])
    return out


def weights_from(moments):
    table = [
        [
            moments[j] if i == 0 else moments[i] if j == 0 else 0.5 * (moments[i + j] + moments[abs(i - j)])
            for j in range(ITERS + 1)
        ]
        for i in range(ITERS)
    ]
    residual = [jnp.ones_like(moments[0])]
    direction = residual
    result = []
    norm_now = moments[0]
    for iteration in range(ITERS):
        image = times_operator(direction)
        step = norm_now / inner(direction, image, table)
        result = add_scaled(result, step, direction)
        if iteration + 1 < ITERS:
            residual = add_scaled(residual, -step, image)
            norm_next = inner(residual, residual, table)
            direction = add_scaled(residual, norm_next / norm_now, direction)
            norm_now = norm_next
    return result


def lane_index(rows):
    return lax.broadcasted_iota(jnp.int32, (rows, LANES), 1)


def roll(x, amount):
    return pltpu.roll(x, amount % LANES if isinstance(amount, int) else amount & (LANES - 1), 1)


def shifted(parts, ends, by, lane):
    if by > 0:
        joined = [jnp.where(lane < by, nearby, p) for p, nearby in zip(parts, parts[1:] + [ends])]
    else:
        joined = [jnp.where(lane >= LANES + by, nearby, p) for p, nearby in zip(parts, [ends] + parts[:-1])]
    return [roll(p, -by) for p in joined]


GROUP = 5


def by_groups(start, stop, group, body, carry):
    count = (stop - start) // group
    carry = lax.fori_loop(0, count, lambda i, c: body([start + i * group + u for u in range(group)], c), carry)
    rest = list(range(start + count * group, stop))
    return body(rest, carry) if rest else carry


def signed_sum(terms):
    return terms[0] + (((terms[1] + terms[2]) - (terms[5] + terms[6])) + ((terms[3] + terms[4]) - (terms[7] + terms[8])))


def guarded(condition, action):
    @pl.when(condition)
    def _():
        action()


def solve_kernel(
    sizes,
    theta_in, salt_in, vx_in, vy_in, land_in, kappa_in, forcing_in, bottom_in, theta_cot_in, salt_cot_in, surface_in,
    theta_grad, salt_grad, kappa_grad, forcing_grad,
    theta, salt, vx, vy, land, kappa, forcing, theta_cot, salt_cot,
    surface, bottom, wet, wet_after, first, second, open_y, inverse, link, ratio, theta_mix, salt_mix,
    seam_own, seam_left, seam_right, ends, slots, cross, k_fixed, k_zeta, zeta,
    local_sem, rim_send, rim_recv, halo_send, halo_recv, sum_send, sum_recv,
):
    depth, rows, cols = sizes
    halves = cols // LANES
    top, end = RIM, RIM + rows
    mesh_rows, mesh_cols = lax.axis_size("trow"), lax.axis_size("tcol")
    count = mesh_rows * mesh_cols
    row, col = lax.axis_index("trow"), lax.axis_index("tcol")
    has_before, has_after = row > 0, row < mesh_rows - 1
    has_left, has_right = col > 0, col < mesh_cols - 1
    lane = lane_index(rows)
    spot = ((lane + 2) & 3) - 2
    blank = jnp.zeros((rows, LANES), F32)
    span = range(halves)

    chunks = depth // GROUP
    per_chunk = 3 * halves * GROUP

    def at(f, h, k):
        return (k * 3 + f) * halves + h

    surface[...] = jnp.zeros_like(surface)
    bottom[...] = jnp.zeros_like(bottom)
    seam_left[...] = jnp.zeros_like(seam_left)
    seam_right[...] = jnp.zeros_like(seam_right)

    barrier = pltpu.get_barrier_semaphore()

    def others(action):
        for dc in range(1, mesh_cols):
            action(dc, (row, lax.rem(col + dc, mesh_cols)))

        def one_row(dr, carry):
            there = lax.rem(row + dr, mesh_rows)
            for dc in range(mesh_cols):
                action(dr * mesh_cols + dc, (there, lax.rem(col + dc, mesh_cols)))
            return carry

        lax.fori_loop(1, mesh_rows, one_row, 0)

    others(lambda i, device: pl.semaphore_signal(barrier, inc=1, device_id=device, device_id_type=MESH))

    started = []

    def fetch(src, dst):
        copy = pltpu.make_async_copy(src, dst, local_sem.at[len(started)])
        copy.start()
        started.append(copy)
        return copy

    middle = pl.ds(LANES, cols)
    get_surface = fetch(surface_in, surface.at[pl.ds(RIM, rows), middle])
    get_bottom = fetch(bottom_in, bottom.at[pl.ds(RIM, rows), middle])

    def fetch_halves(src, dst):
        return [
            fetch(src.at[:, :, pl.ds(h * LANES, LANES)], dst.at[pl.ds(h * src.shape[0], src.shape[0])]) for h in span
        ]

    get_land = fetch_halves(land_in, land)
    get_theta = fetch_halves(theta_in, theta)
    get_salt = fetch_halves(salt_in, salt)
    get_vx = fetch_halves(vx_in, vx)
    get_vy = fetch_halves(vy_in, vy)
    get_forcing = fetch(forcing_in, forcing)
    get_kappa = fetch_halves(kappa_in, kappa)
    get_theta_cot = fetch_halves(theta_cot_in, theta_cot)
    get_salt_cot = fetch_halves(salt_cot_in, salt_cot)

    def arrived(copies):
        for copy in copies:
            copy.wait()

    arrived([get_bottom] + get_land)

    def wet_levels(levels, carry):
        for k in levels:
            for h in span:
                depth_here = bottom[top:end, LANES * (h + 1) : LANES * (h + 2)]
                wet[h * depth + k, 0:rows] = jnp.where(k < depth_here, land[h * depth + k].astype(F32), 0.0)
                wet[h * depth + k, rows : rows + RIM] = jnp.ones((RIM, LANES), F32)
        return carry

    by_groups(0, depth, 5, wet_levels, 0)

    def wet_at(h, k):
        return wet[h * depth + k, 0:rows]

    arrived(get_theta + get_salt + get_vx + get_vy)

    def pack(k, parts, packed):
        both = jnp.where(lane < LANES // 2, parts[0], parts[-1])
        here = ((lane + 2 - 4 * k) & (LANES - 1)) < 4
        return jnp.where(here, roll(both, 4 * k), packed)

    def prepare(levels, packs):
        for k in levels:
            wets = [wet_at(h, k) for h in span]
            qt, qs, uy = [], [], []
            for h in span:
                i = h * depth + k
                qt.append(theta[i] * wets[h])
                qs.append(salt[i] * wets[h])
                uy.append(vy[i])
                first[at(0, h, k), top:end] = qt[h]
                first[at(1, h, k), top:end] = qs[h]
                first[at(2, h, k), top:end] = vx[i] * wets[h] * wet[i, 1 : rows + 1] * (1.0 / 12.0)
            packs = tuple(pack(k, parts, packed) for parts, packed in zip((qt, qs, uy, wets), packs))
        return packs

    for f, packed in enumerate(by_groups(0, depth, 5, prepare, (blank,) * 4)):
        seam_own[f] = packed

    pl.semaphore_wait(barrier, count - 1)

    rims = []
    for dr in (-1, 0, 1):
        for dc in (-1, 0, 1):
            if dr == 0 and dc == 0:
                continue
            targets = [has_before] * (dr < 0) + [has_after] * (dr > 0) + [has_left] * (dc < 0) + [has_right] * (dc > 0)
            sources = [has_after] * (dr < 0) + [has_before] * (dr > 0) + [has_right] * (dc < 0) + [has_left] * (dc > 0)
            src_rows = pl.ds(0, RIM) if dr < 0 else pl.ds(rows - RIM, RIM) if dr > 0 else pl.ds(0, rows)
            src_cols = pl.ds(0, LANES) if dc < 0 else pl.ds(cols - LANES, LANES) if dc > 0 else pl.ds(0, cols)
            dst_rows = pl.ds(end, RIM) if dr < 0 else pl.ds(0, RIM) if dr > 0 else pl.ds(top, rows)
            dst_cols = pl.ds(LANES + cols, LANES) if dc < 0 else pl.ds(0, LANES) if dc > 0 else middle
            for src, dst in ((surface_in, surface), (bottom_in, bottom)):
                i = len(rims)
                copy = pltpu.make_async_remote_copy(
                    src_ref=src.at[src_rows, src_cols],
                    dst_ref=dst.at[dst_rows, dst_cols],
                    send_sem=rim_send.at[i],
                    recv_sem=rim_recv.at[i],
                    device_id=(row + dr, col + dc),
                    device_id_type=MESH,
                )
                rims.append((copy, functools.reduce(jnp.logical_and, targets), functools.reduce(jnp.logical_and, sources)))
    for copy, sends, _ in rims:
        guarded(sends, copy.start)

    def remote(src, dst, i, device):
        return pltpu.make_async_remote_copy(
            src_ref=src, dst_ref=dst, send_sem=halo_send.at[i], recv_sem=halo_recv.at[i], device_id=device, device_id_type=MESH
        )

    after, before = (row + 1, col), (row - 1, col)
    right, left = (row, col + 1), (row, col - 1)
    def row_copies(ref, base, g):
        part = pl.ds(g * per_chunk, per_chunk)
        return [
            (remote(ref.at[part, pl.ds(end - 2, 2)], ref.at[part, pl.ds(top - 2, 2)], base + g, after), has_after, has_before),
            (remote(ref.at[part, pl.ds(top, 2)], ref.at[part, pl.ds(end, 2)], base + chunks + g, before), has_before, has_after),
        ]

    def edge_copies(first_field, fields, base):
        part = pl.ds(first_field, fields)
        return [
            (remote(seam_own.at[part], seam_left.at[part], base, right), has_right, has_left),
            (remote(seam_own.at[part], seam_right.at[part], base + 1, left), has_left, has_right),
        ]

    def send_rows(ref, base):
        for g in range(chunks):
            for copy, sends, _ in row_copies(ref, base, g):
                guarded(sends, copy.start)

    edges_one, edges_two = edge_copies(0, 4, 0), edge_copies(4, 3, 2)
    wet_copy = remote(wet.at[:, pl.ds(0, 1)], wet_after.at[:, pl.ds(0, 1)], 4, before)
    rows_one, rows_two = 5, 5 + 2 * chunks
    for copy, sends, _ in edges_one + [(wet_copy, has_before, has_after)]:
        guarded(sends, copy.start)
    send_rows(first, rows_one)

    def clear(missing, ref, start):
        @pl.when(missing)
        def _():
            ref[:, start : start + 2] = jnp.zeros((ref.shape[0], 2, LANES), F32)

    for ref in (first, second):
        clear(jnp.logical_not(has_before), ref, top - 2)
        clear(jnp.logical_not(has_after), ref, end)
    clear(jnp.logical_not(has_after), wet_after, 0)

    arrived(get_kappa + get_theta_cot + get_salt_cot)

    def down_level(k, last, carry):
        out = []
        for h in span:
            num, den, couple_before, yt, ys, yw = carry[h]
            i = h * depth + k
            wet_here = wet_at(h, k)
            if last:
                den_next = num_next = num
                couple = couple_before
            else:
                couple = kappa[h * (depth - 1) + k] * wet_here * wet_at(h, k + 1)
                den_next = num + couple * den
                num_next = den_next + couple * num
            inv = den * (1.0 / den_next)
            lower = couple_before * inv
            inverse[i] = inv
            link[i] = lower
            if not last:
                ratio[i] = couple * inv
            yt = theta_cot[i] * inv + lower * yt
            ys = salt_cot[i] * inv + lower * ys
            yw = wet_here * inv + lower * yw
            second[at(0, h, k), top:end] = yt
            second[at(1, h, k), top:end] = ys
            second[at(2, h, k), top:end] = yw
            out.append((num_next, den_next, couple, yt, ys, yw))
        return tuple(out)

    def down(levels, carry):
        for k in levels:
            carry = down_level(k, False, carry)
        return carry

    one = jnp.ones((rows, LANES), F32)
    carry = by_groups(0, depth - 1, 4, down, ((one, one, blank, blank, blank, blank),) * halves)
    carry = down_level(depth - 1, True, carry)

    def up(steps, values):
        for n in steps:
            k = depth - 2 - n
            new = []
            for f in range(3):
                parts = []
                for h in span:
                    x = second[at(f, h, k), top:end] + ratio[h * depth + k] * values[f][h]
                    second[at(f, h, k), top:end] = x
                    parts.append(x)
                new.append(tuple(parts))
            values = tuple(new)
        return values

    by_groups(0, depth - 1, 4, up, tuple(tuple(carry[h][3 + f] for h in span) for f in range(3)))

    def pack_second(levels, packs):
        for k in levels:
            packs = tuple(pack(k, [second[at(f, h, k), top:end] for h in span], packs[f]) for f in range(3))
        return packs

    for f, packed in enumerate(by_groups(0, depth, 5, pack_second, (blank,) * 3)):
        seam_own[4 + f] = packed
    get_surface.wait()
    for copy, _, receives in rims:
        guarded(receives, copy.wait_recv)
    wide = (rows + 2 * RIM, cols + 2 * LANES)
    row_at = lax.broadcasted_iota(jnp.int32, wide, 0) - RIM + row * rows
    col_at = lax.broadcasted_iota(jnp.int32, wide, 1) - LANES + col * cols
    inside = ((row_at >= 0) & (row_at < rows * mesh_rows)) & ((col_at >= 0) & (col_at < cols * mesh_cols))
    scaled = (bottom[...].astype(F32) * (1.0 / depth) + (4.2 - CENTRE)) * (1.0 / RADIUS)
    basis = [surface[...]]
    for k in range(ITERS):
        field = basis[-1]
        beside = (pltpu.roll(field, 1, 0) + pltpu.roll(field, wide[0] - 1, 0)) + (
            pltpu.roll(field, 1, 1) + pltpu.roll(field, wide[1] - 1, 1)
        )
        image = scaled * field - beside * (1.0 / RADIUS)
        if k > 0:
            image = 2.0 * image - basis[-2]
        basis.append(jnp.where(inside, image, 0.0))

    def own_product(a, b):
        product = basis[a][top:end, LANES : LANES + cols] * basis[b][top:end, LANES : LANES + cols]
        tiles = [product[i : i + 8, j : j + LANES] for i in range(0, rows, 8) for j in range(0, cols, LANES)]
        return functools.reduce(jnp.add, tiles)

    partial = [own_product(a, b) for a, b in ((0, 0), (0, 1), (0, 2), (0, 3), (0, 4), (2, 3), (3, 3), (3, 4))]
    small_lane = lane_index(8)
    width = LANES // 2
    while len(partial) > 1:
        half = len(partial) // 2
        take_first = (small_lane & (2 * width - 1)) < width
        partial = [
            jnp.where(take_first, a + roll(a, -width), b + roll(b, width)) for a, b in zip(partial[:half], partial[half:])
        ]
        width //= 2
    slots[0:1] = jnp.sum(partial[0], axis=0, keepdims=True)

    def sum_copy(i, device):
        return pltpu.make_async_remote_copy(
            src_ref=slots.at[pl.ds(0, 1)],
            dst_ref=slots.at[pl.ds(i, 1)],
            send_sem=sum_send.at[i],
            recv_sem=sum_recv.at[i],
            device_id=device,
            device_id_type=MESH,
        )

    others(lambda i, device: sum_copy(i, device).start())
    for k in range(ITERS):
        for h in range(halves + 2):
            zeta[k * (halves + 2) + h] = basis[k][:, h * LANES : (h + 1) * LANES]

    for copy, sends, _ in edges_two:
        guarded(sends, copy.start)
    send_rows(second, rows_two)

    for copy, sends, receives in edges_one + [(wet_copy, has_before, has_after)]:
        guarded(sends, copy.wait_send)
        guarded(receives, copy.wait_recv)

    def open_across(uy, near):
        return uy * near * roll(near, -1) * (1.0 / 12.0)

    inner_side = spot < 0
    open_left = open_across(seam_left[2], jnp.where(inner_side, seam_left[3], seam_own[3]))
    open_right = open_across(seam_right[2], seam_right[3])

    def unpack(fields):
        def one_group(levels, carry):
            for k in levels:
                for f, packed in fields:
                    ends[f * depth + k] = roll(packed, LANES - 4 * k)
            return carry

        by_groups(0, depth, 5, one_group, 0)

    def both_sides(f):
        return jnp.where(inner_side, seam_left[f], seam_right[f])

    unpack([(0, both_sides(0)), (1, both_sides(1)), (2, jnp.where(inner_side, open_left, open_right)), (3, both_sides(3))])

    def open_columns(levels, carry):
        ahead = [shifted([wet_at(h, k) for h in span], ends[3 * depth + k], 1, lane) for k in levels]
        for k, wets_ahead in zip(levels, ahead):
            for h in span:
                i = h * depth + k
                open_y[i] = vy[i] * wet_at(h, k) * wets_ahead[h] * (1.0 / 12.0)
        return carry

    by_groups(0, depth, 5, open_columns, 0)
    get_forcing.wait()
    for h in span:
        theta[h * depth] = theta[h * depth] + forcing[:, h * LANES : (h + 1) * LANES] * wet_at(h, 0)

    def column_shifts(ref, f, k, beyond):
        centre = [ref[at(f, h, k), top:end] for h in span]
        return {s: shifted(centre, ends[beyond * depth + k], s, lane) for s in (-2, -1, 1, 2)}

    def face_shifts(k, steps):
        centre = [open_y[h * depth + k] for h in span]
        return {s: shifted(centre, ends[2 * depth + k], s, lane) for s in steps}

    def got_rows(ref, base, levels, sent_too):
        for copy, sends, receives in row_copies(ref, base, lax.div(levels[0], GROUP)):
            if sent_too:
                guarded(sends, copy.wait_send)
            guarded(receives, copy.wait_recv)

    def forward_down(levels, carry):
        got_rows(first, rows_one, levels, True)
        for k in levels:
            for h in span:
                f, i = at(2, h, k), h * depth + k
                first[f, top - 1 : top] = first[f, top - 1 : top] * wet[i, 0:1]
                first[f, end - 1 : end] = first[f, end - 1 : end] * wet_after[i, 0:1]
        moved = [(face_shifts(k, (-1,)), [column_shifts(first, f, k, f) for f in range(2)]) for k in levels]
        for k, (uy, turned) in zip(levels, moved):
            out = []
            for h in span:
                i = h * depth + k
                found = []
                for f, raw in ((0, theta), (1, salt)):
                    q = [first[at(f, h, k), top + s : end + s] for s in (-2, -1, 0, 1, 2)]
                    c = turned[f]
                    row_here = first[at(2, h, k), top:end] * (7.0 * (q[2] + q[3]) - (q[1] + q[4]))
                    row_back = first[at(2, h, k), top - 1 : end - 1] * (7.0 * (q[1] + q[2]) - (q[0] + q[3]))
                    col_here = open_y[i] * (7.0 * (q[2] + c[1][h]) - (c[-1][h] + c[2][h]))
                    col_back = uy[-1][h] * (7.0 * (c[-1][h] + q[2]) - (c[-2][h] + c[1][h]))
                    value = raw[i] - (row_here - row_back) - (col_here - col_back)
                    found.append(value * inverse[i] + link[i] * carry[h][f])
                theta_mix[i] = found[0]
                salt_mix[i] = found[1]
                out.append(tuple(found))
            carry = tuple(out)
        return carry

    carry = by_groups(0, depth, GROUP, forward_down, ((blank, blank),) * halves)

    def forward_up(steps, carry):
        for n in steps:
            k = depth - 2 - n
            out = []
            for h in span:
                i = h * depth + k
                xt = theta_mix[i] + ratio[i] * carry[h][0]
                xs = salt_mix[i] + ratio[i] * carry[h][1]
                dt, ds = xt - carry[h][0], xs - carry[h][1]
                step_t, step_s, step_w = [
                    second[at(f, h, k), top:end] - second[at(f, h, k + 1), top:end] for f in range(3)
                ]
                closed = -wet_at(h, k) * wet_at(h, k + 1)
                k_fixed[h * (depth - 1) + k] = closed * (step_t * dt + step_s * ds)
                k_zeta[h * (depth - 1) + k] = closed * step_w * (0.2 * dt - 0.15 * ds)
                out.append((xt, xs))
            carry = tuple(out)
        return carry

    by_groups(0, depth - 1, 4, forward_up, carry)

    def arms(u, wets):
        v = [wets * x for x in u]
        back, here = 7.0 * v[1], 7.0 * v[2]
        return v[0], back + v[0], back - here, here + v[3], v[3]

    def coefficients(levels, carry):
        moved = [face_shifts(k, (-2, -1, 1)) for k in levels]
        for k, uy in zip(levels, moved):
            for h in span:
                i = h * depth + k
                wets = wet_at(h, k)
                r = arms([first[at(2, h, k), top + s : end + s] for s in (-2, -1, 0, 1)], wets)
                c = arms([uy[-2][h], uy[-1][h], open_y[i], uy[1][h]], wets)
                for n, w in enumerate([(1.0 + r[2]) + c[2], r[0], r[3], c[0], c[3], r[1], r[4], c[1], c[4]]):
                    cross[9 * i + n] = w
        return carry

    by_groups(0, depth, GROUP, coefficients, 0)

    others(lambda i, device: sum_copy(i, device).wait_recv())
    total = jnp.broadcast_to(jnp.sum(slots[...], axis=0, keepdims=True), (8, LANES))
    for step in (8, 4, 2, 1):
        total = total + roll(total, -step)
    m = [jnp.broadcast_to(total[:, 16 * g : 16 * g + 1], (8, LANES)) for g in range(8)]
    m = m[:5] + [2.0 * m[5] - m[1], 2.0 * m[6] - m[0], 2.0 * m[7] - m[1]]
    weights = [jnp.concatenate([w] * (wide[0] // 8), axis=0) for w in weights_from(m)]
    tiles = halves + 2
    for h in range(tiles):
        b = [zeta[k * tiles + h] for k in range(ITERS)]
        zeta[h] = (weights[0] * b[0] + weights[1] * b[1]) + (weights[2] * b[2] + weights[3] * b[3])

    for copy, sends, receives in edges_two:
        guarded(sends, copy.wait_send)
        guarded(receives, copy.wait_recv)
    beyond = jnp.where(lane >= LANES // 2, zeta[0, top:end], zeta[tiles - 1, top:end])
    far_t, far_s, far_w = both_sides(4), both_sides(5), both_sides(6)

    def unpack_mu(levels, carry):
        for k in levels:
            turned = [roll(p, LANES - 4 * k) for p in (far_t, far_s, far_w)]
            lifted = turned[2] * beyond
            ends[4 * depth + k] = turned[0] + 0.2 * lifted
            ends[5 * depth + k] = turned[1] - 0.15 * lifted
        return carry

    by_groups(0, depth, 5, unpack_mu, 0)

    def finish(levels, carry):
        got_rows(second, rows_two, levels, True)
        for k in levels:
            for h in span:
                area = pl.ds(top - 2, rows + 8)
                lifted = second[at(2, h, k), area] * zeta[h + 1, area]
                second[at(0, h, k), area] = second[at(0, h, k), area] + 0.2 * lifted
                second[at(1, h, k), area] = second[at(1, h, k), area] - 0.15 * lifted
        moved = [[column_shifts(second, f, k, 4 + f) for f in range(2)] for k in levels]
        for k, turned in zip(levels, moved):
            for h in span:
                i = h * depth + k
                where = slice(h * LANES, (h + 1) * LANES)
                for f, out in ((0, theta_grad), (1, salt_grad)):
                    values = [second[at(f, h, k), top + s : end + s] for s in (0, -2, 1)]
                    values += [turned[f][s][h] for s in (-2, 1)]
                    values += [second[at(f, h, k), top + s : end + s] for s in (-1, 2)]
                    values += [turned[f][s][h] for s in (-1, 2)]
                    out[k, :, where] = signed_sum([cross[9 * i + n] * v for n, v in enumerate(values)])
        return carry

    by_groups(0, depth, GROUP, finish, 0)

    def finish_kappa(levels, carry):
        for k in levels:
            for h in span:
                j = h * (depth - 1) + k
                kappa_grad[k, :, h * LANES : (h + 1) * LANES] = k_fixed[j] + k_zeta[j] * zeta[h + 1, top:end]
        return carry

    by_groups(0, depth - 1, 4, finish_kappa, 0)
    for h in span:
        forcing_grad[:, h * LANES : (h + 1) * LANES] = zeta[h + 1, top:end] + wet_at(h, 0) * second[at(0, h, 0), top:end]

    for copy, sends, _ in rims:
        guarded(sends, copy.wait_send)
    others(lambda i, device: sum_copy(i, device).wait_send())


def write_kernel(*refs):
    count = (len(refs) - 1) // 2
    sems = refs[-1]
    copies = [pltpu.make_async_copy(refs[i], refs[count + i], sems.at[i]) for i in range(count)]
    for copy in copies:
        copy.start()
    for copy in copies:
        copy.wait()


def shards(*args):
    theta = args[0]
    depth, rows, cols = theta.shape
    halves = cols // LANES
    count = lax.axis_size("trow") * lax.axis_size("tcol")
    tall = rows + 2 * RIM
    V = pltpu.VMEM
    DMA = pltpu.SemaphoreType.DMA
    flat = V((halves * depth, rows, LANES), F32)
    ints = V((halves * depth, rows, LANES), jnp.int32)
    upper = V((halves * (depth - 1), rows, LANES), F32)
    tile = V((7, rows, LANES), F32)
    halo = DMA((5 + 4 * (depth // GROUP),))
    scratch = [
        flat, flat, flat, flat, ints, upper, V((rows, cols), F32), flat, flat,
        V((tall, cols + 2 * LANES), F32), V((tall, cols + 2 * LANES), jnp.int32),
        V((halves * depth, rows + RIM, LANES), F32), V((halves * depth, RIM, LANES), F32),
        V((3 * halves * depth, tall, LANES), F32), V((3 * halves * depth, tall, LANES), F32),
        flat, flat, flat, flat, flat, flat,
        tile, tile, tile, V((7 * depth, rows, LANES), F32), V((count, LANES), F32),
        V((9 * halves * depth, rows, LANES), F32), upper, upper, V((ITERS * (halves + 2), tall, LANES), F32),
        DMA((3 + 8 * halves,)), DMA((16,)), DMA((16,)), halo, halo, DMA((count,)), DMA((count,)),
    ]
    outs = [(depth, rows, cols), (depth, rows, cols), (depth - 1, rows, cols), (rows, cols)]
    shapes = [jax.ShapeDtypeStruct(o, F32) for o in outs]
    found = pl.pallas_call(
        functools.partial(solve_kernel, (depth, rows, cols)),
        out_shape=shapes,
        in_specs=[pl.BlockSpec(memory_space=pltpu.HBM)] * len(args),
        out_specs=[pl.BlockSpec(memory_space=V)] * len(outs),
        scratch_shapes=scratch,
        compiler_params=pltpu.CompilerParams(
            collective_id=0, has_side_effects=True, vmem_limit_bytes=40 * 1024 * 1024
        ),
    )(*[pltpu.with_memory_space_constraint(a, pltpu.HBM) for a in args])
    return tuple(
        pl.pallas_call(
            write_kernel,
            out_shape=shapes,
            in_specs=[pl.BlockSpec(memory_space=V)] * len(outs),
            out_specs=[pl.BlockSpec(memory_space=pltpu.HBM)] * len(outs),
            scratch_shapes=[DMA((len(outs),))],
            compiler_params=pltpu.CompilerParams(vmem_limit_bytes=1024 * 1024),
        )(*found)
    )


def solution(mesh):
    cube, plane = P(None, "trow", "tcol"), P("trow", "tcol")
    in_specs = (cube,) * 6 + (plane,) * 2 + (cube,) * 2 + (plane,)
    out_specs = (cube,) * 3 + (plane,)
    return jax.shard_map(shards, mesh=mesh, in_specs=in_specs, out_specs=out_specs, check_vma=False)
```

```python
import functools
import jax
import jax.numpy as jnp
from jax import lax
from jax.experimental import pallas as pl
from jax.experimental.pallas import tpu as pltpu
from jax.sharding import PartitionSpec as P

ITERS = 4
LANES = 128
RIM = 8
LOW, HIGH = 0.2, 9.2
CENTRE, RADIUS = (HIGH + LOW) / 2, (HIGH - LOW) / 2
MESH = pl.DeviceIdType.MESH
F32 = jnp.float32


def put(out, k, value):
    out[k] = value if out[k] is None else out[k] + value


def times_operator(poly):
    out = [None] * (len(poly) + 1)
    for k, c in enumerate(poly):
        put(out, k, CENTRE * c)
        if k == 0:
            put(out, 1, RADIUS * c)
        else:
            half = (0.5 * RADIUS) * c
            put(out, k + 1, half)
            put(out, k - 1, half)
    return out


def inner(p, q, table):
    total = None
    for i, a in enumerate(p):
        part = None
        for j, b in enumerate(q):
            term = b * table[i][j]
            part = term if part is None else part + term
        part = a * part
        total = part if total is None else total + part
    return total


def add_scaled(p, scale, q):
    out = []
    for k in range(max(len(p), len(q))):
        if k >= len(p):
            out.append(scale * q[k])
        elif k >= len(q):
            out.append(p[k])
        else:
            out.append(p[k] + scale * q[k])
    return out


def weights_from(moments):
    table = [
        [
            moments[j] if i == 0 else moments[i] if j == 0 else 0.5 * (moments[i + j] + moments[abs(i - j)])
            for j in range(ITERS + 1)
        ]
        for i in range(ITERS)
    ]
    residual = [jnp.ones_like(moments[0])]
    direction = residual
    result = []
    norm_now = moments[0]
    for iteration in range(ITERS):
        image = times_operator(direction)
        step = norm_now / inner(direction, image, table)
        result = add_scaled(result, step, direction)
        if iteration + 1 < ITERS:
            residual = add_scaled(residual, -step, image)
            norm_next = inner(residual, residual, table)
            direction = add_scaled(residual, norm_next / norm_now, direction)
            norm_now = norm_next
    return result


def lane_index(rows):
    return lax.broadcasted_iota(jnp.int32, (rows, LANES), 1)


def roll(x, amount):
    return pltpu.roll(x, amount % LANES if isinstance(amount, int) else amount & (LANES - 1), 1)


def shifted(parts, ends, by, lane):
    if by > 0:
        joined = [jnp.where(lane < by, nearby, p) for p, nearby in zip(parts, parts[1:] + [ends])]
    else:
        joined = [jnp.where(lane >= LANES + by, nearby, p) for p, nearby in zip(parts, [ends] + parts[:-1])]
    return [roll(p, -by) for p in joined]


GROUP = 5


def by_groups(start, stop, group, body, carry):
    count = (stop - start) // group
    carry = lax.fori_loop(0, count, lambda i, c: body([start + i * group + u for u in range(group)], c), carry)
    rest = list(range(start + count * group, stop))
    return body(rest, carry) if rest else carry


def signed_sum(terms):
    return terms[0] + (((terms[1] + terms[2]) - (terms[5] + terms[6])) + ((terms[3] + terms[4]) - (terms[7] + terms[8])))


def guarded(condition, action):
    @pl.when(condition)
    def _():
        action()


def solve_kernel(
    sizes,
    theta_in, salt_in, vx_in, vy_in, land_in, kappa_in, forcing_in, bottom_in, theta_cot_in, salt_cot_in, surface_in,
    theta_grad, salt_grad, kappa_grad, forcing_grad,
    theta, salt, vx, vy, land, kappa, forcing, theta_cot, salt_cot,
    surface, bottom, wet, wet_after, face_x, first, second, open_y, inverse, link, ratio, theta_mix, salt_mix,
    seam_own, seam_left, seam_right, ends, slots, cross, k_fixed, k_zeta, zeta,
    local_sem, rim_send, rim_recv, halo_send, halo_recv, sum_send, sum_recv,
):
    depth, rows, cols = sizes
    halves = cols // LANES
    top, end = RIM, RIM + rows
    mesh_rows, mesh_cols = lax.axis_size("trow"), lax.axis_size("tcol")
    count = mesh_rows * mesh_cols
    row, col = lax.axis_index("trow"), lax.axis_index("tcol")
    has_before, has_after = row > 0, row < mesh_rows - 1
    has_left, has_right = col > 0, col < mesh_cols - 1
    lane = lane_index(rows)
    spot = ((lane + 2) & 3) - 2
    blank = jnp.zeros((rows, LANES), F32)
    span = range(halves)

    chunks = depth // GROUP

    def at(f, h, k):
        return (k * 3 + f) * halves + h

    def at_first(f, h, k):
        return (k * 2 + f) * halves + h

    surface[...] = jnp.zeros_like(surface)
    bottom[...] = jnp.zeros_like(bottom)
    seam_left[...] = jnp.zeros_like(seam_left)
    seam_right[...] = jnp.zeros_like(seam_right)

    barrier = pltpu.get_barrier_semaphore()

    def others(action):
        for dc in range(1, mesh_cols):
            action(dc, (row, lax.rem(col + dc, mesh_cols)))

        def one_row(dr, carry):
            there = lax.rem(row + dr, mesh_rows)
            for dc in range(mesh_cols):
                action(dr * mesh_cols + dc, (there, lax.rem(col + dc, mesh_cols)))
            return carry

        lax.fori_loop(1, mesh_rows, one_row, 0)

    others(lambda i, device: pl.semaphore_signal(barrier, inc=1, device_id=device, device_id_type=MESH))

    started = []

    def fetch(src, dst):
        copy = pltpu.make_async_copy(src, dst, local_sem.at[len(started)])
        copy.start()
        started.append(copy)
        return copy

    middle = pl.ds(LANES, cols)
    get_surface = fetch(surface_in, surface.at[pl.ds(RIM, rows), middle])
    get_bottom = fetch(bottom_in, bottom.at[pl.ds(RIM, rows), middle])

    def fetch_halves(src, dst):
        return [
            fetch(src.at[:, :, pl.ds(h * LANES, LANES)], dst.at[pl.ds(h * src.shape[0], src.shape[0])]) for h in span
        ]

    get_land = fetch_halves(land_in, land)
    get_theta = fetch_halves(theta_in, theta)
    get_salt = fetch_halves(salt_in, salt)
    get_vx = fetch_halves(vx_in, vx)
    get_vy = fetch_halves(vy_in, vy)
    get_forcing = fetch(forcing_in, forcing)
    get_kappa = fetch_halves(kappa_in, kappa)
    get_theta_cot = fetch_halves(theta_cot_in, theta_cot)
    get_salt_cot = fetch_halves(salt_cot_in, salt_cot)

    def arrived(copies):
        for copy in copies:
            copy.wait()

    arrived([get_bottom] + get_land)

    def wet_levels(levels, carry):
        for k in levels:
            for h in span:
                depth_here = bottom[top:end, LANES * (h + 1) : LANES * (h + 2)]
                wet[h * depth + k, 0:rows] = jnp.where(k < depth_here, land[h * depth + k].astype(F32), 0.0)
                wet[h * depth + k, rows : rows + RIM] = jnp.ones((RIM, LANES), F32)
        return carry

    by_groups(0, depth, 5, wet_levels, 0)

    def wet_at(h, k):
        return wet[h * depth + k, 0:rows]

    arrived(get_theta + get_salt + get_vx + get_vy)

    def pack(k, parts, packed):
        both = jnp.where(lane < LANES // 2, parts[0], parts[-1])
        here = ((lane + 2 - 4 * k) & (LANES - 1)) < 4
        return jnp.where(here, roll(both, 4 * k), packed)

    def prepare(levels, packs):
        for k in levels:
            wets = [wet_at(h, k) for h in span]
            qt, qs, uy = [], [], []
            for h in span:
                i = h * depth + k
                qt.append(theta[i] * wets[h])
                qs.append(salt[i] * wets[h])
                uy.append(vy[i])
                first[at_first(0, h, k), top:end] = qt[h]
                first[at_first(1, h, k), top:end] = qs[h]
                face_x[i, top:end] = vx[i] * wets[h] * wet[i, 1 : rows + 1] * (1.0 / 12.0)
            packs = tuple(pack(k, parts, packed) for parts, packed in zip((qt, qs, uy, wets), packs))
        return packs

    for f, packed in enumerate(by_groups(0, depth, 5, prepare, (blank,) * 4)):
        seam_own[f] = packed

    pl.semaphore_wait(barrier, count - 1)

    rims = []
    for dr in (-1, 0, 1):
        for dc in (-1, 0, 1):
            if dr == 0 and dc == 0:
                continue
            targets = [has_before] * (dr < 0) + [has_after] * (dr > 0) + [has_left] * (dc < 0) + [has_right] * (dc > 0)
            sources = [has_after] * (dr < 0) + [has_before] * (dr > 0) + [has_right] * (dc < 0) + [has_left] * (dc > 0)
            src_rows = pl.ds(0, RIM) if dr < 0 else pl.ds(rows - RIM, RIM) if dr > 0 else pl.ds(0, rows)
            src_cols = pl.ds(0, LANES) if dc < 0 else pl.ds(cols - LANES, LANES) if dc > 0 else pl.ds(0, cols)
            dst_rows = pl.ds(end, RIM) if dr < 0 else pl.ds(0, RIM) if dr > 0 else pl.ds(top, rows)
            dst_cols = pl.ds(LANES + cols, LANES) if dc < 0 else pl.ds(0, LANES) if dc > 0 else middle
            for src, dst in ((surface_in, surface), (bottom_in, bottom)):
                i = len(rims)
                copy = pltpu.make_async_remote_copy(
                    src_ref=src.at[src_rows, src_cols],
                    dst_ref=dst.at[dst_rows, dst_cols],
                    send_sem=rim_send.at[i],
                    recv_sem=rim_recv.at[i],
                    device_id=(row + dr, col + dc),
                    device_id_type=MESH,
                )
                rims.append((copy, functools.reduce(jnp.logical_and, targets), functools.reduce(jnp.logical_and, sources)))
    for copy, sends, _ in rims:
        guarded(sends, copy.start)

    def remote(src, dst, i, device):
        return pltpu.make_async_remote_copy(
            src_ref=src, dst_ref=dst, send_sem=halo_send.at[i], recv_sem=halo_recv.at[i], device_id=device, device_id_type=MESH
        )

    after, before = (row + 1, col), (row - 1, col)
    right, left = (row, col + 1), (row, col - 1)
    def row_copies(ref, base, g):
        per_chunk = ref.shape[0] // chunks
        part = pl.ds(g * per_chunk, per_chunk)
        return [
            (remote(ref.at[part, pl.ds(end - 2, 2)], ref.at[part, pl.ds(top - 2, 2)], base + g, after), has_after, has_before),
            (remote(ref.at[part, pl.ds(top, 2)], ref.at[part, pl.ds(end, 2)], base + chunks + g, before), has_before, has_after),
        ]

    def edge_copies(first_field, fields, base):
        part = pl.ds(first_field, fields)
        return [
            (remote(seam_own.at[part], seam_left.at[part], base, right), has_right, has_left),
            (remote(seam_own.at[part], seam_right.at[part], base + 1, left), has_left, has_right),
        ]

    def send_rows(ref, base):
        for g in range(chunks):
            for copy, sends, _ in row_copies(ref, base, g):
                guarded(sends, copy.start)

    edges_one, edges_two = edge_copies(0, 4, 0), edge_copies(4, 3, 2)
    wet_copy = remote(wet.at[:, pl.ds(0, 1)], wet_after.at[:, pl.ds(0, 1)], 4, before)
    faces_down = remote(face_x.at[:, pl.ds(end - 2, 2)], face_x.at[:, pl.ds(top - 2, 2)], 5, after)
    faces_up = remote(face_x.at[:, pl.ds(top, 1)], face_x.at[:, pl.ds(end, 1)], 6, before)
    early = [(wet_copy, has_before, has_after), (faces_down, has_after, has_before), (faces_up, has_before, has_after)]
    rows_one, rows_two = 7, 7 + 2 * chunks
    for copy, sends, _ in edges_one + early:
        guarded(sends, copy.start)
    send_rows(first, rows_one)

    def clear(missing, ref, start):
        @pl.when(missing)
        def _():
            ref[:, start : start + 2] = jnp.zeros((ref.shape[0], 2, LANES), F32)

    for ref in (face_x, first, second):
        clear(jnp.logical_not(has_before), ref, top - 2)
        clear(jnp.logical_not(has_after), ref, end)
    clear(jnp.logical_not(has_after), wet_after, 0)

    arrived(get_kappa + get_theta_cot + get_salt_cot)

    def down_level(k, last, carry):
        out = []
        for h in span:
            num, den, couple_before, yt, ys, yw = carry[h]
            i = h * depth + k
            wet_here = wet_at(h, k)
            if last:
                den_next = num_next = num
                couple = couple_before
            else:
                couple = kappa[h * (depth - 1) + k] * wet_here * wet_at(h, k + 1)
                den_next = num + couple * den
                num_next = den_next + couple * num
            inv = den * (1.0 / den_next)
            lower = couple_before * inv
            inverse[i] = inv
            link[i] = lower
            if not last:
                ratio[i] = couple * inv
            yt = theta_cot[i] * inv + lower * yt
            ys = salt_cot[i] * inv + lower * ys
            yw = wet_here * inv + lower * yw
            second[at(0, h, k), top:end] = yt
            second[at(1, h, k), top:end] = ys
            second[at(2, h, k), top:end] = yw
            out.append((num_next, den_next, couple, yt, ys, yw))
        return tuple(out)

    def down(levels, carry):
        for k in levels:
            carry = down_level(k, False, carry)
        return carry

    one = jnp.ones((rows, LANES), F32)
    carry = by_groups(0, depth - 1, 4, down, ((one, one, blank, blank, blank, blank),) * halves)
    carry = down_level(depth - 1, True, carry)

    def up(steps, values):
        for n in steps:
            k = depth - 2 - n
            new = []
            for f in range(3):
                parts = []
                for h in span:
                    x = second[at(f, h, k), top:end] + ratio[h * depth + k] * values[f][h]
                    second[at(f, h, k), top:end] = x
                    parts.append(x)
                new.append(tuple(parts))
            values = tuple(new)
        return values

    by_groups(0, depth - 1, 4, up, tuple(tuple(carry[h][3 + f] for h in span) for f in range(3)))

    def pack_second(levels, packs):
        for k in levels:
            packs = tuple(pack(k, [second[at(f, h, k), top:end] for h in span], packs[f]) for f in range(3))
        return packs

    for f, packed in enumerate(by_groups(0, depth, depth, pack_second, (blank,) * 3)):
        seam_own[4 + f] = packed
    get_surface.wait()
    for copy, _, receives in rims:
        guarded(receives, copy.wait_recv)
    wide = (rows + 2 * RIM, cols + 2 * LANES)
    row_at = lax.broadcasted_iota(jnp.int32, wide, 0) - RIM + row * rows
    col_at = lax.broadcasted_iota(jnp.int32, wide, 1) - LANES + col * cols
    inside = ((row_at >= 0) & (row_at < rows * mesh_rows)) & ((col_at >= 0) & (col_at < cols * mesh_cols))
    scaled = (bottom[...].astype(F32) * (1.0 / depth) + (4.2 - CENTRE)) * (1.0 / RADIUS)
    basis = [surface[...]]
    for k in range(ITERS):
        field = basis[-1]
        beside = (pltpu.roll(field, 1, 0) + pltpu.roll(field, wide[0] - 1, 0)) + (
            pltpu.roll(field, 1, 1) + pltpu.roll(field, wide[1] - 1, 1)
        )
        image = scaled * field - beside * (1.0 / RADIUS)
        if k > 0:
            image = 2.0 * image - basis[-2]
        basis.append(jnp.where(inside, image, 0.0))

    def own_product(a, b):
        product = basis[a][top:end, LANES : LANES + cols] * basis[b][top:end, LANES : LANES + cols]
        tiles = [product[i : i + 8, j : j + LANES] for i in range(0, rows, 8) for j in range(0, cols, LANES)]
        return functools.reduce(jnp.add, tiles)

    partial = [own_product(a, b) for a, b in ((0, 0), (0, 1), (0, 2), (0, 3), (0, 4), (2, 3), (3, 3), (3, 4))]
    place = lax.broadcasted_iota(jnp.int32, (8, LANES), 0)
    stacked = jnp.zeros((8, LANES), F32)
    for g, p in enumerate(partial):
        stacked = jnp.where(place == g, jnp.sum(p, axis=0, keepdims=True), stacked)
    stacked = jnp.broadcast_to(jnp.sum(stacked, axis=1, keepdims=True), (8, LANES))
    mine = jnp.where((lane_index(8) >> 4) == place, stacked, 0.0)
    slots[0:1] = jnp.sum(mine, axis=0, keepdims=True)

    def sum_copy(i, device):
        return pltpu.make_async_remote_copy(
            src_ref=slots.at[pl.ds(0, 1)],
            dst_ref=slots.at[pl.ds(i, 1)],
            send_sem=sum_send.at[i],
            recv_sem=sum_recv.at[i],
            device_id=device,
            device_id_type=MESH,
        )

    others(lambda i, device: sum_copy(i, device).start())
    for k in range(ITERS):
        for h in range(halves + 2):
            zeta[k * (halves + 2) + h] = basis[k][:, h * LANES : (h + 1) * LANES]

    for copy, sends, _ in edges_two:
        guarded(sends, copy.start)
    send_rows(second, rows_two)

    for copy, sends, receives in edges_one:
        guarded(sends, copy.wait_send)
        guarded(receives, copy.wait_recv)

    def open_across(uy, near):
        return uy * near * roll(near, -1) * (1.0 / 12.0)

    inner_side = spot < 0
    open_left = open_across(seam_left[2], jnp.where(inner_side, seam_left[3], seam_own[3]))
    open_right = open_across(seam_right[2], seam_right[3])

    def unpack(fields):
        def one_group(levels, carry):
            for k in levels:
                for f, packed in fields:
                    ends[f * depth + k] = roll(packed, LANES - 4 * k)
            return carry

        by_groups(0, depth, depth, one_group, 0)

    def both_sides(f):
        return jnp.where(inner_side, seam_left[f], seam_right[f])

    unpack([(0, both_sides(0)), (1, both_sides(1)), (2, jnp.where(inner_side, open_left, open_right)), (3, both_sides(3))])

    def open_columns(levels, carry):
        ahead = [shifted([wet_at(h, k) for h in span], ends[3 * depth + k], 1, lane) for k in levels]
        for k, wets_ahead in zip(levels, ahead):
            for h in span:
                i = h * depth + k
                open_y[i] = vy[i] * wet_at(h, k) * wets_ahead[h] * (1.0 / 12.0)
        return carry

    by_groups(0, depth, depth, open_columns, 0)
    get_forcing.wait()
    for h in span:
        theta[h * depth] = theta[h * depth] + forcing[:, h * LANES : (h + 1) * LANES] * wet_at(h, 0)

    def column_shifts(ref, where, f, k, beyond):
        centre = [ref[where(f, h, k), top:end] for h in span]
        return {s: shifted(centre, ends[beyond * depth + k], s, lane) for s in (-2, -1, 1, 2)}

    def face_shifts(k, steps):
        centre = [open_y[h * depth + k] for h in span]
        return {s: shifted(centre, ends[2 * depth + k], s, lane) for s in steps}

    def got_rows(ref, base, levels, sent_too):
        for copy, sends, receives in row_copies(ref, base, lax.div(levels[0], GROUP)):
            if sent_too:
                guarded(sends, copy.wait_send)
            guarded(receives, copy.wait_recv)

    def arms(u, wets):
        v = [wets * x for x in u]
        back, here = 7.0 * v[1], 7.0 * v[2]
        return v[0], back + v[0], back - here, here + v[3], v[3]

    for copy, sends, receives in early:
        guarded(sends, copy.wait_send)
        guarded(receives, copy.wait_recv)

    def coefficients(levels, carry):
        for k in levels:
            for h in span:
                i = h * depth + k
                face_x[i, top - 1 : top] = face_x[i, top - 1 : top] * wet[i, 0:1]
                face_x[i, end - 1 : end] = face_x[i, end - 1 : end] * wet_after[i, 0:1]
        moved = [face_shifts(k, (-2, -1, 1)) for k in levels]
        for k, uy in zip(levels, moved):
            for h in span:
                i = h * depth + k
                wets = wet_at(h, k)
                r = arms([face_x[i, top + s : end + s] for s in (-2, -1, 0, 1)], wets)
                c = arms([uy[-2][h], uy[-1][h], open_y[i], uy[1][h]], wets)
                for n, w in enumerate([(1.0 + r[2]) + c[2], r[0], r[3], c[0], c[3], r[1], r[4], c[1], c[4]]):
                    cross[9 * i + n] = w
        return carry

    by_groups(0, depth, GROUP, coefficients, 0)

    def forward_down(levels, carry):
        got_rows(first, rows_one, levels, True)
        moved = [
            (face_shifts(k, (-1,)), [column_shifts(first, at_first, f, k, f) for f in range(2)]) for k in levels
        ]
        for k, (uy, turned) in zip(levels, moved):
            out = []
            for h in span:
                i = h * depth + k
                found = []
                for f, raw in ((0, theta), (1, salt)):
                    q = [first[at_first(f, h, k), top + s : end + s] for s in (-2, -1, 0, 1, 2)]
                    c = turned[f]
                    row_here = face_x[i, top:end] * (7.0 * (q[2] + q[3]) - (q[1] + q[4]))
                    row_back = face_x[i, top - 1 : end - 1] * (7.0 * (q[1] + q[2]) - (q[0] + q[3]))
                    col_here = open_y[i] * (7.0 * (q[2] + c[1][h]) - (c[-1][h] + c[2][h]))
                    col_back = uy[-1][h] * (7.0 * (c[-1][h] + q[2]) - (c[-2][h] + c[1][h]))
                    value = raw[i] - (row_here - row_back) - (col_here - col_back)
                    found.append(value * inverse[i] + link[i] * carry[h][f])
                theta_mix[i] = found[0]
                salt_mix[i] = found[1]
                out.append(tuple(found))
            carry = tuple(out)
        return carry

    carry = by_groups(0, depth, GROUP, forward_down, ((blank, blank),) * halves)

    def forward_up(steps, carry):
        for n in steps:
            k = depth - 2 - n
            out = []
            for h in span:
                i = h * depth + k
                xt = theta_mix[i] + ratio[i] * carry[h][0]
                xs = salt_mix[i] + ratio[i] * carry[h][1]
                dt, ds = xt - carry[h][0], xs - carry[h][1]
                step_t, step_s, step_w = [
                    second[at(f, h, k), top:end] - second[at(f, h, k + 1), top:end] for f in range(3)
                ]
                closed = -wet_at(h, k) * wet_at(h, k + 1)
                k_fixed[h * (depth - 1) + k] = closed * (step_t * dt + step_s * ds)
                k_zeta[h * (depth - 1) + k] = closed * step_w * (0.2 * dt - 0.15 * ds)
                out.append((xt, xs))
            carry = tuple(out)
        return carry

    by_groups(0, depth - 1, 4, forward_up, carry)

    others(lambda i, device: sum_copy(i, device).wait_recv())
    total = jnp.broadcast_to(jnp.sum(slots[...], axis=0, keepdims=True), (8, LANES))
    m = [jnp.broadcast_to(total[:, 16 * g : 16 * g + 1], (8, LANES)) for g in range(8)]
    m = m[:5] + [2.0 * m[5] - m[1], 2.0 * m[6] - m[0], 2.0 * m[7] - m[1]]
    weights = [jnp.concatenate([w] * (wide[0] // 8), axis=0) for w in weights_from(m)]
    tiles = halves + 2
    for h in range(tiles):
        b = [zeta[k * tiles + h] for k in range(ITERS)]
        zeta[h] = (weights[0] * b[0] + weights[1] * b[1]) + (weights[2] * b[2] + weights[3] * b[3])

    for copy, sends, receives in edges_two:
        guarded(sends, copy.wait_send)
        guarded(receives, copy.wait_recv)
    beyond = jnp.where(lane >= LANES // 2, zeta[0, top:end], zeta[tiles - 1, top:end])
    far_t, far_s, far_w = both_sides(4), both_sides(5), both_sides(6)

    def unpack_mu(levels, carry):
        for k in levels:
            turned = [roll(p, LANES - 4 * k) for p in (far_t, far_s, far_w)]
            lifted = turned[2] * beyond
            ends[4 * depth + k] = turned[0] + 0.2 * lifted
            ends[5 * depth + k] = turned[1] - 0.15 * lifted
        return carry

    by_groups(0, depth, depth, unpack_mu, 0)

    def finish(levels, carry):
        got_rows(second, rows_two, levels, True)
        for k in levels:
            for h in span:
                area = pl.ds(top - 2, rows + 8)
                lifted = second[at(2, h, k), area] * zeta[h + 1, area]
                second[at(0, h, k), area] = second[at(0, h, k), area] + 0.2 * lifted
                second[at(1, h, k), area] = second[at(1, h, k), area] - 0.15 * lifted
        moved = [[column_shifts(second, at, f, k, 4 + f) for f in range(2)] for k in levels]
        for k, turned in zip(levels, moved):
            for h in span:
                i = h * depth + k
                where = slice(h * LANES, (h + 1) * LANES)
                for f, out in ((0, theta_grad), (1, salt_grad)):
                    values = [second[at(f, h, k), top + s : end + s] for s in (0, -2, 1)]
                    values += [turned[f][s][h] for s in (-2, 1)]
                    values += [second[at(f, h, k), top + s : end + s] for s in (-1, 2)]
                    values += [turned[f][s][h] for s in (-1, 2)]
                    out[k, :, where] = signed_sum([cross[9 * i + n] * v for n, v in enumerate(values)])
        return carry

    by_groups(0, depth, GROUP, finish, 0)

    def finish_kappa(levels, carry):
        for k in levels:
            for h in span:
                j = h * (depth - 1) + k
                kappa_grad[k, :, h * LANES : (h + 1) * LANES] = k_fixed[j] + k_zeta[j] * zeta[h + 1, top:end]
        return carry

    by_groups(0, depth - 1, 4, finish_kappa, 0)
    for h in span:
        forcing_grad[:, h * LANES : (h + 1) * LANES] = zeta[h + 1, top:end] + wet_at(h, 0) * second[at(0, h, 0), top:end]

    for copy, sends, _ in rims:
        guarded(sends, copy.wait_send)
    others(lambda i, device: sum_copy(i, device).wait_send())


def write_kernel(*refs):
    count = (len(refs) - 1) // 2
    sems = refs[-1]
    copies = []
    for i in range(count):
        pieces = 1
        bounds = [refs[i].shape[0] * n // pieces for n in range(pieces + 1)]
        for first, last in zip(bounds, bounds[1:]):
            part = pl.ds(first, last - first)
            copies.append(pltpu.make_async_copy(refs[i].at[part], refs[count + i].at[part], sems.at[len(copies)]))
    for copy in copies:
        copy.start()
    for copy in copies:
        copy.wait()


def shards(*args):
    theta = args[0]
    depth, rows, cols = theta.shape
    halves = cols // LANES
    count = lax.axis_size("trow") * lax.axis_size("tcol")
    tall = rows + 2 * RIM
    V = pltpu.VMEM
    DMA = pltpu.SemaphoreType.DMA
    flat = V((halves * depth, rows, LANES), F32)
    ints = V((halves * depth, rows, LANES), jnp.int32)
    upper = V((halves * (depth - 1), rows, LANES), F32)
    tile = V((7, rows, LANES), F32)
    halo = DMA((7 + 4 * (depth // GROUP),))
    scratch = [
        flat, flat, flat, flat, ints, upper, V((rows, cols), F32), flat, flat,
        V((tall, cols + 2 * LANES), F32), V((tall, cols + 2 * LANES), jnp.int32),
        V((halves * depth, rows + RIM, LANES), F32), V((halves * depth, RIM, LANES), F32),
        V((halves * depth, tall, LANES), F32), V((2 * halves * depth, tall, LANES), F32),
        V((3 * halves * depth, tall, LANES), F32),
        flat, flat, flat, flat, flat, flat,
        tile, tile, tile, V((7 * depth, rows, LANES), F32), V((count, LANES), F32),
        V((9 * halves * depth, rows, LANES), F32), upper, upper, V((ITERS * (halves + 2), tall, LANES), F32),
        DMA((3 + 8 * halves,)), DMA((16,)), DMA((16,)), halo, halo, DMA((count,)), DMA((count,)),
    ]
    outs = [(depth, rows, cols), (depth, rows, cols), (depth - 1, rows, cols), (rows, cols)]
    shapes = [jax.ShapeDtypeStruct(o, F32) for o in outs]
    found = pl.pallas_call(
        functools.partial(solve_kernel, (depth, rows, cols)),
        out_shape=shapes,
        in_specs=[pl.BlockSpec(memory_space=pltpu.HBM)] * len(args),
        out_specs=[pl.BlockSpec(memory_space=V)] * len(outs),
        scratch_shapes=scratch,
        compiler_params=pltpu.CompilerParams(
            collective_id=0, has_side_effects=True, vmem_limit_bytes=40 * 1024 * 1024
        ),
    )(*[pltpu.with_memory_space_constraint(a, pltpu.HBM) for a in args])
    return tuple(
        pl.pallas_call(
            write_kernel,
            out_shape=shapes,
            in_specs=[pl.BlockSpec(memory_space=V)] * len(outs),
            out_specs=[pl.BlockSpec(memory_space=pltpu.HBM)] * len(outs),
            scratch_shapes=[DMA((4 * len(outs),))],
            compiler_params=pltpu.CompilerParams(vmem_limit_bytes=1024 * 1024),
        )(*found)
    )


def solution(mesh):
    cube, plane = P(None, "trow", "tcol"), P("trow", "tcol")
    in_specs = (cube,) * 6 + (plane,) * 2 + (cube,) * 2 + (plane,)
    out_specs = (cube,) * 3 + (plane,)
    return jax.shard_map(shards, mesh=mesh, in_specs=in_specs, out_specs=out_specs, check_vma=False)
```

```python
import functools
import jax
import jax.numpy as jnp
from jax import lax
from jax.experimental import pallas as pl
from jax.experimental.pallas import tpu as pltpu
from jax.sharding import PartitionSpec as P

ITERS = 4
LANES = 128
RIM = 8
LOW, HIGH = 0.2, 9.2
CENTRE, RADIUS = (HIGH + LOW) / 2, (HIGH - LOW) / 2
MESH = pl.DeviceIdType.MESH
F32 = jnp.float32


def put(out, k, value):
    out[k] = value if out[k] is None else out[k] + value


def times_operator(poly):
    out = [None] * (len(poly) + 1)
    for k, c in enumerate(poly):
        put(out, k, CENTRE * c)
        if k == 0:
            put(out, 1, RADIUS * c)
        else:
            half = (0.5 * RADIUS) * c
            put(out, k + 1, half)
            put(out, k - 1, half)
    return out


def inner(p, q, table):
    total = None
    for i, a in enumerate(p):
        part = None
        for j, b in enumerate(q):
            term = b * table[i][j]
            part = term if part is None else part + term
        part = a * part
        total = part if total is None else total + part
    return total


def add_scaled(p, scale, q):
    out = []
    for k in range(max(len(p), len(q))):
        if k >= len(p):
            out.append(scale * q[k])
        elif k >= len(q):
            out.append(p[k])
        else:
            out.append(p[k] + scale * q[k])
    return out


def weights_from(moments):
    table = [
        [
            moments[j] if i == 0 else moments[i] if j == 0 else 0.5 * (moments[i + j] + moments[abs(i - j)])
            for j in range(ITERS + 1)
        ]
        for i in range(ITERS)
    ]
    residual = [jnp.ones_like(moments[0])]
    direction = residual
    result = []
    norm_now = moments[0]
    for iteration in range(ITERS):
        image = times_operator(direction)
        step = norm_now / inner(direction, image, table)
        result = add_scaled(result, step, direction)
        if iteration + 1 < ITERS:
            residual = add_scaled(residual, -step, image)
            norm_next = inner(residual, residual, table)
            direction = add_scaled(residual, norm_next / norm_now, direction)
            norm_now = norm_next
    return result


def lane_index(rows):
    return lax.broadcasted_iota(jnp.int32, (rows, LANES), 1)


def roll(x, amount):
    return pltpu.roll(x, amount % LANES if isinstance(amount, int) else amount & (LANES - 1), 1)


def shifted(parts, ends, by, lane):
    if by > 0:
        joined = [jnp.where(lane < by, nearby, p) for p, nearby in zip(parts, parts[1:] + [ends])]
    else:
        joined = [jnp.where(lane >= LANES + by, nearby, p) for p, nearby in zip(parts, [ends] + parts[:-1])]
    return [roll(p, -by) for p in joined]


GROUP = 5


def by_groups(start, stop, group, body, carry):
    count = (stop - start) // group
    carry = lax.fori_loop(0, count, lambda i, c: body([start + i * group + u for u in range(group)], c), carry)
    rest = list(range(start + count * group, stop))
    return body(rest, carry) if rest else carry


def signed_sum(terms):
    return terms[0] + (((terms[1] + terms[2]) - (terms[5] + terms[6])) + ((terms[3] + terms[4]) - (terms[7] + terms[8])))


def guarded(condition, action):
    @pl.when(condition)
    def _():
        action()


def solve_kernel(
    sizes,
    theta_in, salt_in, vx_in, vy_in, land_in, kappa_in, forcing_in, bottom_in, theta_cot_in, salt_cot_in, surface_in,
    theta_grad, salt_grad, kappa_grad, forcing_grad, second, cross, zeta, ends,
    theta, salt, vx, vy, land, kappa, forcing, theta_cot, salt_cot,
    surface, bottom, wet, wet_after, face_x, first, open_y, inverse, link, ratio, theta_mix, salt_mix,
    seam_own, seam_left, seam_right, slots, k_fixed, k_zeta,
    local_sem, rim_send, rim_recv, halo_send, halo_recv, sum_send, sum_recv,
):
    depth, rows, cols = sizes
    halves = cols // LANES
    top, end = RIM, RIM + rows
    mesh_rows, mesh_cols = lax.axis_size("trow"), lax.axis_size("tcol")
    count = mesh_rows * mesh_cols
    row, col = lax.axis_index("trow"), lax.axis_index("tcol")
    has_before, has_after = row > 0, row < mesh_rows - 1
    has_left, has_right = col > 0, col < mesh_cols - 1
    lane = lane_index(rows)
    spot = ((lane + 2) & 3) - 2
    blank = jnp.zeros((rows, LANES), F32)
    span = range(halves)

    chunks = depth // GROUP

    def at(f, h, k):
        return (k * 3 + f) * halves + h

    def at_first(f, h, k):
        return (k * 2 + f) * halves + h

    surface[...] = jnp.zeros_like(surface)
    bottom[...] = jnp.zeros_like(bottom)
    seam_left[...] = jnp.zeros_like(seam_left)
    seam_right[...] = jnp.zeros_like(seam_right)

    barrier = pltpu.get_barrier_semaphore()

    def others(action):
        for dc in range(1, mesh_cols):
            action(dc, (row, lax.rem(col + dc, mesh_cols)))

        def one_row(dr, carry):
            there = lax.rem(row + dr, mesh_rows)
            for dc in range(mesh_cols):
                action(dr * mesh_cols + dc, (there, lax.rem(col + dc, mesh_cols)))
            return carry

        lax.fori_loop(1, mesh_rows, one_row, 0)

    others(lambda i, device: pl.semaphore_signal(barrier, inc=1, device_id=device, device_id_type=MESH))

    started = []

    def fetch(src, dst):
        copy = pltpu.make_async_copy(src, dst, local_sem.at[len(started)])
        copy.start()
        started.append(copy)
        return copy

    middle = pl.ds(LANES, cols)
    get_surface = fetch(surface_in, surface.at[pl.ds(RIM, rows), middle])
    get_bottom = fetch(bottom_in, bottom.at[pl.ds(RIM, rows), middle])

    def fetch_halves(src, dst):
        return [
            fetch(src.at[:, :, pl.ds(h * LANES, LANES)], dst.at[pl.ds(h * src.shape[0], src.shape[0])]) for h in span
        ]

    get_land = fetch_halves(land_in, land)
    get_theta = fetch_halves(theta_in, theta)
    get_salt = fetch_halves(salt_in, salt)
    get_vx = fetch_halves(vx_in, vx)
    get_vy = fetch_halves(vy_in, vy)
    get_forcing = fetch(forcing_in, forcing)
    get_kappa = fetch_halves(kappa_in, kappa)
    get_theta_cot = fetch_halves(theta_cot_in, theta_cot)
    get_salt_cot = fetch_halves(salt_cot_in, salt_cot)

    def arrived(copies):
        for copy in copies:
            copy.wait()

    arrived([get_bottom] + get_land)

    def wet_levels(levels, carry):
        for k in levels:
            for h in span:
                depth_here = bottom[top:end, LANES * (h + 1) : LANES * (h + 2)]
                wet[h * depth + k, 0:rows] = jnp.where(k < depth_here, land[h * depth + k].astype(F32), 0.0)
                wet[h * depth + k, rows : rows + RIM] = jnp.ones((RIM, LANES), F32)
        return carry

    by_groups(0, depth, 5, wet_levels, 0)

    def wet_at(h, k):
        return wet[h * depth + k, 0:rows]

    arrived(get_theta + get_salt + get_vx + get_vy)

    def pack(k, parts, packed):
        both = jnp.where(lane < LANES // 2, parts[0], parts[-1])
        here = ((lane + 2 - 4 * k) & (LANES - 1)) < 4
        return jnp.where(here, roll(both, 4 * k), packed)

    def prepare(levels, packs):
        for k in levels:
            wets = [wet_at(h, k) for h in span]
            qt, qs, uy = [], [], []
            for h in span:
                i = h * depth + k
                qt.append(theta[i] * wets[h])
                qs.append(salt[i] * wets[h])
                uy.append(vy[i])
                first[at_first(0, h, k), top:end] = qt[h]
                first[at_first(1, h, k), top:end] = qs[h]
                face_x[i, top:end] = vx[i] * wets[h] * wet[i, 1 : rows + 1] * (1.0 / 12.0)
            packs = tuple(pack(k, parts, packed) for parts, packed in zip((qt, qs, uy, wets), packs))
        return packs

    for f, packed in enumerate(by_groups(0, depth, 5, prepare, (blank,) * 4)):
        seam_own[f] = packed

    pl.semaphore_wait(barrier, count - 1)

    rims = []
    for dr in (-1, 0, 1):
        for dc in (-1, 0, 1):
            if dr == 0 and dc == 0:
                continue
            targets = [has_before] * (dr < 0) + [has_after] * (dr > 0) + [has_left] * (dc < 0) + [has_right] * (dc > 0)
            sources = [has_after] * (dr < 0) + [has_before] * (dr > 0) + [has_right] * (dc < 0) + [has_left] * (dc > 0)
            src_rows = pl.ds(0, RIM) if dr < 0 else pl.ds(rows - RIM, RIM) if dr > 0 else pl.ds(0, rows)
            src_cols = pl.ds(0, LANES) if dc < 0 else pl.ds(cols - LANES, LANES) if dc > 0 else pl.ds(0, cols)
            dst_rows = pl.ds(end, RIM) if dr < 0 else pl.ds(0, RIM) if dr > 0 else pl.ds(top, rows)
            dst_cols = pl.ds(LANES + cols, LANES) if dc < 0 else pl.ds(0, LANES) if dc > 0 else middle
            for src, dst in ((surface_in, surface), (bottom_in, bottom)):
                i = len(rims)
                copy = pltpu.make_async_remote_copy(
                    src_ref=src.at[src_rows, src_cols],
                    dst_ref=dst.at[dst_rows, dst_cols],
                    send_sem=rim_send.at[i],
                    recv_sem=rim_recv.at[i],
                    device_id=(row + dr, col + dc),
                    device_id_type=MESH,
                )
                rims.append((copy, functools.reduce(jnp.logical_and, targets), functools.reduce(jnp.logical_and, sources)))
    for copy, sends, _ in rims:
        guarded(sends, copy.start)

    def remote(src, dst, i, device):
        return pltpu.make_async_remote_copy(
            src_ref=src, dst_ref=dst, send_sem=halo_send.at[i], recv_sem=halo_recv.at[i], device_id=device, device_id_type=MESH
        )

    after, before = (row + 1, col), (row - 1, col)
    right, left = (row, col + 1), (row, col - 1)
    def row_copies(ref, base, g):
        per_chunk = ref.shape[0] // chunks
        part = pl.ds(g * per_chunk, per_chunk)
        return [
            (remote(ref.at[part, pl.ds(end - 2, 2)], ref.at[part, pl.ds(top - 2, 2)], base + g, after), has_after, has_before),
            (remote(ref.at[part, pl.ds(top, 2)], ref.at[part, pl.ds(end, 2)], base + chunks + g, before), has_before, has_after),
        ]

    def edge_copies(first_field, fields, base):
        part = pl.ds(first_field, fields)
        return [
            (remote(seam_own.at[part], seam_left.at[part], base, right), has_right, has_left),
            (remote(seam_own.at[part], seam_right.at[part], base + 1, left), has_left, has_right),
        ]

    def send_rows(ref, base):
        for g in range(chunks):
            for copy, sends, _ in row_copies(ref, base, g):
                guarded(sends, copy.start)

    edges_one, edges_two = edge_copies(0, 4, 0), edge_copies(4, 3, 2)
    wet_copy = remote(wet.at[:, pl.ds(0, 1)], wet_after.at[:, pl.ds(0, 1)], 4, before)
    faces_down = remote(face_x.at[:, pl.ds(end - 2, 2)], face_x.at[:, pl.ds(top - 2, 2)], 5, after)
    faces_up = remote(face_x.at[:, pl.ds(top, 1)], face_x.at[:, pl.ds(end, 1)], 6, before)
    early = [(wet_copy, has_before, has_after), (faces_down, has_after, has_before), (faces_up, has_before, has_after)]
    rows_one, rows_two = 7, 7 + 2 * chunks
    for copy, sends, _ in edges_one + early:
        guarded(sends, copy.start)
    send_rows(first, rows_one)

    def clear(missing, ref, start):
        @pl.when(missing)
        def _():
            ref[:, start : start + 2] = jnp.zeros((ref.shape[0], 2, LANES), F32)

    for ref in (face_x, first, second):
        clear(jnp.logical_not(has_before), ref, top - 2)
        clear(jnp.logical_not(has_after), ref, end)
    clear(jnp.logical_not(has_after), wet_after, 0)

    arrived(get_kappa + get_theta_cot + get_salt_cot)

    def down_level(k, last, carry):
        out = []
        for h in span:
            num, den, couple_before, yt, ys, yw = carry[h]
            i = h * depth + k
            wet_here = wet_at(h, k)
            if last:
                den_next = num_next = num
                couple = couple_before
            else:
                couple = kappa[h * (depth - 1) + k] * wet_here * wet_at(h, k + 1)
                den_next = num + couple * den
                num_next = den_next + couple * num
            inv = den * (1.0 / den_next)
            lower = couple_before * inv
            inverse[i] = inv
            link[i] = lower
            if not last:
                ratio[i] = couple * inv
            yt = theta_cot[i] * inv + lower * yt
            ys = salt_cot[i] * inv + lower * ys
            yw = wet_here * inv + lower * yw
            second[at(0, h, k), top:end] = yt
            second[at(1, h, k), top:end] = ys
            second[at(2, h, k), top:end] = yw
            out.append((num_next, den_next, couple, yt, ys, yw))
        return tuple(out)

    def down(levels, carry):
        for k in levels:
            carry = down_level(k, False, carry)
        return carry

    one = jnp.ones((rows, LANES), F32)
    carry = by_groups(0, depth - 1, 4, down, ((one, one, blank, blank, blank, blank),) * halves)
    carry = down_level(depth - 1, True, carry)

    def up(steps, values):
        for n in steps:
            k = depth - 2 - n
            new = []
            for f in range(3):
                parts = []
                for h in span:
                    x = second[at(f, h, k), top:end] + ratio[h * depth + k] * values[f][h]
                    second[at(f, h, k), top:end] = x
                    parts.append(x)
                new.append(tuple(parts))
            values = tuple(new)
        return values

    by_groups(0, depth - 1, 4, up, tuple(tuple(carry[h][3 + f] for h in span) for f in range(3)))

    def pack_second(levels, packs):
        for k in levels:
            packs = tuple(pack(k, [second[at(f, h, k), top:end] for h in span], packs[f]) for f in range(3))
        return packs

    for f, packed in enumerate(by_groups(0, depth, depth, pack_second, (blank,) * 3)):
        seam_own[4 + f] = packed
    get_surface.wait()
    for copy, _, receives in rims:
        guarded(receives, copy.wait_recv)
    wide = (rows + 2 * RIM, cols + 2 * LANES)
    row_at = lax.broadcasted_iota(jnp.int32, wide, 0) - RIM + row * rows
    col_at = lax.broadcasted_iota(jnp.int32, wide, 1) - LANES + col * cols
    inside = ((row_at >= 0) & (row_at < rows * mesh_rows)) & ((col_at >= 0) & (col_at < cols * mesh_cols))
    scaled = (bottom[...].astype(F32) * (1.0 / depth) + (4.2 - CENTRE)) * (1.0 / RADIUS)
    basis = [surface[...]]
    for k in range(ITERS):
        field = basis[-1]
        beside = (pltpu.roll(field, 1, 0) + pltpu.roll(field, wide[0] - 1, 0)) + (
            pltpu.roll(field, 1, 1) + pltpu.roll(field, wide[1] - 1, 1)
        )
        image = scaled * field - beside * (1.0 / RADIUS)
        if k > 0:
            image = 2.0 * image - basis[-2]
        basis.append(jnp.where(inside, image, 0.0))

    def own_product(a, b):
        product = basis[a][top:end, LANES : LANES + cols] * basis[b][top:end, LANES : LANES + cols]
        tiles = [product[i : i + 8, j : j + LANES] for i in range(0, rows, 8) for j in range(0, cols, LANES)]
        return functools.reduce(jnp.add, tiles)

    partial = [own_product(a, b) for a, b in ((0, 0), (0, 1), (0, 2), (0, 3), (0, 4), (2, 3), (3, 3), (3, 4))]
    place = lax.broadcasted_iota(jnp.int32, (8, LANES), 0)
    stacked = jnp.zeros((8, LANES), F32)
    for g, p in enumerate(partial):
        stacked = jnp.where(place == g, jnp.sum(p, axis=0, keepdims=True), stacked)
    stacked = jnp.broadcast_to(jnp.sum(stacked, axis=1, keepdims=True), (8, LANES))
    mine = jnp.where((lane_index(8) >> 4) == place, stacked, 0.0)
    slots[0:1] = jnp.sum(mine, axis=0, keepdims=True)

    def sum_copy(i, device):
        return pltpu.make_async_remote_copy(
            src_ref=slots.at[pl.ds(0, 1)],
            dst_ref=slots.at[pl.ds(i, 1)],
            send_sem=sum_send.at[i],
            recv_sem=sum_recv.at[i],
            device_id=device,
            device_id_type=MESH,
        )

    others(lambda i, device: sum_copy(i, device).start())
    for k in range(ITERS):
        for h in range(halves + 2):
            zeta[k * (halves + 2) + h] = basis[k][:, h * LANES : (h + 1) * LANES]

    for copy, sends, _ in edges_two:
        guarded(sends, copy.start)
    send_rows(second, rows_two)

    for copy, sends, receives in edges_one:
        guarded(sends, copy.wait_send)
        guarded(receives, copy.wait_recv)

    def open_across(uy, near):
        return uy * near * roll(near, -1) * (1.0 / 12.0)

    inner_side = spot < 0
    open_left = open_across(seam_left[2], jnp.where(inner_side, seam_left[3], seam_own[3]))
    open_right = open_across(seam_right[2], seam_right[3])

    def unpack(fields):
        def one_group(levels, carry):
            for k in levels:
                for f, packed in fields:
                    ends[f * depth + k] = roll(packed, LANES - 4 * k)
            return carry

        by_groups(0, depth, depth, one_group, 0)

    def both_sides(f):
        return jnp.where(inner_side, seam_left[f], seam_right[f])

    unpack([(0, both_sides(0)), (1, both_sides(1)), (2, jnp.where(inner_side, open_left, open_right)), (3, both_sides(3))])

    def open_columns(levels, carry):
        ahead = [shifted([wet_at(h, k) for h in span], ends[3 * depth + k], 1, lane) for k in levels]
        for k, wets_ahead in zip(levels, ahead):
            for h in span:
                i = h * depth + k
                open_y[i] = vy[i] * wet_at(h, k) * wets_ahead[h] * (1.0 / 12.0)
        return carry

    by_groups(0, depth, depth, open_columns, 0)
    get_forcing.wait()
    for h in span:
        theta[h * depth] = theta[h * depth] + forcing[:, h * LANES : (h + 1) * LANES] * wet_at(h, 0)

    def column_shifts(ref, where, f, k, beyond):
        centre = [ref[where(f, h, k), top:end] for h in span]
        return {s: shifted(centre, ends[beyond * depth + k], s, lane) for s in (-2, -1, 1, 2)}

    def face_shifts(k, steps):
        centre = [open_y[h * depth + k] for h in span]
        return {s: shifted(centre, ends[2 * depth + k], s, lane) for s in steps}

    def got_rows(ref, base, levels, sent_too):
        for copy, sends, receives in row_copies(ref, base, levels[0] // GROUP if isinstance(levels[0], int) else lax.div(levels[0], GROUP)):
            if sent_too:
                guarded(sends, copy.wait_send)
            guarded(receives, copy.wait_recv)

    def arms(u, wets):
        v = [wets * x for x in u]
        back, here = 7.0 * v[1], 7.0 * v[2]
        return v[0], back + v[0], back - here, here + v[3], v[3]

    for copy, sends, receives in early:
        guarded(sends, copy.wait_send)
        guarded(receives, copy.wait_recv)

    def coefficients(levels, carry):
        for k in levels:
            for h in span:
                i = h * depth + k
                face_x[i, top - 1 : top] = face_x[i, top - 1 : top] * wet[i, 0:1]
                face_x[i, end - 1 : end] = face_x[i, end - 1 : end] * wet_after[i, 0:1]
        moved = [face_shifts(k, (-2, -1, 1)) for k in levels]
        for k, uy in zip(levels, moved):
            for h in span:
                i = h * depth + k
                wets = wet_at(h, k)
                r = arms([face_x[i, top + s : end + s] for s in (-2, -1, 0, 1)], wets)
                c = arms([uy[-2][h], uy[-1][h], open_y[i], uy[1][h]], wets)
                for n, w in enumerate([(1.0 + r[2]) + c[2], r[0], r[3], c[0], c[3], r[1], r[4], c[1], c[4]]):
                    cross[9 * i + n] = w
        return carry

    by_groups(0, depth, depth, coefficients, 0)

    def forward_down(levels, carry):
        moved = [
            (face_shifts(k, (-1,)), [column_shifts(first, at_first, f, k, f) for f in range(2)]) for k in levels
        ]
        for k, (uy, turned) in zip(levels, moved):
            out = []
            for h in span:
                i = h * depth + k
                found = []
                for f, raw in ((0, theta), (1, salt)):
                    q = [first[at_first(f, h, k), top + s : end + s] for s in (-2, -1, 0, 1, 2)]
                    c = turned[f]
                    row_here = face_x[i, top:end] * (7.0 * (q[2] + q[3]) - (q[1] + q[4]))
                    row_back = face_x[i, top - 1 : end - 1] * (7.0 * (q[1] + q[2]) - (q[0] + q[3]))
                    col_here = open_y[i] * (7.0 * (q[2] + c[1][h]) - (c[-1][h] + c[2][h]))
                    col_back = uy[-1][h] * (7.0 * (c[-1][h] + q[2]) - (c[-2][h] + c[1][h]))
                    value = raw[i] - (row_here - row_back) - (col_here - col_back)
                    found.append(value * inverse[i] + link[i] * carry[h][f])
                theta_mix[i] = found[0]
                salt_mix[i] = found[1]
                out.append(tuple(found))
            carry = tuple(out)
        return carry

    for g in range(chunks):
        got_rows(first, rows_one, [g * GROUP], True)
    carry = by_groups(0, depth, 25, forward_down, ((blank, blank),) * halves)

    def forward_up(steps, carry):
        for n in steps:
            k = depth - 2 - n
            out = []
            for h in span:
                i = h * depth + k
                xt = theta_mix[i] + ratio[i] * carry[h][0]
                xs = salt_mix[i] + ratio[i] * carry[h][1]
                dt, ds = xt - carry[h][0], xs - carry[h][1]
                step_t, step_s, step_w = [
                    second[at(f, h, k), top:end] - second[at(f, h, k + 1), top:end] for f in range(3)
                ]
                closed = -wet_at(h, k) * wet_at(h, k + 1)
                k_fixed[h * (depth - 1) + k] = closed * (step_t * dt + step_s * ds)
                k_zeta[h * (depth - 1) + k] = closed * step_w * (0.2 * dt - 0.15 * ds)
                out.append((xt, xs))
            carry = tuple(out)
        return carry

    by_groups(0, depth - 1, 4, forward_up, carry)

    others(lambda i, device: sum_copy(i, device).wait_recv())
    total = jnp.broadcast_to(jnp.sum(slots[...], axis=0, keepdims=True), (8, LANES))
    m = [jnp.broadcast_to(total[:, 16 * g : 16 * g + 1], (8, LANES)) for g in range(8)]
    m = m[:5] + [2.0 * m[5] - m[1], 2.0 * m[6] - m[0], 2.0 * m[7] - m[1]]
    weights = [jnp.concatenate([w] * (wide[0] // 8), axis=0) for w in weights_from(m)]
    tiles = halves + 2
    for h in range(tiles):
        b = [zeta[k * tiles + h] for k in range(ITERS)]
        zeta[h] = (weights[0] * b[0] + weights[1] * b[1]) + (weights[2] * b[2] + weights[3] * b[3])

    for copy, sends, receives in edges_two:
        guarded(sends, copy.wait_send)
        guarded(receives, copy.wait_recv)
    beyond = jnp.where(lane >= LANES // 2, zeta[0, top:end], zeta[tiles - 1, top:end])
    far_t, far_s, far_w = both_sides(4), both_sides(5), both_sides(6)

    def unpack_mu(levels, carry):
        for k in levels:
            turned = [roll(p, LANES - 4 * k) for p in (far_t, far_s, far_w)]
            lifted = turned[2] * beyond
            ends[4 * depth + k] = turned[0] + 0.2 * lifted
            ends[5 * depth + k] = turned[1] - 0.15 * lifted
        return carry

    by_groups(0, depth, depth, unpack_mu, 0)

    def finish(levels, carry):
        got_rows(second, rows_two, levels, True)
        for k in levels:
            for h in span:
                area = pl.ds(top - 2, rows + 8)
                lifted = second[at(2, h, k), area] * zeta[h + 1, area]
                second[at(0, h, k), area] = second[at(0, h, k), area] + 0.2 * lifted
                second[at(1, h, k), area] = second[at(1, h, k), area] - 0.15 * lifted
        moved = [[column_shifts(second, at, f, k, 4 + f) for f in range(2)] for k in levels]
        for k, turned in zip(levels, moved):
            for h in span:
                i = h * depth + k
                where = slice(h * LANES, (h + 1) * LANES)
                for f, out in ((0, theta_grad), (1, salt_grad)):
                    values = [second[at(f, h, k), top + s : end + s] for s in (0, -2, 1)]
                    values += [turned[f][s][h] for s in (-2, 1)]
                    values += [second[at(f, h, k), top + s : end + s] for s in (-1, 2)]
                    values += [turned[f][s][h] for s in (-1, 2)]
                    out[k, :, where] = signed_sum([cross[9 * i + n] * v for n, v in enumerate(values)])
        return carry

    by_groups(0, theta_grad.shape[0], GROUP, finish, 0)

    def finish_kappa(levels, carry):
        for k in levels:
            for h in span:
                j = h * (depth - 1) + k
                kappa_grad[k, :, h * LANES : (h + 1) * LANES] = k_fixed[j] + k_zeta[j] * zeta[h + 1, top:end]
        return carry

    by_groups(0, depth - 1, 4, finish_kappa, 0)
    for h in span:
        forcing_grad[:, h * LANES : (h + 1) * LANES] = zeta[h + 1, top:end] + wet_at(h, 0) * second[at(0, h, 0), top:end]

    for g in range(theta_grad.shape[0] // GROUP, chunks):
        got_rows(second, rows_two, [g * GROUP], True)
    for copy, sends, _ in rims:
        guarded(sends, copy.wait_send)
    others(lambda i, device: sum_copy(i, device).wait_send())


def finish_kernel(
    sizes,
    theta_done, salt_done, kappa_done, forcing_done, second, cross, zeta, ends,
    theta_out, salt_out, kappa_out, forcing_out,
    mu, theta_grad, salt_grad, sems,
):
    depth, rows, cols = sizes
    halves = cols // LANES
    top, end = RIM, RIM + rows
    span = range(halves)
    lane = lane_index(rows)
    area = pl.ds(top - 2, rows + 8)
    split = theta_done.shape[0]
    copies = []

    def put(src, dst):
        copy = pltpu.make_async_copy(src, dst, sems.at[len(copies)])
        copy.start()
        copies.append(copy)

    put(theta_done, theta_out.at[pl.ds(0, split)])
    put(salt_done, salt_out.at[pl.ds(0, split)])
    put(kappa_done, kappa_out)
    put(forcing_done, forcing_out)

    def at(f, h, k):
        return (k * 3 + f) * halves + h

    def mu_at(f, h, k):
        return ((k - split) * 2 + f) * halves + h

    def column_shifts(f, k):
        centre = [mu[mu_at(f, h, k), top:end] for h in span]
        return {s: shifted(centre, ends[(4 + f) * depth + k], s, lane) for s in (-2, -1, 1, 2)}

    for first in range(split, depth, GROUP):
        levels = range(first, min(depth, first + GROUP))
        for k in levels:
            for h in span:
                lifted = second[at(2, h, k), area] * zeta[h + 1, area]
                mu[mu_at(0, h, k), area] = second[at(0, h, k), area] + 0.2 * lifted
                mu[mu_at(1, h, k), area] = second[at(1, h, k), area] - 0.15 * lifted
        moved = [[column_shifts(f, k) for f in range(2)] for k in levels]
        for k, turned in zip(levels, moved):
            for h in span:
                i = h * depth + k
                where = slice(h * LANES, (h + 1) * LANES)
                for f, out in ((0, theta_grad), (1, salt_grad)):
                    values = [mu[mu_at(f, h, k), top + s : end + s] for s in (0, -2, 1)]
                    values += [turned[f][s][h] for s in (-2, 1)]
                    values += [mu[mu_at(f, h, k), top + s : end + s] for s in (-1, 2)]
                    values += [turned[f][s][h] for s in (-1, 2)]
                    out[k - split, :, where] = signed_sum([cross[9 * i + n] * v for n, v in enumerate(values)])
        here, there = pl.ds(first - split, len(levels)), pl.ds(first, len(levels))
        put(theta_grad.at[here], theta_out.at[there])
        put(salt_grad.at[here], salt_out.at[there])
    for copy in copies:
        copy.wait()


def shards(*args):
    theta = args[0]
    depth, rows, cols = theta.shape
    halves = cols // LANES
    count = lax.axis_size("trow") * lax.axis_size("tcol")
    tall = rows + 2 * RIM
    V = pltpu.VMEM
    DMA = pltpu.SemaphoreType.DMA
    flat = V((halves * depth, rows, LANES), F32)
    ints = V((halves * depth, rows, LANES), jnp.int32)
    upper = V((halves * (depth - 1), rows, LANES), F32)
    tile = V((7, rows, LANES), F32)
    halo = DMA((7 + 4 * (depth // GROUP),))
    scratch = [
        flat, flat, flat, flat, ints, upper, V((rows, cols), F32), flat, flat,
        V((tall, cols + 2 * LANES), F32), V((tall, cols + 2 * LANES), jnp.int32),
        V((halves * depth, rows + RIM, LANES), F32), V((halves * depth, RIM, LANES), F32),
        V((halves * depth, tall, LANES), F32), V((2 * halves * depth, tall, LANES), F32),
        flat, flat, flat, flat, flat, flat,
        tile, tile, tile, V((count, LANES), F32), upper, upper,
        DMA((3 + 8 * halves,)), DMA((16,)), DMA((16,)), halo, halo, DMA((count,)), DMA((count,)),
    ]
    outs = [(depth, rows, cols), (depth, rows, cols), (depth - 1, rows, cols), (rows, cols)]
    split = depth // GROUP * 3 // 5 * GROUP
    parts = [
        (split, rows, cols), (split, rows, cols), outs[2], outs[3], (3 * halves * depth, tall, LANES),
        (9 * halves * depth, rows, LANES), (ITERS * (halves + 2), tall, LANES), (7 * depth, rows, LANES),
    ]
    found = pl.pallas_call(
        functools.partial(solve_kernel, (depth, rows, cols)),
        out_shape=[jax.ShapeDtypeStruct(o, F32) for o in parts],
        in_specs=[pl.BlockSpec(memory_space=pltpu.HBM)] * len(args),
        out_specs=[pl.BlockSpec(memory_space=V)] * len(parts),
        scratch_shapes=scratch,
        compiler_params=pltpu.CompilerParams(
            collective_id=0, has_side_effects=True, vmem_limit_bytes=32 * 1024 * 1024
        ),
    )(*[pltpu.with_memory_space_constraint(a, pltpu.HBM) for a in args])
    left = (depth - split, rows, cols)
    return tuple(
        pl.pallas_call(
            functools.partial(finish_kernel, (depth, rows, cols)),
            out_shape=[jax.ShapeDtypeStruct(o, F32) for o in outs],
            in_specs=[pl.BlockSpec(memory_space=V)] * len(parts),
            out_specs=[pl.BlockSpec(memory_space=pltpu.HBM)] * len(outs),
            scratch_shapes=[V((2 * halves * left[0], tall, LANES), F32), V(left, F32), V(left, F32)]
            + [DMA((4 + 2 * (left[0] // GROUP + 1),))],
            compiler_params=pltpu.CompilerParams(vmem_limit_bytes=8 * 1024 * 1024),
        )(*found)
    )


def solution(mesh):
    cube, plane = P(None, "trow", "tcol"), P("trow", "tcol")
    in_specs = (cube,) * 6 + (plane,) * 2 + (cube,) * 2 + (plane,)
    out_specs = (cube,) * 3 + (plane,)
    return jax.shard_map(shards, mesh=mesh, in_specs=in_specs, out_specs=out_specs, check_vma=False)
```

```python
import functools
import jax
import jax.numpy as jnp
from jax import lax
from jax.experimental import pallas as pl
from jax.experimental.pallas import tpu as pltpu
from jax.sharding import PartitionSpec as P

ITERS = 4
LANES = 128
RIM = 8
LOW, HIGH = 0.2, 9.2
CENTRE, RADIUS = (HIGH + LOW) / 2, (HIGH - LOW) / 2
MESH = pl.DeviceIdType.MESH
F32 = jnp.float32


def put(out, k, value):
    out[k] = value if out[k] is None else out[k] + value


def times_operator(poly):
    out = [None] * (len(poly) + 1)
    for k, c in enumerate(poly):
        put(out, k, CENTRE * c)
        if k == 0:
            put(out, 1, RADIUS * c)
        else:
            half = (0.5 * RADIUS) * c
            put(out, k + 1, half)
            put(out, k - 1, half)
    return out


def inner(p, q, table):
    total = None
    for i, a in enumerate(p):
        part = None
        for j, b in enumerate(q):
            term = b * table[i][j]
            part = term if part is None else part + term
        part = a * part
        total = part if total is None else total + part
    return total


def add_scaled(p, scale, q):
    out = []
    for k in range(max(len(p), len(q))):
        if k >= len(p):
            out.append(scale * q[k])
        elif k >= len(q):
            out.append(p[k])
        else:
            out.append(p[k] + scale * q[k])
    return out


def weights_from(moments):
    table = [
        [
            moments[j] if i == 0 else moments[i] if j == 0 else 0.5 * (moments[i + j] + moments[abs(i - j)])
            for j in range(ITERS + 1)
        ]
        for i in range(ITERS)
    ]
    residual = [jnp.ones_like(moments[0])]
    direction = residual
    result = []
    norm_now = moments[0]
    for iteration in range(ITERS):
        image = times_operator(direction)
        step = norm_now / inner(direction, image, table)
        result = add_scaled(result, step, direction)
        if iteration + 1 < ITERS:
            residual = add_scaled(residual, -step, image)
            norm_next = inner(residual, residual, table)
            direction = add_scaled(residual, norm_next / norm_now, direction)
            norm_now = norm_next
    return result


def lane_index(rows):
    return lax.broadcasted_iota(jnp.int32, (rows, LANES), 1)


def roll(x, amount):
    return pltpu.roll(x, amount % LANES if isinstance(amount, int) else amount & (LANES - 1), 1)


def shifted(parts, ends, by, lane):
    if by > 0:
        joined = [jnp.where(lane < by, nearby, p) for p, nearby in zip(parts, parts[1:] + [ends])]
    else:
        joined = [jnp.where(lane >= LANES + by, nearby, p) for p, nearby in zip(parts, [ends] + parts[:-1])]
    return [roll(p, -by) for p in joined]


GROUP = 5


def by_groups(start, stop, group, body, carry):
    count = (stop - start) // group
    carry = lax.fori_loop(0, count, lambda i, c: body([start + i * group + u for u in range(group)], c), carry)
    rest = list(range(start + count * group, stop))
    return body(rest, carry) if rest else carry


def signed_sum(terms):
    return terms[0] + (((terms[1] + terms[2]) - (terms[5] + terms[6])) + ((terms[3] + terms[4]) - (terms[7] + terms[8])))


def guarded(condition, action):
    @pl.when(condition)
    def _():
        action()


def solve_kernel(
    sizes,
    theta_in, salt_in, vx_in, vy_in, land_in, kappa_in, forcing_in, bottom_in, theta_cot_in, salt_cot_in, surface_in,
    theta_grad, salt_grad, kappa_grad, forcing_grad, second, cross, zeta, ends,
    theta, salt, vx, vy, land, kappa, forcing, theta_cot, salt_cot,
    surface, bottom, wet, wet_after, face_x, first, open_y, inverse, link, ratio, theta_mix, salt_mix,
    seam_own, seam_left, seam_right, slots, k_fixed, k_zeta,
    local_sem, rim_send, rim_recv, halo_send, halo_recv, sum_send, sum_recv,
):
    depth, rows, cols = sizes
    halves = cols // LANES
    top, end = RIM, RIM + rows
    mesh_rows, mesh_cols = lax.axis_size("trow"), lax.axis_size("tcol")
    count = mesh_rows * mesh_cols
    row, col = lax.axis_index("trow"), lax.axis_index("tcol")
    has_before, has_after = row > 0, row < mesh_rows - 1
    has_left, has_right = col > 0, col < mesh_cols - 1
    lane = lane_index(rows)
    spot = ((lane + 2) & 3) - 2
    blank = jnp.zeros((rows, LANES), F32)
    span = range(halves)

    chunks = depth // GROUP

    def at(f, h, k):
        return (k * 3 + f) * halves + h

    def at_first(f, h, k):
        return (k * 2 + f) * halves + h

    surface[...] = jnp.zeros_like(surface)
    bottom[...] = jnp.zeros_like(bottom)
    seam_left[...] = jnp.zeros_like(seam_left)
    seam_right[...] = jnp.zeros_like(seam_right)

    barrier = pltpu.get_barrier_semaphore()

    def others(action):
        for dc in range(1, mesh_cols):
            action(dc, (row, lax.rem(col + dc, mesh_cols)))

        def one_row(dr, carry):
            there = lax.rem(row + dr, mesh_rows)
            for dc in range(mesh_cols):
                action(dr * mesh_cols + dc, (there, lax.rem(col + dc, mesh_cols)))
            return carry

        lax.fori_loop(1, mesh_rows, one_row, 0)

    def farthest_first(action):
        for dr in sorted(range(mesh_rows), key=lambda d: abs(2 * d - mesh_rows)):
            there = lax.rem(row + dr, mesh_rows)
            for dc in sorted(range(mesh_cols), key=lambda d: abs(2 * d - mesh_cols)):
                if dr or dc:
                    action(dr * mesh_cols + dc, (there, lax.rem(col + dc, mesh_cols)))

    farthest_first(lambda i, device: pl.semaphore_signal(barrier, inc=1, device_id=device, device_id_type=MESH))

    started = []

    def fetch(src, dst):
        copy = pltpu.make_async_copy(src, dst, local_sem.at[len(started)])
        copy.start()
        started.append(copy)
        return copy

    middle = pl.ds(LANES, cols)
    get_surface = fetch(surface_in, surface.at[pl.ds(RIM, rows), middle])
    get_bottom = fetch(bottom_in, bottom.at[pl.ds(RIM, rows), middle])

    def fetch_halves(src, dst):
        return [
            fetch(src.at[:, :, pl.ds(h * LANES, LANES)], dst.at[pl.ds(h * src.shape[0], src.shape[0])]) for h in span
        ]

    get_land = fetch_halves(land_in, land)
    get_theta = fetch_halves(theta_in, theta)
    get_salt = fetch_halves(salt_in, salt)
    get_vx = fetch_halves(vx_in, vx)
    get_vy = fetch_halves(vy_in, vy)
    get_forcing = fetch(forcing_in, forcing)
    get_kappa = fetch_halves(kappa_in, kappa)
    get_theta_cot = fetch_halves(theta_cot_in, theta_cot)
    get_salt_cot = fetch_halves(salt_cot_in, salt_cot)

    def arrived(copies):
        for copy in copies:
            copy.wait()

    arrived([get_bottom] + get_land)

    def wet_levels(levels, carry):
        for k in levels:
            for h in span:
                depth_here = bottom[top:end, LANES * (h + 1) : LANES * (h + 2)]
                wet[h * depth + k, 0:rows] = jnp.where(k < depth_here, land[h * depth + k].astype(F32), 0.0)
                wet[h * depth + k, rows : rows + RIM] = jnp.ones((RIM, LANES), F32)
        return carry

    by_groups(0, depth, 5, wet_levels, 0)

    def wet_at(h, k):
        return wet[h * depth + k, 0:rows]

    arrived(get_theta + get_salt + get_vx + get_vy)

    def pack(k, parts, packed):
        both = jnp.where(lane < LANES // 2, parts[0], parts[-1])
        here = ((lane + 2 - 4 * k) & (LANES - 1)) < 4
        return jnp.where(here, roll(both, 4 * k), packed)

    def prepare(levels, packs):
        for k in levels:
            wets = [wet_at(h, k) for h in span]
            qt, qs, uy = [], [], []
            for h in span:
                i = h * depth + k
                qt.append(theta[i] * wets[h])
                qs.append(salt[i] * wets[h])
                uy.append(vy[i])
                first[at_first(0, h, k), top:end] = qt[h]
                first[at_first(1, h, k), top:end] = qs[h]
                face_x[i, top:end] = vx[i] * wets[h] * wet[i, 1 : rows + 1] * (1.0 / 12.0)
            packs = tuple(pack(k, parts, packed) for parts, packed in zip((qt, qs, uy, wets), packs))
        return packs

    for f, packed in enumerate(by_groups(0, depth, 5, prepare, (blank,) * 4)):
        seam_own[f] = packed

    pl.semaphore_wait(barrier, count - 1)

    rims = []
    for dr in (-1, 0, 1):
        for dc in (-1, 0, 1):
            if dr == 0 and dc == 0:
                continue
            targets = [has_before] * (dr < 0) + [has_after] * (dr > 0) + [has_left] * (dc < 0) + [has_right] * (dc > 0)
            sources = [has_after] * (dr < 0) + [has_before] * (dr > 0) + [has_right] * (dc < 0) + [has_left] * (dc > 0)
            src_rows = pl.ds(0, RIM) if dr < 0 else pl.ds(rows - RIM, RIM) if dr > 0 else pl.ds(0, rows)
            src_cols = pl.ds(0, LANES) if dc < 0 else pl.ds(cols - LANES, LANES) if dc > 0 else pl.ds(0, cols)
            dst_rows = pl.ds(end, RIM) if dr < 0 else pl.ds(0, RIM) if dr > 0 else pl.ds(top, rows)
            dst_cols = pl.ds(LANES + cols, LANES) if dc < 0 else pl.ds(0, LANES) if dc > 0 else middle
            for src, dst in ((surface_in, surface), (bottom_in, bottom)):
                i = len(rims)
                copy = pltpu.make_async_remote_copy(
                    src_ref=src.at[src_rows, src_cols],
                    dst_ref=dst.at[dst_rows, dst_cols],
                    send_sem=rim_send.at[i],
                    recv_sem=rim_recv.at[i],
                    device_id=(row + dr, col + dc),
                    device_id_type=MESH,
                )
                rims.append((copy, functools.reduce(jnp.logical_and, targets), functools.reduce(jnp.logical_and, sources)))
    for copy, sends, _ in rims:
        guarded(sends, copy.start)

    def remote(src, dst, i, device):
        return pltpu.make_async_remote_copy(
            src_ref=src, dst_ref=dst, send_sem=halo_send.at[i], recv_sem=halo_recv.at[i], device_id=device, device_id_type=MESH
        )

    after, before = (row + 1, col), (row - 1, col)
    right, left = (row, col + 1), (row, col - 1)
    def row_copies(ref, base, g):
        per_chunk = ref.shape[0] // chunks
        part = pl.ds(g * per_chunk, per_chunk)
        return [
            (remote(ref.at[part, pl.ds(end - 2, 2)], ref.at[part, pl.ds(top - 2, 2)], base + g, after), has_after, has_before),
            (remote(ref.at[part, pl.ds(top, 2)], ref.at[part, pl.ds(end, 2)], base + chunks + g, before), has_before, has_after),
        ]

    def edge_copies(first_field, fields, base):
        part = pl.ds(first_field, fields)
        return [
            (remote(seam_own.at[part], seam_left.at[part], base, right), has_right, has_left),
            (remote(seam_own.at[part], seam_right.at[part], base + 1, left), has_left, has_right),
        ]

    def send_rows(ref, base):
        for g in range(chunks):
            for copy, sends, _ in row_copies(ref, base, g):
                guarded(sends, copy.start)

    edges_one, edges_two = edge_copies(0, 4, 0), edge_copies(4, 3, 2)
    wet_copy = remote(wet.at[:, pl.ds(0, 1)], wet_after.at[:, pl.ds(0, 1)], 4, before)
    faces_down = remote(face_x.at[:, pl.ds(end - 2, 2)], face_x.at[:, pl.ds(top - 2, 2)], 5, after)
    faces_up = remote(face_x.at[:, pl.ds(top, 1)], face_x.at[:, pl.ds(end, 1)], 6, before)
    early = [(wet_copy, has_before, has_after), (faces_down, has_after, has_before), (faces_up, has_before, has_after)]
    rows_one, rows_two = 7, 7 + 2 * chunks
    for copy, sends, _ in edges_one + early:
        guarded(sends, copy.start)
    send_rows(first, rows_one)

    def clear(missing, ref, start):
        @pl.when(missing)
        def _():
            ref[:, start : start + 2] = jnp.zeros((ref.shape[0], 2, LANES), F32)

    for ref in (face_x, first, second):
        clear(jnp.logical_not(has_before), ref, top - 2)
        clear(jnp.logical_not(has_after), ref, end)
    clear(jnp.logical_not(has_after), wet_after, 0)

    arrived(get_kappa + get_theta_cot + get_salt_cot)

    def down_level(k, last, carry):
        out = []
        for h in span:
            num, den, couple_before, yt, ys, yw = carry[h]
            i = h * depth + k
            wet_here = wet_at(h, k)
            if last:
                den_next = num_next = num
                couple = couple_before
            else:
                couple = kappa[h * (depth - 1) + k] * wet_here * wet_at(h, k + 1)
                den_next = num + couple * den
                num_next = den_next + couple * num
            inv = den * (1.0 / den_next)
            lower = couple_before * inv
            inverse[i] = inv
            link[i] = lower
            if not last:
                ratio[i] = couple * inv
            yt = theta_cot[i] * inv + lower * yt
            ys = salt_cot[i] * inv + lower * ys
            yw = wet_here * inv + lower * yw
            second[at(0, h, k), top:end] = yt
            second[at(1, h, k), top:end] = ys
            second[at(2, h, k), top:end] = yw
            out.append((num_next, den_next, couple, yt, ys, yw))
        return tuple(out)

    def down(levels, carry):
        for k in levels:
            carry = down_level(k, False, carry)
        return carry

    one = jnp.ones((rows, LANES), F32)
    carry = by_groups(0, depth - 1, 4, down, ((one, one, blank, blank, blank, blank),) * halves)
    carry = down_level(depth - 1, True, carry)

    def up(steps, values):
        for n in steps:
            k = depth - 2 - n
            new = []
            for f in range(3):
                parts = []
                for h in span:
                    x = second[at(f, h, k), top:end] + ratio[h * depth + k] * values[f][h]
                    second[at(f, h, k), top:end] = x
                    parts.append(x)
                new.append(tuple(parts))
            values = tuple(new)
        return values

    by_groups(0, depth - 1, 4, up, tuple(tuple(carry[h][3 + f] for h in span) for f in range(3)))

    def pack_second(levels, packs):
        for k in levels:
            packs = tuple(pack(k, [second[at(f, h, k), top:end] for h in span], packs[f]) for f in range(3))
        return packs

    for f, packed in enumerate(by_groups(0, depth, depth, pack_second, (blank,) * 3)):
        seam_own[4 + f] = packed
    get_surface.wait()
    for copy, _, receives in rims:
        guarded(receives, copy.wait_recv)
    wide = (rows + 2 * RIM, cols + 2 * LANES)
    row_at = lax.broadcasted_iota(jnp.int32, wide, 0) - RIM + row * rows
    col_at = lax.broadcasted_iota(jnp.int32, wide, 1) - LANES + col * cols
    inside = ((row_at >= 0) & (row_at < rows * mesh_rows)) & ((col_at >= 0) & (col_at < cols * mesh_cols))
    scaled = (bottom[...].astype(F32) * (1.0 / depth) + (4.2 - CENTRE)) * (1.0 / RADIUS)
    basis = [surface[...]]
    for k in range(ITERS):
        field = basis[-1]
        beside = (pltpu.roll(field, 1, 0) + pltpu.roll(field, wide[0] - 1, 0)) + (
            pltpu.roll(field, 1, 1) + pltpu.roll(field, wide[1] - 1, 1)
        )
        image = scaled * field - beside * (1.0 / RADIUS)
        if k > 0:
            image = 2.0 * image - basis[-2]
        basis.append(jnp.where(inside, image, 0.0))

    def own_product(a, b):
        product = basis[a][top:end, LANES : LANES + cols] * basis[b][top:end, LANES : LANES + cols]
        tiles = [product[i : i + 8, j : j + LANES] for i in range(0, rows, 8) for j in range(0, cols, LANES)]
        return functools.reduce(jnp.add, tiles)

    partial = [own_product(a, b) for a, b in ((0, 0), (0, 1), (0, 2), (0, 3), (0, 4), (2, 3), (3, 3), (3, 4))]
    place = lax.broadcasted_iota(jnp.int32, (8, LANES), 0)
    stacked = jnp.zeros((8, LANES), F32)
    for g, p in enumerate(partial):
        stacked = jnp.where(place == g, jnp.sum(p, axis=0, keepdims=True), stacked)
    stacked = jnp.broadcast_to(jnp.sum(stacked, axis=1, keepdims=True), (8, LANES))
    mine = jnp.where((lane_index(8) >> 4) == place, stacked, 0.0)
    slots[0:1] = jnp.sum(mine, axis=0, keepdims=True)

    def sum_copy(i, device):
        return pltpu.make_async_remote_copy(
            src_ref=slots.at[pl.ds(0, 1)],
            dst_ref=slots.at[pl.ds(i, 1)],
            send_sem=sum_send.at[i],
            recv_sem=sum_recv.at[i],
            device_id=device,
            device_id_type=MESH,
        )

    farthest_first(lambda i, device: sum_copy(i, device).start())
    for k in range(ITERS):
        for h in range(halves + 2):
            zeta[k * (halves + 2) + h] = basis[k][:, h * LANES : (h + 1) * LANES]

    for copy, sends, _ in edges_two:
        guarded(sends, copy.start)
    send_rows(second, rows_two)

    for copy, sends, receives in edges_one:
        guarded(sends, copy.wait_send)
        guarded(receives, copy.wait_recv)

    def open_across(uy, near):
        return uy * near * roll(near, -1) * (1.0 / 12.0)

    inner_side = spot < 0
    open_left = open_across(seam_left[2], jnp.where(inner_side, seam_left[3], seam_own[3]))
    open_right = open_across(seam_right[2], seam_right[3])

    def unpack(fields):
        def one_group(levels, carry):
            for k in levels:
                for f, packed in fields:
                    ends[f * depth + k] = roll(packed, LANES - 4 * k)
            return carry

        by_groups(0, depth, depth, one_group, 0)

    def both_sides(f):
        return jnp.where(inner_side, seam_left[f], seam_right[f])

    unpack([(0, both_sides(0)), (1, both_sides(1)), (2, jnp.where(inner_side, open_left, open_right)), (3, both_sides(3))])

    def open_columns(levels, carry):
        ahead = [shifted([wet_at(h, k) for h in span], ends[3 * depth + k], 1, lane) for k in levels]
        for k, wets_ahead in zip(levels, ahead):
            for h in span:
                i = h * depth + k
                open_y[i] = vy[i] * wet_at(h, k) * wets_ahead[h] * (1.0 / 12.0)
        return carry

    by_groups(0, depth, depth, open_columns, 0)
    get_forcing.wait()
    for h in span:
        theta[h * depth] = theta[h * depth] + forcing[:, h * LANES : (h + 1) * LANES] * wet_at(h, 0)

    def column_shifts(ref, where, f, k, beyond):
        centre = [ref[where(f, h, k), top:end] for h in span]
        return {s: shifted(centre, ends[beyond * depth + k], s, lane) for s in (-2, -1, 1, 2)}

    def face_shifts(k, steps):
        centre = [open_y[h * depth + k] for h in span]
        return {s: shifted(centre, ends[2 * depth + k], s, lane) for s in steps}

    def got_rows(ref, base, levels, sent_too):
        for copy, sends, receives in row_copies(ref, base, levels[0] // GROUP if isinstance(levels[0], int) else lax.div(levels[0], GROUP)):
            if sent_too:
                guarded(sends, copy.wait_send)
            guarded(receives, copy.wait_recv)

    def arms(u, wets):
        v = [wets * x for x in u]
        back, here = 7.0 * v[1], 7.0 * v[2]
        return v[0], back + v[0], back - here, here + v[3], v[3]

    for copy, sends, receives in early:
        guarded(sends, copy.wait_send)
        guarded(receives, copy.wait_recv)

    def coefficients(levels, carry):
        for k in levels:
            for h in span:
                i = h * depth + k
                face_x[i, top - 1 : top] = face_x[i, top - 1 : top] * wet[i, 0:1]
                face_x[i, end - 1 : end] = face_x[i, end - 1 : end] * wet_after[i, 0:1]
        moved = [face_shifts(k, (-2, -1, 1)) for k in levels]
        for k, uy in zip(levels, moved):
            for h in span:
                i = h * depth + k
                wets = wet_at(h, k)
                r = arms([face_x[i, top + s : end + s] for s in (-2, -1, 0, 1)], wets)
                c = arms([uy[-2][h], uy[-1][h], open_y[i], uy[1][h]], wets)
                for n, w in enumerate([(1.0 + r[2]) + c[2], r[0], r[3], c[0], c[3], r[1], r[4], c[1], c[4]]):
                    cross[9 * i + n] = w
        return carry

    by_groups(0, depth, depth, coefficients, 0)

    def forward_down(levels, carry):
        moved = [
            (face_shifts(k, (-1,)), [column_shifts(first, at_first, f, k, f) for f in range(2)]) for k in levels
        ]
        for k, (uy, turned) in zip(levels, moved):
            out = []
            for h in span:
                i = h * depth + k
                found = []
                for f, raw in ((0, theta), (1, salt)):
                    q = [first[at_first(f, h, k), top + s : end + s] for s in (-2, -1, 0, 1, 2)]
                    c = turned[f]
                    row_here = face_x[i, top:end] * (7.0 * (q[2] + q[3]) - (q[1] + q[4]))
                    row_back = face_x[i, top - 1 : end - 1] * (7.0 * (q[1] + q[2]) - (q[0] + q[3]))
                    col_here = open_y[i] * (7.0 * (q[2] + c[1][h]) - (c[-1][h] + c[2][h]))
                    col_back = uy[-1][h] * (7.0 * (c[-1][h] + q[2]) - (c[-2][h] + c[1][h]))
                    value = raw[i] - (row_here - row_back) - (col_here - col_back)
                    found.append(value * inverse[i] + link[i] * carry[h][f])
                theta_mix[i] = found[0]
                salt_mix[i] = found[1]
                out.append(tuple(found))
            carry = tuple(out)
        return carry

    for g in range(chunks):
        got_rows(first, rows_one, [g * GROUP], True)
    carry = by_groups(0, depth, 25, forward_down, ((blank, blank),) * halves)

    def forward_up(steps, carry):
        for n in steps:
            k = depth - 2 - n
            out = []
            for h in span:
                i = h * depth + k
                xt = theta_mix[i] + ratio[i] * carry[h][0]
                xs = salt_mix[i] + ratio[i] * carry[h][1]
                dt, ds = xt - carry[h][0], xs - carry[h][1]
                step_t, step_s, step_w = [
                    second[at(f, h, k), top:end] - second[at(f, h, k + 1), top:end] for f in range(3)
                ]
                closed = -wet_at(h, k) * wet_at(h, k + 1)
                k_fixed[h * (depth - 1) + k] = closed * (step_t * dt + step_s * ds)
                k_zeta[h * (depth - 1) + k] = closed * step_w * (0.2 * dt - 0.15 * ds)
                out.append((xt, xs))
            carry = tuple(out)
        return carry

    by_groups(0, depth - 1, 4, forward_up, carry)

    others(lambda i, device: sum_copy(i, device).wait_recv())
    total = jnp.broadcast_to(jnp.sum(slots[...], axis=0, keepdims=True), (8, LANES))
    m = [jnp.broadcast_to(total[:, 16 * g : 16 * g + 1], (8, LANES)) for g in range(8)]
    m = m[:5] + [2.0 * m[5] - m[1], 2.0 * m[6] - m[0], 2.0 * m[7] - m[1]]
    weights = [jnp.concatenate([w] * (wide[0] // 8), axis=0) for w in weights_from(m)]
    tiles = halves + 2
    for h in range(tiles):
        b = [zeta[k * tiles + h] for k in range(ITERS)]
        zeta[h] = (weights[0] * b[0] + weights[1] * b[1]) + (weights[2] * b[2] + weights[3] * b[3])

    for copy, sends, receives in edges_two:
        guarded(sends, copy.wait_send)
        guarded(receives, copy.wait_recv)
    beyond = jnp.where(lane >= LANES // 2, zeta[0, top:end], zeta[tiles - 1, top:end])
    far_t, far_s, far_w = both_sides(4), both_sides(5), both_sides(6)

    def unpack_mu(levels, carry):
        for k in levels:
            turned = [roll(p, LANES - 4 * k) for p in (far_t, far_s, far_w)]
            lifted = turned[2] * beyond
            ends[4 * depth + k] = turned[0] + 0.2 * lifted
            ends[5 * depth + k] = turned[1] - 0.15 * lifted
        return carry

    by_groups(0, depth, depth, unpack_mu, 0)

    def finish(levels, carry):
        got_rows(second, rows_two, levels, True)
        for k in levels:
            for h in span:
                area = pl.ds(top - 2, rows + 8)
                lifted = second[at(2, h, k), area] * zeta[h + 1, area]
                second[at(0, h, k), area] = second[at(0, h, k), area] + 0.2 * lifted
                second[at(1, h, k), area] = second[at(1, h, k), area] - 0.15 * lifted
        moved = [[column_shifts(second, at, f, k, 4 + f) for f in range(2)] for k in levels]
        for k, turned in zip(levels, moved):
            for h in span:
                i = h * depth + k
                where = slice(h * LANES, (h + 1) * LANES)
                for f, out in ((0, theta_grad), (1, salt_grad)):
                    values = [second[at(f, h, k), top + s : end + s] for s in (0, -2, 1)]
                    values += [turned[f][s][h] for s in (-2, 1)]
                    values += [second[at(f, h, k), top + s : end + s] for s in (-1, 2)]
                    values += [turned[f][s][h] for s in (-1, 2)]
                    out[k, :, where] = signed_sum([cross[9 * i + n] * v for n, v in enumerate(values)])
        return carry

    by_groups(0, theta_grad.shape[0], GROUP, finish, 0)

    def finish_kappa(levels, carry):
        for k in levels:
            for h in span:
                j = h * (depth - 1) + k
                kappa_grad[k, :, h * LANES : (h + 1) * LANES] = k_fixed[j] + k_zeta[j] * zeta[h + 1, top:end]
        return carry

    by_groups(0, depth - 1, 4, finish_kappa, 0)
    for h in span:
        forcing_grad[:, h * LANES : (h + 1) * LANES] = zeta[h + 1, top:end] + wet_at(h, 0) * second[at(0, h, 0), top:end]

    for g in range(theta_grad.shape[0] // GROUP, chunks):
        got_rows(second, rows_two, [g * GROUP], True)
    for copy, sends, _ in rims:
        guarded(sends, copy.wait_send)
    others(lambda i, device: sum_copy(i, device).wait_send())


def finish_kernel(
    sizes,
    theta_done, salt_done, kappa_done, forcing_done, second, cross, zeta, ends,
    theta_out, salt_out, kappa_out, forcing_out,
    mu, theta_grad, salt_grad, sems,
):
    depth, rows, cols = sizes
    halves = cols // LANES
    top, end = RIM, RIM + rows
    span = range(halves)
    lane = lane_index(rows)
    area = pl.ds(top - 2, rows + 8)
    split = theta_done.shape[0]
    copies = []

    def put(src, dst):
        copy = pltpu.make_async_copy(src, dst, sems.at[len(copies)])
        copy.start()
        copies.append(copy)

    put(theta_done, theta_out.at[pl.ds(0, split)])
    put(salt_done, salt_out.at[pl.ds(0, split)])
    put(kappa_done, kappa_out)
    put(forcing_done, forcing_out)

    def at(f, h, k):
        return (k * 3 + f) * halves + h

    def mu_at(f, h, k):
        return ((k - split) * 2 + f) * halves + h

    def column_shifts(f, k):
        centre = [mu[mu_at(f, h, k), top:end] for h in span]
        return {s: shifted(centre, ends[(4 + f) * depth + k], s, lane) for s in (-2, -1, 1, 2)}

    for first in range(split, depth, GROUP):
        levels = range(first, min(depth, first + GROUP))
        for k in levels:
            for h in span:
                lifted = second[at(2, h, k), area] * zeta[h + 1, area]
                mu[mu_at(0, h, k), area] = second[at(0, h, k), area] + 0.2 * lifted
                mu[mu_at(1, h, k), area] = second[at(1, h, k), area] - 0.15 * lifted
        moved = [[column_shifts(f, k) for f in range(2)] for k in levels]
        for k, turned in zip(levels, moved):
            for h in span:
                i = h * depth + k
                where = slice(h * LANES, (h + 1) * LANES)
                for f, out in ((0, theta_grad), (1, salt_grad)):
                    values = [mu[mu_at(f, h, k), top + s : end + s] for s in (0, -2, 1)]
                    values += [turned[f][s][h] for s in (-2, 1)]
                    values += [mu[mu_at(f, h, k), top + s : end + s] for s in (-1, 2)]
                    values += [turned[f][s][h] for s in (-1, 2)]
                    out[k - split, :, where] = signed_sum([cross[9 * i + n] * v for n, v in enumerate(values)])
        here, there = pl.ds(first - split, len(levels)), pl.ds(first, len(levels))
        put(theta_grad.at[here], theta_out.at[there])
        put(salt_grad.at[here], salt_out.at[there])
    for copy in copies:
        copy.wait()


def shards(*args):
    theta = args[0]
    depth, rows, cols = theta.shape
    halves = cols // LANES
    count = lax.axis_size("trow") * lax.axis_size("tcol")
    tall = rows + 2 * RIM
    V = pltpu.VMEM
    DMA = pltpu.SemaphoreType.DMA
    flat = V((halves * depth, rows, LANES), F32)
    ints = V((halves * depth, rows, LANES), jnp.int32)
    upper = V((halves * (depth - 1), rows, LANES), F32)
    tile = V((7, rows, LANES), F32)
    halo = DMA((7 + 4 * (depth // GROUP),))
    scratch = [
        flat, flat, flat, flat, ints, upper, V((rows, cols), F32), flat, flat,
        V((tall, cols + 2 * LANES), F32), V((tall, cols + 2 * LANES), jnp.int32),
        V((halves * depth, rows + RIM, LANES), F32), V((halves * depth, RIM, LANES), F32),
        V((halves * depth, tall, LANES), F32), V((2 * halves * depth, tall, LANES), F32),
        flat, flat, flat, flat, flat, flat,
        tile, tile, tile, V((count, LANES), F32), upper, upper,
        DMA((3 + 8 * halves,)), DMA((16,)), DMA((16,)), halo, halo, DMA((count,)), DMA((count,)),
    ]
    outs = [(depth, rows, cols), (depth, rows, cols), (depth - 1, rows, cols), (rows, cols)]
    split = depth // GROUP * 3 // 5 * GROUP
    parts = [
        (split, rows, cols), (split, rows, cols), outs[2], outs[3], (3 * halves * depth, tall, LANES),
        (9 * halves * depth, rows, LANES), (ITERS * (halves + 2), tall, LANES), (7 * depth, rows, LANES),
    ]
    found = pl.pallas_call(
        functools.partial(solve_kernel, (depth, rows, cols)),
        out_shape=[jax.ShapeDtypeStruct(o, F32) for o in parts],
        in_specs=[pl.BlockSpec(memory_space=pltpu.HBM)] * len(args),
        out_specs=[pl.BlockSpec(memory_space=V)] * len(parts),
        scratch_shapes=scratch,
        compiler_params=pltpu.CompilerParams(
            collective_id=0, has_side_effects=True, vmem_limit_bytes=32 * 1024 * 1024
        ),
    )(*[pltpu.with_memory_space_constraint(a, pltpu.HBM) for a in args])
    left = (depth - split, rows, cols)
    return tuple(
        pl.pallas_call(
            functools.partial(finish_kernel, (depth, rows, cols)),
            out_shape=[jax.ShapeDtypeStruct(o, F32) for o in outs],
            in_specs=[pl.BlockSpec(memory_space=V)] * len(parts),
            out_specs=[pl.BlockSpec(memory_space=pltpu.HBM)] * len(outs),
            scratch_shapes=[V((2 * halves * left[0], tall, LANES), F32), V(left, F32), V(left, F32)]
            + [DMA((4 + 2 * (left[0] // GROUP + 1),))],
            compiler_params=pltpu.CompilerParams(vmem_limit_bytes=8 * 1024 * 1024),
        )(*found)
    )


def solution(mesh):
    cube, plane = P(None, "trow", "tcol"), P("trow", "tcol")
    in_specs = (cube,) * 6 + (plane,) * 2 + (cube,) * 2 + (plane,)
    out_specs = (cube,) * 3 + (plane,)
    return jax.shard_map(shards, mesh=mesh, in_specs=in_specs, out_specs=out_specs, check_vma=False)
```
